256 devices in a mesh: particle: 4 (over z_hi), slab: 32 (over y, x, z_lo), half: 2 (over core).
Axes of the slice: x: 4, y: 4, z: 8 (z_hi: 4, z_lo: 2; z = z_hi * 2 + z_lo), core: 2. Of those that a mesh axis runs over, the one named last changes fastest.
Arguments:
- tiles: bfloat16 [2, 256, 128, 4096], P('half', 'particle', 'slab'), may hold values from -1.5 to 1.5
- tile_index: int32 [2, 256, 128], P('half', 'particle', 'slab'), may hold values from 0 to 255
- pose_bin: int32 [2, 256], P('half', 'particle'), may hold values from 0 to 31
- bin_gain: bfloat16 [2, 32], P('half'), may hold values from 0.25 to 4
- cutoffs: int32 [6], replicated, may hold values from 32 to 128, as said below
Outputs:
- refined: float32 [2, 256, 256, 256], P('half', None, ('particle', 'slab'))
The draws below stay inside these ranges and needn't reach their ends.
Inputs may be any that keep to these rules, and one draw needn't show every extreme that they name: `cutoffs`: the last band's cutoff is 128.
All inputs are finite; a program needn't handle non-finite values.
Results may differ from the reference program's by a relative error of at most 0.0003.
Values sent between devices are 32-bit elements; how exact they have to be, the bound alone decides.
No kernel may reach another device: no remote copies, remote signals or barrier semaphores. Data moves between devices by JAX's collectives and lax.ppermute only.
A program may use at most 64 MiB of HBM per device.

```python
import math
import jax
import jax.numpy as jnp
from jax import lax

BOX = 256
BANDS = 6
TILE_ROWS = 8
TOUCH = 4
POSE_BINS = 32
PARTICLES = 64
SLOTS = 256
N_PARTICLE = 4
N_SLAB = 32


def draw_cutoffs(key, part):
    drawn = jax.random.randint(key, (BANDS,), BOX // 8, BOX // 2 + 1)
    positions = jnp.arange(BANDS)
    return jnp.where(positions == BANDS - 1, BOX // 2, drawn).astype(jnp.int32)


def with_ends(array, key, least, top_value):
    shape = array.shape
    place = [jax.random.randint(jax.random.fold_in(key, axis), (), 0, shape[axis]) for axis in range(len(shape))]
    array = array.at[tuple(place)].set(least)
    longest = shape.index(max(shape))
    place[longest] = (place[longest] + 1) % shape[longest]
    return array.at[tuple(place)].set(top_value)


def block_levels(stream_key, shape, pieces, least, top_value):
    def one(position, parts):
        draws = jax.random.uniform(jax.random.fold_in(jax.random.fold_in(stream_key, 6), position), (parts,), jnp.float32, least / len(pieces), top_value / len(pieces))
        return jnp.repeat(jnp.exp(draws), shape[position] // parts).reshape((-1,) + (1,) * (len(shape) - position - 1))

    gain = one(*pieces[0])
    for cut in pieces[1:]:
        gain = gain * one(*cut)
    return gain


def scatter_about(rng, shape, width, limit, pieces=(), kind=jnp.bfloat16):
    loudness = block_levels(rng, shape, pieces, -0.22, 0.18) if pieces else 1.0
    values = jax.random.normal(rng, shape, jnp.float32) * width * loudness
    return jnp.minimum(jnp.maximum(values, -limit), limit).astype(kind)


def setup_inputs(seed: int = 0) -> dict:
    splits = jax.random.split(jax.random.key(seed), 6)
    tiles = scatter_about(splits[0], (2, PARTICLES * N_PARTICLE, TOUCH * N_SLAB, 2 * TILE_ROWS * BOX), 0.25, 1.5, ((0, 2), (1, 4), (2, 32)))
    tile_index = with_ends(jax.random.randint(splits[1], (2, PARTICLES * N_PARTICLE, TOUCH * N_SLAB), 0, SLOTS), jax.random.fold_in(splits[1], 1), 0, SLOTS - 1).astype(jnp.int32)
    pose_bin = with_ends(jax.random.randint(splits[2], (2, PARTICLES * N_PARTICLE), 0, POSE_BINS), jax.random.fold_in(splits[2], 1), 0, POSE_BINS - 1).astype(jnp.int32)
    bin_gain = jnp.clip(jnp.exp(math.log(4.0) - 2.7725887 * jax.random.uniform(splits[3], (2, POSE_BINS), jnp.float32) ** block_levels(splits[3], (2, POSE_BINS), ((0, 2),), -0.2, 0.2)), 0.25, 4.0).astype(jnp.bfloat16)
    cutoffs = draw_cutoffs(jax.random.fold_in(splits[5], 71), 0)
    return {"tiles": tiles, "tile_index": tile_index, "pose_bin": pose_bin, "bin_gain": bin_gain, "cutoffs": cutoffs}


error_floor = 1.0


def signed_wave(frequency, length):
    return (frequency + length // 2) % length - length // 2


def half_spectrum(half_tiles, half_index, half_bins, half_gain):
    slab_depth = BOX // N_SLAB
    blocks = BOX // TILE_ROWS
    slot_count = slab_depth * blocks
    touched = half_index.shape[1] // N_SLAB
    particle_gain = half_gain.astype(jnp.float32)[half_bins]

    def one_slab(slab_pos):
        part_tiles = lax.dynamic_slice_in_dim(half_tiles, slab_pos * touched, touched, 1).astype(jnp.float32)
        part_slots = lax.dynamic_slice_in_dim(half_index, slab_pos * touched, touched, 1)
        scaled = part_tiles * particle_gain[:, None, None]
        summed = jax.ops.segment_sum(scaled.reshape(-1, scaled.shape[2]), part_slots.reshape(-1), num_segments=slot_count)
        shaped = summed.reshape(slab_depth, blocks, 2, TILE_ROWS, BOX)
        return jnp.transpose(shaped, (2, 0, 1, 3, 4)).reshape(2, slab_depth, BOX, BOX)

    slabs = lax.map(one_slab, jnp.arange(N_SLAB, dtype=jnp.int32))
    return jnp.transpose(slabs, (1, 0, 2, 3, 4)).reshape(2, BOX, BOX, BOX)


def reference(tiles, tile_index, pose_bin, bin_gain, cutoffs):
    grid = jnp.arange(BOX, dtype=jnp.int32)
    signed_all = signed_wave(grid, BOX)
    square = signed_all * signed_all
    radius = square[:, None, None] + square[None, :, None] + square[None, None, :]
    filtered = []
    for half_id in range(2):
        spectrum = half_spectrum(tiles[half_id], tile_index[half_id], pose_bin[half_id], bin_gain[half_id])
        volume = lax.complex(spectrum[0], spectrum[1])

        def one_band(cutoff_now):
            retained = jnp.where(radius <= cutoff_now * cutoff_now, volume, jnp.zeros_like(volume))
            return jnp.real(jnp.fft.ifftn(retained)) * (BOX * BOX)

        filtered.append(lax.map(one_band, cutoffs))
    first, second = filtered
    smoothed = (first - second) ** 2
    for axis_id in (1, 2, 3):
        smoothed = smoothed + jnp.roll(smoothed, 1, axis=axis_id) + jnp.roll(smoothed, -1, axis=axis_id)
    errors = smoothed / 27.0
    weights = 1.0 / (errors + error_floor)
    total = jnp.sum(weights, axis=0)
    outputs = []
    for band_maps in (first, second):
        outputs.append(jnp.sum(weights * band_maps, axis=0) / total)
    return jnp.stack(outputs)
```

```python
import math

import jax
import jax.numpy as jnp
import numpy as np
from jax import lax
from jax.experimental import pallas as pl
from jax.experimental.pallas import tpu as pltpu
from jax.sharding import PartitionSpec as P

BOX = 256
HALF = BOX // 2
TILE_ROWS = 8
BLOCKS = BOX // TILE_ROWS
BANDS = 6
GROUPS = 4
SLABS = 32
SENDERS = GROUPS * SLABS
PER = BANDS * 8
LANES = 128
error_floor = 1.0
bf16 = jnp.bfloat16
f32 = jnp.float32
VMEM = pl.BlockSpec(memory_space=pltpu.VMEM)
SMEM = pl.BlockSpec(memory_space=pltpu.SMEM)


def split(table):
    high = table.astype(np.float32).astype(jnp.bfloat16)
    low = (table - high.astype(np.float64)).astype(np.float32).astype(jnp.bfloat16)
    return high, low


def angles(left, right):
    return (np.outer(left, right) % BOX) * (2.0 * math.pi / BOX)


def tables():
    places = np.arange(BOX)
    y_order = (places % 64) * 4 + places // 64
    ky_order = (places % BLOCKS) * TILE_ROWS + places // BLOCKS
    turn = angles(y_order, ky_order)
    cosine, sine = np.cos(turn), np.sin(turn)
    along_y = np.block([[cosine, -sine], [sine, cosine]])
    turn = angles(places, places)
    cosine, sine = np.cos(turn), np.sin(turn)
    along_x_even = np.concatenate([cosine, -sine], axis=0)
    along_x_odd = np.concatenate([sine, cosine], axis=0)
    sender = np.arange(SENDERS)
    group, slab = sender // SLABS, sender % SLABS
    plane = slab * 8 + group * 2 + (slab >= SLABS // 2)
    turn = angles(places, plane)
    even, odd = np.cos(turn), -np.sin(turn)
    odd[:, 0] = np.cos(math.pi * places)
    along_z = np.concatenate([even, odd], axis=1) / BOX
    return split(along_y) + split(along_x_even) + split(along_x_odd) + split(along_z)


def two(value):
    high = value.astype(bf16)
    return high, (value - high.astype(f32)).astype(bf16)


def dot(a, b):
    return jnp.dot(a, b, preferred_element_type=f32)


def planes_kernel(
    cut_ref, kz_ref, keep_ref, come_ref, yh_ref, yl_ref, eh_ref, el_ref, oh_ref, ol_ref, out_ref, sh, sl, dh, dl, radius
):
    alone = kz_ref[0] == 0
    last = come_ref[0:1, 0:1]
    for i in range(16):
        kept = keep_ref[:, i * BOX : (i + 1) * BOX]
        come = jnp.where(alone, 0.0, come_ref[:, i * BOX : (i + 1) * BOX])
        rows = pl.ds(i * BLOCKS, BLOCKS)
        sh[rows, :], sl[rows, :] = two(kept + come)
        dh[rows, :], dl[rows, :] = two(kept - come)
    line = lax.broadcasted_iota(jnp.int32, (BOX, BOX), 0)
    col = lax.broadcasted_iota(jnp.int32, (BOX, BOX), 1)
    ky = (line & (BLOCKS - 1)) * TILE_ROWS + (line >> 5)
    ky = ((ky + HALF) & (BOX - 1)) - HALF
    kx = ((col + HALF) & (BOX - 1)) - HALF
    kz = ((kz_ref[0] + HALF) & (BOX - 1)) - HALF
    radius[...] = (ky * ky + kx * kx + kz * kz).astype(f32)

    @pl.loop(0, BANDS)
    def _(b):
        limit = (cut_ref[b] * cut_ref[b]).astype(f32)
        mask = jnp.where(radius[...] <= limit, 1.0, 0.0).astype(bf16)
        mask = jnp.concatenate([mask, mask], axis=0)

        def plane(high_ref, low_ref, th_ref, tl_ref):
            high, low = high_ref[...] * mask, low_ref[...] * mask
            mid = dot(yh_ref[...], high) + dot(yl_ref[...], high) + dot(yh_ref[...], low)
            mid = jnp.concatenate([mid[:BOX], mid[BOX:]], axis=1)
            high, low = two(mid)
            return dot(high, th_ref[...]) + dot(low, th_ref[...]) + dot(high, tl_ref[...])

        even = plane(sh, sl, eh_ref, el_ref)
        odd = plane(dh, dl, oh_ref, ol_ref)
        top = jnp.where(cut_ref[b] >= HALF, last, 0.0)
        odd = jnp.where(alone, jnp.broadcast_to(top, odd.shape), odd)
        for c, part in enumerate((even, odd)):
            for j in range(4):
                for side in range(2):
                    block = part[j * 64 : (j + 1) * 64, side * LANES : (side + 1) * LANES]
                    out_ref[pl.ds(side * PER + b * 8 + c * 4 + j, 64, stride=2 * PER), :] = block


def depth_kernel(core_ref, come_ref, zh_ref, zl_ref, own_ref, other_ref):
    b = pl.program_id(0)
    for out_ref, core in ((own_ref, core_ref[0]), (other_ref, 1 - core_ref[0])):
        start = b * 8 + core * 2
        sides = [
            jnp.concatenate(
                [come_ref[pl.ds(start + c * 4 + j, SENDERS, stride=PER), :] for j in range(2)], axis=1
            )
            for c in range(2)
        ]
        high, low = two(jnp.concatenate(sides, axis=0))
        full = dot(zh_ref[...], high) + dot(zl_ref[...], high) + dot(zh_ref[...], low)
        out_ref[0, 0] = full[:, :LANES]
        out_ref[0, 1] = full[:, LANES:]


def square_kernel(own_ref, other_ref, first_ref, second_ref, edge_ref):
    b = pl.program_id(0)
    lane = lax.broadcasted_iota(jnp.int32, (BOX, LANES), 1)

    @pl.when(b == 0)
    def _():
        edge_ref[...] = jnp.zeros_like(edge_ref)

    edge = edge_ref[...]
    for row, ref in enumerate((first_ref, second_ref)):
        gap = own_ref[0, row] - other_ref[0, row]
        square = gap * gap
        ref[0] = square
        spot = row * 32 + b
        edge = jnp.where(lane == spot, pltpu.roll(square, spot + 1, 1), edge)
        edge = jnp.where(lane == spot + 64, pltpu.roll(square, spot + 64, 1), edge)
    edge_ref[...] = edge


def blend_kernel(
    swap_ref,
    own_ref,
    other_ref,
    first_ref,
    second_ref,
    before_ref,
    after_ref,
    edge_ref,
    edge_before_ref,
    edge_after_ref,
    out_a_ref,
    out_b_ref,
    sums,
):
    b = pl.program_id(0)
    lane = lax.broadcasted_iota(jnp.int32, (BOX, LANES), 1)

    @pl.when(b == 0)
    def _():
        sums[...] = jnp.zeros_like(sums)

    middle = first_ref[0] + second_ref[0]
    edge = edge_ref[...]
    edge = edge + pltpu.roll(edge, LANES - 32, 1)
    for row in range(2):
        if row == 0:
            tall = middle + before_ref[0]
            border = edge + pltpu.roll(edge_before_ref[...], LANES - 32, 1)
        else:
            tall = middle + after_ref[0]
            border = edge + edge_after_ref[...]
        left = jnp.where(lane == 0, pltpu.roll(border, LANES - b, 1), pltpu.roll(tall, 1, 1))
        right = jnp.where(lane == LANES - 1, pltpu.roll(border, 63 - b, 1), pltpu.roll(tall, LANES - 1, 1))
        wide = tall + left + right
        full = wide + pltpu.roll(wide, 1, 0) + pltpu.roll(wide, BOX - 1, 0)
        weight = 1.0 / (full / 27.0 + error_floor)
        sums[row, 0] += weight * own_ref[0, row]
        sums[row, 1] += weight * other_ref[0, row]
        sums[row, 2] += weight

    @pl.when(b == BANDS - 1)
    def _():
        swap = swap_ref[0] == 1
        for row in range(2):
            mine = sums[row, 0] / sums[row, 2]
            theirs = sums[row, 1] / sums[row, 2]
            out_a_ref[row] = jnp.where(swap, theirs, mine)
            out_b_ref[row] = jnp.where(swap, mine, theirs)


def place(group, slab, half):
    return (group * SLABS + slab) * 2 + half


def mirror_pairs():
    pairs = []
    for group in range(GROUPS):
        for slab in range(SLABS):
            if slab < SLABS // 2:
                goal = (GROUPS - 1 - group, SLABS - 1 - slab)
            elif group:
                goal = (GROUPS - group, SLABS - 1 - slab)
            else:
                goal = (0, (SLABS - slab) % (SLABS // 2))
            pairs.append((group * SLABS + slab, goal[0] * SLABS + goal[1]))
    return pairs


def row_pairs(step, flip):
    pairs = []
    for n in range(SENDERS):
        goal = (n + step) % SENDERS
        for side in range(2):
            pairs.append((n // 2 * 4 + side * 2 + n % 2, goal // 2 * 4 + (side ^ flip) * 2 + goal % 2))
    return pairs


def home_pairs(flip):
    pairs = []
    for chips in range(SENDERS // 2):
        for side in range(2):
            for half in range(2):
                pairs.append((chips * 4 + side * 2 + half, chips * 4 + half * 2 + (side ^ flip)))
    return pairs


def on_device(tiles, tile_index, pose_bin, bin_gain, cutoffs):
    slab_pos = lax.axis_index("slab")
    group_pos = lax.axis_index("particle")
    half_pos = lax.axis_index("half")
    side_pos = slab_pos % 2
    everyone = ("particle", "slab", "half")
    slot_count = BOX // SLABS * BLOCKS
    tile_width = 2 * TILE_ROWS * BOX
    touched = tile_index.shape[2]
    flat_tiles = tiles[0].reshape(-1, tile_width)
    entry_slot = tile_index[0].reshape(-1)
    bin_ids = jnp.arange(bin_gain.shape[1], dtype=jnp.int32)
    particle_gain = jnp.sum(
        jnp.where(pose_bin[0][:, None] == bin_ids[None, :], bin_gain[0][None, :].astype(f32), 0.0),
        axis=1,
    )
    entry_gain = jnp.repeat(particle_gain, touched)
    slot_ids = jnp.arange(slot_count, dtype=jnp.int32)
    placing = jnp.where(slot_ids[:, None] == entry_slot[None, :], entry_gain[None, :], 0.0).astype(bf16)
    owned = lax.psum_scatter(
        jnp.dot(placing, flat_tiles, preferred_element_type=f32), "particle", scatter_dimension=0, tiled=True
    )
    late = (slab_pos >= SLABS // 2).astype(jnp.int32)
    kept = lax.dynamic_slice_in_dim(owned, late * BLOCKS, BLOCKS, 0)
    leaving = lax.dynamic_slice_in_dim(owned, (1 - late) * BLOCKS, BLOCKS, 0)
    come = lax.ppermute(leaving, ("particle", "slab"), mirror_pairs())
    plane = (slab_pos * 8 + group_pos * 2 + late).reshape(1)

    constants = [jnp.asarray(t) for t in tables()]
    square = (2 * BOX, BOX)
    sent = pl.pallas_call(
        planes_kernel,
        out_shape=jax.ShapeDtypeStruct((SENDERS * PER, LANES), f32),
        in_specs=[SMEM, SMEM] + [VMEM] * 8,
        out_specs=VMEM,
        scratch_shapes=[pltpu.VMEM(square, bf16)] * 4 + [pltpu.VMEM((BOX, BOX), f32)],
        name="planes",
    )(cutoffs, plane, kept, come, *constants[:6])
    gathered = lax.all_to_all(
        sent.reshape(SENDERS, PER, LANES), ("particle", "slab"), split_axis=0, concat_axis=0, tiled=True
    ).reshape(SENDERS * PER, LANES)

    rows_block = (1, 2, BOX, LANES)
    rows_spec = pl.BlockSpec(rows_block, lambda b: (b, 0, 0, 0))
    rows_shape = jax.ShapeDtypeStruct((BANDS, 2, BOX, LANES), f32)
    row_spec = pl.BlockSpec((1, BOX, LANES), lambda b: (b, 0, 0))
    row_shape = jax.ShapeDtypeStruct((BANDS, BOX, LANES), f32)
    edge_spec = pl.BlockSpec((BOX, LANES), lambda b: (0, 0))
    edge_shape = jax.ShapeDtypeStruct((BOX, LANES), f32)
    own, leaving = pl.pallas_call(
        depth_kernel,
        grid=(BANDS,),
        out_shape=(rows_shape, rows_shape),
        in_specs=[
            SMEM,
            pl.BlockSpec((SENDERS * PER, LANES), lambda b: (0, 0)),
            pl.BlockSpec((BOX, BOX), lambda b: (0, 0)),
            pl.BlockSpec((BOX, BOX), lambda b: (0, 0)),
        ],
        out_specs=(rows_spec, rows_spec),
        name="depth",
    )(half_pos.reshape(1), gathered, *constants[6:])
    other = lax.ppermute(leaving, "half", [(0, 1), (1, 0)])
    first, second, edge = pl.pallas_call(
        square_kernel,
        grid=(BANDS,),
        out_shape=(row_shape, row_shape, edge_shape),
        in_specs=[rows_spec, rows_spec],
        out_specs=(row_spec, row_spec, edge_spec),
        name="square",
    )(own, other)
    before = lax.ppermute(second, everyone, row_pairs(1, 0))
    after = lax.ppermute(first, everyone, row_pairs(-1, 0))
    edge_here = lax.ppermute(edge, everyone, row_pairs(0, 1))
    edge_before = lax.ppermute(edge, everyone, row_pairs(1, 1))
    edge_after = lax.ppermute(edge, everyone, row_pairs(-1, 1))
    swap = (side_pos != half_pos).astype(jnp.int32).reshape(1)
    block_spec = pl.BlockSpec((2, BOX, LANES), lambda b: (0, 0, 0))
    block_shape = jax.ShapeDtypeStruct((2, BOX, LANES), f32)
    near, far = pl.pallas_call(
        blend_kernel,
        grid=(BANDS,),
        out_shape=(block_shape, block_shape),
        in_specs=[SMEM, rows_spec, rows_spec] + [row_spec] * 4 + [edge_spec] * 3,
        out_specs=(block_spec, block_spec),
        scratch_shapes=[pltpu.VMEM((2, 3, BOX, LANES), f32)],
        name="blend",
    )(swap, own, other, first, second, before, after, edge_here, edge_before, edge_after)
    near = lax.ppermute(near, everyone, home_pairs(0))
    far = lax.ppermute(far, everyone, home_pairs(1))
    low = jnp.where(half_pos == 0, near, far)
    high = jnp.where(half_pos == 0, far, near)
    refined = jnp.concatenate([low, high], axis=2)
    return jnp.transpose(refined, (1, 0, 2))[None]


def solution(mesh):
    placed = (
        P("half", "particle", "slab", None),
        P("half", "particle", "slab"),
        P("half", "particle"),
        P("half", None),
        P(),
    )
    return jax.shard_map(
        on_device,
        mesh=mesh,
        in_specs=placed,
        out_specs=P("half", None, ("particle", "slab"), None),
        check_vma=False,
    )
```

```python
import math

import jax
import jax.numpy as jnp
import numpy as np
from jax import lax
from jax.experimental import pallas as pl
from jax.experimental.pallas import tpu as pltpu
from jax.sharding import PartitionSpec as P

BOX = 256
HALF = BOX // 2
TILE_ROWS = 8
BLOCKS = BOX // TILE_ROWS
BANDS = 6
GROUPS = 4
SLABS = 32
SENDERS = GROUPS * SLABS
PER = BANDS * 8
LANES = 128
error_floor = 1.0
bf16 = jnp.bfloat16
f32 = jnp.float32
VMEM = pl.BlockSpec(memory_space=pltpu.VMEM)
SMEM = pl.BlockSpec(memory_space=pltpu.SMEM)


def split(table):
    high = table.astype(np.float32).astype(jnp.bfloat16)
    low = (table - high.astype(np.float64)).astype(np.float32).astype(jnp.bfloat16)
    return high, low


def angles(left, right):
    return (np.outer(left, right) % BOX) * (2.0 * math.pi / BOX)


def tables():
    places = np.arange(BOX)
    y_order = (places % 64) * 4 + places // 64
    ky_order = (places % BLOCKS) * TILE_ROWS + places // BLOCKS
    turn = angles(y_order, ky_order)
    cosine, sine = np.cos(turn), np.sin(turn)
    along_y = np.block([[cosine, -sine], [sine, cosine]])
    turn = angles(places, places)
    cosine, sine = np.cos(turn), np.sin(turn)
    along_x = np.block([[cosine, sine], [-sine, cosine]])
    sender = np.arange(SENDERS)
    group, slab = sender // SLABS, sender % SLABS
    plane = slab * 8 + group * 2 + (slab >= SLABS // 2)
    turn = angles(places, plane)
    even, odd = np.cos(turn), -np.sin(turn)
    odd[:, 0] = np.cos(math.pi * places)
    along_z = np.concatenate([even, odd], axis=1) / BOX
    return split(along_y) + split(along_x) + split(along_z)


def two(value):
    high = value.astype(bf16)
    return high, (value - high.astype(f32)).astype(bf16)


def dot(a, b):
    return jnp.dot(a, b, preferred_element_type=f32)


def mark(rows, slots, gains):
    return jnp.where(rows == slots, gains, 0.0).astype(bf16)


def place_kernel(
    plane_ref, flag_ref, slot_ref, gain_ref, tile_ref, flip_ref, *refs
):
    outs, (kept_mark, sent_mark, sent_mark_first, turn, saved) = refs[:9], refs[9:]
    step = pl.program_id(0)
    row = lax.broadcasted_iota(jnp.int32, (BLOCKS, BOX), 0)
    col = lax.broadcasted_iota(jnp.int32, (BLOCKS, BOX), 1)

    @pl.when(step == 0)
    def _():
        slots = jnp.broadcast_to(slot_ref[...], (BLOCKS, BOX))
        gains = jnp.broadcast_to(gain_ref[...], (BLOCKS, BOX))
        for i in range(4):
            rows = pl.ds(i * BLOCKS, BLOCKS)
            kept_mark[rows, :] = mark(plane_ref[i] * BLOCKS + row, slots, gains)
            start = plane_ref[4 + i] * BLOCKS
            sent_mark[rows, :] = mark(start + BLOCKS - 1 - row, slots, gains)
            sent_mark_first[rows, :] = mark(start + ((BLOCKS - row) & (BLOCKS - 1)), slots, gains)
        line = lax.broadcasted_iota(jnp.int32, (BOX, BOX), 0)
        wide = lax.broadcasted_iota(jnp.int32, (BOX, BOX), 1)
        turn[...] = jnp.where(((line + wide) & (BOX - 1)) == 0, 1.0, 0.0).astype(bf16)

    kept = dot(kept_mark[...], tile_ref[...])
    flipped = dot(flip_ref[...], turn[...])
    flipped = jnp.where(step >= TILE_ROWS, -flipped, flipped).astype(bf16)
    marks = jnp.where((step & (TILE_ROWS - 1)) == 0, sent_mark_first[...], sent_mark[...])
    sent = dot(marks, flipped)

    @pl.when(step == 0)
    def _():
        saved[...] = sent

    corner = (row == 0) & (col == 0) & (step == TILE_ROWS)
    parts = []
    for i in range(4):
        part = kept[i * BLOCKS : (i + 1) * BLOCKS]
        parts.append(jnp.where(corner & (flag_ref[i] == 1), 0.0, part))
    for i in range(4):
        part = sent[i * BLOCKS : (i + 1) * BLOCKS]
        alone = jnp.where(corner, saved[i * BLOCKS : (i + 1) * BLOCKS, :], 0.0)
        parts.append(jnp.where(flag_ref[4 + i] == 1, alone, part))
    parts[2:3] = [parts[2][: BLOCKS // 2], parts[2][BLOCKS // 2 :]]
    for out_ref, part in zip(outs, parts):
        out_ref[...] = part


def planes_kernel(cut_ref, kz_ref, own_ref, up_ref, down_ref, yh_ref, yl_ref, xh_ref, xl_ref, out_ref, sh, sl, radius):
    alone = kz_ref[0] == 0
    for i in range(16):
        cols = pl.ds(i * BOX, BOX)
        rows = pl.ds(i * BLOCKS, BLOCKS)
        whole = own_ref[:, cols] + up_ref[:, cols] + down_ref[:, cols]
        if i == TILE_ROWS:
            last = whole[0:1, 0:1]
        sh[rows, :], sl[rows, :] = two(whole)
    line = lax.broadcasted_iota(jnp.int32, (BOX, BOX), 0)
    col = lax.broadcasted_iota(jnp.int32, (BOX, BOX), 1)
    ky = (line & (BLOCKS - 1)) * TILE_ROWS + (line >> 5)
    ky = ((ky + HALF) & (BOX - 1)) - HALF
    kx = ((col + HALF) & (BOX - 1)) - HALF
    kz = ((kz_ref[0] + HALF) & (BOX - 1)) - HALF
    radius[...] = (ky * ky + kx * kx + kz * kz).astype(f32)

    @pl.loop(0, BANDS)
    def _(b):
        limit = (cut_ref[b] * cut_ref[b]).astype(f32)
        mask = jnp.where(radius[...] <= limit, 1.0, 0.0).astype(bf16)
        mask = jnp.concatenate([mask, mask], axis=0)
        high, low = sh[...] * mask, sl[...] * mask
        mid = dot(yh_ref[...], high) + dot(yl_ref[...], high) + dot(yh_ref[...], low)
        mid = jnp.concatenate([mid[:BOX], mid[BOX:]], axis=1)
        high, low = two(mid)
        both = dot(high, xh_ref[...]) + dot(low, xh_ref[...]) + dot(high, xl_ref[...])
        even, odd = both[:, :BOX], both[:, BOX:]
        top = jnp.where(cut_ref[b] >= HALF, last, 0.0)
        odd = jnp.where(alone, jnp.broadcast_to(top, odd.shape), odd)
        for c, part in enumerate((even, odd)):
            for j in range(4):
                for side in range(2):
                    block = part[j * 64 : (j + 1) * 64, side * LANES : (side + 1) * LANES]
                    out_ref[pl.ds(side * PER + b * 8 + c * 4 + j, 64, stride=2 * PER), :] = block


def depth_kernel(core_ref, come_ref, zh_ref, zl_ref, own_ref, other_ref):
    b = pl.program_id(0)
    for out_ref, core in ((own_ref, core_ref[0]), (other_ref, 1 - core_ref[0])):
        start = b * 8 + core * 2
        sides = [
            jnp.concatenate(
                [come_ref[pl.ds(start + c * 4 + j, SENDERS, stride=PER), :] for j in range(2)], axis=1
            )
            for c in range(2)
        ]
        high, low = two(jnp.concatenate(sides, axis=0))
        full = dot(zh_ref[...], high) + dot(zl_ref[...], high) + dot(zh_ref[...], low)
        out_ref[0, 0] = full[:, :LANES]
        out_ref[0, 1] = full[:, LANES:]


def square_kernel(own_ref, other_ref, first_ref, second_ref, edge_ref):
    b = pl.program_id(0)
    lane = lax.broadcasted_iota(jnp.int32, (BOX, LANES), 1)

    @pl.when(b == 0)
    def _():
        edge_ref[...] = jnp.zeros_like(edge_ref)

    edge = edge_ref[...]
    for row, ref in enumerate((first_ref, second_ref)):
        gap = own_ref[0, row] - other_ref[0, row]
        square = gap * gap
        ref[0] = square
        spot = row * 32 + b
        edge = jnp.where(lane == spot, pltpu.roll(square, spot + 1, 1), edge)
        edge = jnp.where(lane == spot + 64, pltpu.roll(square, spot + 64, 1), edge)
    edge_ref[...] = edge


def blend_kernel(
    swap_ref,
    own_ref,
    other_ref,
    first_ref,
    second_ref,
    before_ref,
    after_ref,
    edge_ref,
    edge_before_ref,
    edge_after_ref,
    out_a_ref,
    out_b_ref,
    sums,
):
    b = pl.program_id(0)
    lane = lax.broadcasted_iota(jnp.int32, (BOX, LANES), 1)

    @pl.when(b == 0)
    def _():
        sums[...] = jnp.zeros_like(sums)

    middle = first_ref[0] + second_ref[0]
    edge = edge_ref[...]
    edge = edge + pltpu.roll(edge, LANES - 32, 1)
    for row in range(2):
        if row == 0:
            tall = middle + before_ref[0]
            border = edge + pltpu.roll(edge_before_ref[...], LANES - 32, 1)
        else:
            tall = middle + after_ref[0]
            border = edge + edge_after_ref[...]
        left = jnp.where(lane == 0, pltpu.roll(border, LANES - b, 1), pltpu.roll(tall, 1, 1))
        right = jnp.where(lane == LANES - 1, pltpu.roll(border, 63 - b, 1), pltpu.roll(tall, LANES - 1, 1))
        wide = tall + left + right
        full = wide + pltpu.roll(wide, 1, 0) + pltpu.roll(wide, BOX - 1, 0)
        weight = 1.0 / (full / 27.0 + error_floor)
        sums[row, 0] += weight * own_ref[0, row]
        sums[row, 1] += weight * other_ref[0, row]
        sums[row, 2] += weight

    @pl.when(b == BANDS - 1)
    def _():
        swap = swap_ref[0] == 1
        for row in range(2):
            mine = sums[row, 0] / sums[row, 2]
            theirs = sums[row, 1] / sums[row, 2]
            out_a_ref[row] = jnp.where(swap, theirs, mine)
            out_b_ref[row] = jnp.where(swap, mine, theirs)


def chip(depth, spot):
    return depth // 2 * SLABS + spot * 2 + depth % 2


def mirror_pairs(ahead):
    pairs = []
    for depth in range(8):
        for spot in range(16):
            goal = (depth, 15 - spot)
            if spot >= 8 and (depth + ahead) % 8 // 2 == 0:
                goal = ((depth + 1) % 8, 15 - spot) if depth % 2 else ((depth - 1) % 8, (16 - spot) % 8)
            pairs.append((chip(depth, spot), chip(*goal)))
    return pairs


def ring_pairs(step):
    return [(chip(d, s), chip((d + step) % 8, s)) for d in range(8) for s in range(16)]


def row_pairs(step, flip):
    pairs = []
    for n in range(SENDERS):
        goal = (n + step) % SENDERS
        for side in range(2):
            pairs.append((n // 2 * 4 + side * 2 + n % 2, goal // 2 * 4 + (side ^ flip) * 2 + goal % 2))
    return pairs


def home_pairs(flip):
    pairs = []
    for chips in range(SENDERS // 2):
        for side in range(2):
            for half in range(2):
                pairs.append((chips * 4 + side * 2 + half, chips * 4 + half * 2 + (side ^ flip)))
    return pairs


def on_device(tiles, tile_index, pose_bin, bin_gain, cutoffs):
    slab_pos = lax.axis_index("slab")
    group_pos = lax.axis_index("particle")
    half_pos = lax.axis_index("half")
    side_pos = slab_pos % 2
    everyone = ("particle", "slab", "half")
    tile_width = 2 * TILE_ROWS * BOX
    touched = tile_index.shape[2]
    flat_tiles = tiles[0].reshape(-1, tile_width)
    entry_slot = tile_index[0].reshape(1, -1)
    bin_ids = jnp.arange(bin_gain.shape[1], dtype=jnp.int32)
    particle_gain = jnp.sum(
        jnp.where(pose_bin[0][:, None] == bin_ids[None, :], bin_gain[0][None, :].astype(f32), 0.0),
        axis=1,
    )
    entry_gain = jnp.repeat(particle_gain, touched).reshape(1, -1)
    late = (slab_pos >= SLABS // 2).astype(jnp.int32)
    depth_pos = group_pos * 2 + side_pos
    own_line = (depth_pos + jnp.array([0, 2, 4, -2], jnp.int32)) % 8 // 2
    sent_line = (depth_pos + jnp.array([3, -3, 1, -1], jnp.int32)) % 8 // 2
    sent_plane = jnp.where(late == 1, (8 - 2 * sent_line) % 8, 7 - 2 * sent_line)
    plane_list = jnp.concatenate([2 * own_line + late, sent_plane]).astype(jnp.int32)
    flags = jnp.concatenate([(slab_pos == 0) & (own_line == 0), (slab_pos == 16) & (sent_line == 0)])
    entries = len(flat_tiles)
    heights = [BLOCKS, BLOCKS, BLOCKS // 2, BLOCKS // 2] + [BLOCKS] * 5
    row_in = pl.BlockSpec((1, entries), lambda i: (0, 0))
    own, ahead, far_a, far_b, behind, *sent = pl.pallas_call(
        place_kernel,
        grid=(2 * TILE_ROWS,),
        out_shape=tuple(jax.ShapeDtypeStruct((h, tile_width), f32) for h in heights),
        in_specs=[
            SMEM,
            SMEM,
            row_in,
            row_in,
            pl.BlockSpec((entries, BOX), lambda i: (0, i)),
            pl.BlockSpec((entries, BOX), lambda i: (0, i // 8 * 8 + (8 - i % 8) % 8)),
        ],
        out_specs=tuple(pl.BlockSpec((h, BOX), lambda i: (0, i)) for h in heights),
        scratch_shapes=[pltpu.VMEM((4 * BLOCKS, entries), bf16)] * 3
        + [pltpu.VMEM((BOX, BOX), bf16), pltpu.VMEM((4 * BLOCKS, BOX), f32)],
        name="place",
    )(plane_list, flags.astype(jnp.int32), entry_slot, entry_gain, flat_tiles, flat_tiles)
    here = ("particle", "slab")
    up, down = ring_pairs(1), ring_pairs(-1)
    rise, sink = lax.ppermute(far_a, here, up), lax.ppermute(far_b, here, down)
    come = [lax.ppermute(part, here, mirror_pairs(e)) for part, e in zip(sent, (3, -3, 1, -1))]
    cut = BLOCKS // 2
    rise = jnp.concatenate([come[0][:cut] + rise, come[0][cut:]], axis=0)
    sink = jnp.concatenate([come[1][:cut], come[1][cut:] + sink], axis=0)
    rise, sink = lax.ppermute(rise, here, up), lax.ppermute(sink, here, down)
    rise, sink = lax.ppermute(ahead + rise, here, up), lax.ppermute(behind + sink, here, down)
    rise, sink = lax.ppermute(come[2] + rise, here, up), lax.ppermute(come[3] + sink, here, down)
    plane = (slab_pos * 8 + group_pos * 2 + late).reshape(1)

    constants = [jnp.asarray(t) for t in tables()]
    square = (2 * BOX, BOX)
    sent = pl.pallas_call(
        planes_kernel,
        out_shape=jax.ShapeDtypeStruct((SENDERS * PER, LANES), f32),
        in_specs=[SMEM, SMEM] + [VMEM] * 7,
        out_specs=VMEM,
        scratch_shapes=[pltpu.VMEM(square, bf16)] * 2 + [pltpu.VMEM((BOX, BOX), f32)],
        name="planes",
    )(cutoffs, plane, own, rise, sink, *constants[:4])
    gathered = lax.all_to_all(
        sent.reshape(SENDERS, PER, LANES), ("particle", "slab"), split_axis=0, concat_axis=0, tiled=True
    ).reshape(SENDERS * PER, LANES)

    rows_block = (1, 2, BOX, LANES)
    rows_spec = pl.BlockSpec(rows_block, lambda b: (b, 0, 0, 0))
    rows_shape = jax.ShapeDtypeStruct((BANDS, 2, BOX, LANES), f32)
    row_spec = pl.BlockSpec((1, BOX, LANES), lambda b: (b, 0, 0))
    row_shape = jax.ShapeDtypeStruct((BANDS, BOX, LANES), f32)
    edge_spec = pl.BlockSpec((BOX, LANES), lambda b: (0, 0))
    edge_shape = jax.ShapeDtypeStruct((BOX, LANES), f32)
    own, leaving = pl.pallas_call(
        depth_kernel,
        grid=(BANDS,),
        out_shape=(rows_shape, rows_shape),
        in_specs=[
            SMEM,
            pl.BlockSpec((SENDERS * PER, LANES), lambda b: (0, 0)),
            pl.BlockSpec((BOX, BOX), lambda b: (0, 0)),
            pl.BlockSpec((BOX, BOX), lambda b: (0, 0)),
        ],
        out_specs=(rows_spec, rows_spec),
        name="depth",
    )(half_pos.reshape(1), gathered, *constants[4:])
    other = lax.ppermute(leaving, "half", [(0, 1), (1, 0)])
    first, second, edge = pl.pallas_call(
        square_kernel,
        grid=(BANDS,),
        out_shape=(row_shape, row_shape, edge_shape),
        in_specs=[rows_spec, rows_spec],
        out_specs=(row_spec, row_spec, edge_spec),
        name="square",
    )(own, other)
    before = lax.ppermute(second, everyone, row_pairs(1, 0))
    after = lax.ppermute(first, everyone, row_pairs(-1, 0))
    edge_here = lax.ppermute(edge, everyone, row_pairs(0, 1))
    edge_before = lax.ppermute(edge, everyone, row_pairs(1, 1))
    edge_after = lax.ppermute(edge, everyone, row_pairs(-1, 1))
    swap = (side_pos != half_pos).astype(jnp.int32).reshape(1)
    block_spec = pl.BlockSpec((2, BOX, LANES), lambda b: (0, 0, 0))
    block_shape = jax.ShapeDtypeStruct((2, BOX, LANES), f32)
    near, far = pl.pallas_call(
        blend_kernel,
        grid=(BANDS,),
        out_shape=(block_shape, block_shape),
        in_specs=[SMEM, rows_spec, rows_spec] + [row_spec] * 4 + [edge_spec] * 3,
        out_specs=(block_spec, block_spec),
        scratch_shapes=[pltpu.VMEM((2, 3, BOX, LANES), f32)],
        name="blend",
    )(swap, own, other, first, second, before, after, edge_here, edge_before, edge_after)
    near = lax.ppermute(near, everyone, home_pairs(0))
    far = lax.ppermute(far, everyone, home_pairs(1))
    low = jnp.where(half_pos == 0, near, far)
    high = jnp.where(half_pos == 0, far, near)
    refined = jnp.concatenate([low, high], axis=2)
    return jnp.transpose(refined, (1, 0, 2))[None]


def solution(mesh):
    placed = (
        P("half", "particle", "slab", None),
        P("half", "particle", "slab"),
        P("half", "particle"),
        P("half", None),
        P(),
    )
    return jax.shard_map(
        on_device,
        mesh=mesh,
        in_specs=placed,
        out_specs=P("half", None, ("particle", "slab"), None),
        check_vma=False,
    )
```

```python
import math

import jax
import jax.numpy as jnp
import numpy as np
from jax import lax
from jax.experimental import pallas as pl
from jax.experimental.pallas import tpu as pltpu
from jax.sharding import PartitionSpec as P

BOX = 256
HALF = BOX // 2
TILE_ROWS = 8
BLOCKS = BOX // TILE_ROWS
BANDS = 6
PACE = 2
GROUPS = 4
SLABS = 32
SENDERS = GROUPS * SLABS
PER = BANDS * 8
LANES = 128
error_floor = 1.0
bf16 = jnp.bfloat16
f32 = jnp.float32
VMEM = pl.BlockSpec(memory_space=pltpu.VMEM)
SMEM = pl.BlockSpec(memory_space=pltpu.SMEM)


def split(table):
    high = table.astype(np.float32).astype(jnp.bfloat16)
    low = (table - high.astype(np.float64)).astype(np.float32).astype(jnp.bfloat16)
    return high, low


def angles(left, right):
    return (np.outer(left, right) % BOX) * (2.0 * math.pi / BOX)


def tables():
    places = np.arange(BOX)
    block = places % 64
    y_order = (block % 32 * 2 + block // 32) * 4 + places // 64
    ky_order = (places % BLOCKS) * TILE_ROWS + places // BLOCKS
    turn = angles(y_order, ky_order)
    cosine, sine = np.cos(turn), np.sin(turn)
    along_y = np.stack(split(cosine) + split(sine))
    turn = angles(places, places)
    along_x = np.stack(split(np.cos(turn)) + split(np.sin(turn)))
    sender = np.arange(SENDERS)
    group, slab = sender // SLABS, sender % SLABS
    plane = slab * 8 + group * 2 + (slab >= SLABS // 2)
    turn = angles(places, plane)
    even, odd = np.cos(turn), -np.sin(turn)
    odd[:, 0] = np.cos(math.pi * places)
    along_z = np.stack(split(np.concatenate([even, odd], axis=1) / BOX))
    return along_y, along_x, along_z


def two(value):
    high = value.astype(bf16)
    return high, (value - high.astype(f32)).astype(bf16)


def dot(a, b):
    return jnp.dot(a, b, preferred_element_type=f32)


def mark(rows, slots, gains):
    return jnp.where(rows == slots, gains, 0.0).astype(bf16)


def place_kernel(slab_ref, group_ref, index_ref, bin_ref, gain_ref, tile_ref, *refs):
    outs, (kept_mark, sent_mark, sent_mark_first, turn, saved) = refs[:9], refs[9:]
    step = pl.program_id(0)
    slab, group = slab_ref[0], group_ref[0]
    depth, late = group * 2 + slab % 2, slab // (SLABS // 2)
    row = lax.broadcasted_iota(jnp.int32, (BLOCKS, BOX), 0)
    col = lax.broadcasted_iota(jnp.int32, (BLOCKS, BOX), 1)
    own_line = [((depth + d) & 7) // 2 for d in (0, 2, 4, 6)]
    sent_line = [((depth + d) & 7) // 2 for d in (3, 5, 1, 7)]

    @pl.when(step == 0)
    def _():
        touched, particles = index_ref.shape
        entries = touched * particles
        bins = gain_ref.shape[1]
        line = lax.broadcasted_iota(jnp.int32, (particles, entries), 0)
        wide = lax.broadcasted_iota(jnp.int32, (particles, entries), 1)
        spread = jnp.where(wide // touched == line, 1.0, 0.0).astype(bf16)
        slots = dot(index_ref[...].astype(f32).astype(bf16), spread)
        line = lax.broadcasted_iota(jnp.int32, slots.shape, 0)
        wide = lax.broadcasted_iota(jnp.int32, slots.shape, 1)
        slots = jnp.sum(jnp.where(wide % touched == line, slots, 0.0), axis=0, keepdims=True)
        slots = jnp.broadcast_to(slots, (BLOCKS, entries)).astype(jnp.int32)
        line = lax.broadcasted_iota(jnp.int32, (bins, bins), 0)
        wide = lax.broadcasted_iota(jnp.int32, (bins, bins), 1)
        table = jnp.broadcast_to(gain_ref[...].astype(f32), (bins, bins))
        table = jnp.sum(jnp.where(line == wide, table, 0.0), axis=1, keepdims=True)
        line = lax.broadcasted_iota(jnp.int32, (bins, particles), 0)
        gains = jnp.where(line == bin_ref[...], table, 0.0).astype(bf16)
        gains = jnp.sum(dot(gains, spread), axis=0, keepdims=True)
        gains = jnp.broadcast_to(gains, (BLOCKS, entries))
        for i in range(4):
            rows = pl.ds(i * BLOCKS, BLOCKS)
            kept_mark[rows, :] = mark((2 * own_line[i] + late) * BLOCKS + row, slots, gains)
            start = jnp.where(late == 1, (8 - 2 * sent_line[i]) & 7, 7 - 2 * sent_line[i]) * BLOCKS
            sent_mark[rows, :] = mark(start + BLOCKS - 1 - row, slots, gains)
            sent_mark_first[rows, :] = mark(start + ((BLOCKS - row) & (BLOCKS - 1)), slots, gains)
        line = lax.broadcasted_iota(jnp.int32, (BOX, BOX), 0)
        wide = lax.broadcasted_iota(jnp.int32, (BOX, BOX), 1)
        turn[...] = jnp.where(((line + wide) & (BOX - 1)) == 0, 1.0, 0.0).astype(bf16)

    sign = jnp.where(step == 1, -1.0, 1.0)
    tile = tile_ref[...].reshape(-1, TILE_ROWS * BOX)
    for r in range(TILE_ROWS):
        cols = pl.ds(r * BOX, BOX)
        back = (TILE_ROWS - r) % TILE_ROWS * BOX
        kept = dot(kept_mark[...], tile[:, r * BOX : (r + 1) * BOX])
        flipped = (dot(tile[:, back : back + BOX], turn[...]) * sign).astype(bf16)
        sent = dot((sent_mark if r else sent_mark_first)[...], flipped)
        if r == 0:
            first = (row == 0) & (col == 0)
            last_sent = saved[...]
            saved[...] = sent
        parts = []
        for i in range(4):
            part = kept[i * BLOCKS : (i + 1) * BLOCKS]
            if r == 0:
                part = jnp.where(first & (step == 1) & (slab == 0) & (own_line[i] == 0), 0.0, part)
            parts.append(part)
        for i in range(4):
            part = sent[i * BLOCKS : (i + 1) * BLOCKS]
            alone = 0.0
            if r == 0:
                alone = jnp.where(first & (step == 1), last_sent[i * BLOCKS : (i + 1) * BLOCKS], 0.0)
            parts.append(jnp.where((slab == SLABS // 2) & (sent_line[i] == 0), alone, part))
        parts[2:3] = [parts[2][: BLOCKS // 2], parts[2][BLOCKS // 2 :]]
        for out_ref, part in zip(outs, parts):
            out_ref[:, cols] = part


def fill(four_ref, out_ref, down):
    for third, low in enumerate((0, 0, 1) if down else (0, 1, 0)):
        cosine, sine = four_ref[low], four_ref[2 + low]
        start = third * 2 * BOX
        for i in range(2):
            for j in range(2):
                block = cosine if i == j else (sine if (i == 1) != down else -sine)
                if down:
                    out_ref[start + i * BOX : start + (i + 1) * BOX, j * BOX : (j + 1) * BOX] = block
                else:
                    out_ref[i * BOX : (i + 1) * BOX, start + j * BOX : start + (j + 1) * BOX] = block


def planes_kernel(cut_ref, kz_ref, own_ref, up_ref, down_ref, cy_ref, cx_ref, out_ref, sh, sl, radius, y_ref, x_ref):
    fill(cy_ref, y_ref, False)
    fill(cx_ref, x_ref, True)
    alone = kz_ref[0] == 0
    for i in range(16):
        cols = pl.ds(i * BOX, BOX)
        rows = pl.ds(i * BLOCKS, BLOCKS)
        whole = own_ref[:, cols] + up_ref[:, cols] + down_ref[:, cols]
        if i == TILE_ROWS:
            last = whole[0:1, 0:1]
        sh[rows, :], sl[rows, :] = two(whole)
    line = lax.broadcasted_iota(jnp.int32, (BOX, BOX), 0)
    col = lax.broadcasted_iota(jnp.int32, (BOX, BOX), 1)
    ky = (line & (BLOCKS - 1)) * TILE_ROWS + (line >> 5)
    ky = ((ky + HALF) & (BOX - 1)) - HALF
    kx = ((col + HALF) & (BOX - 1)) - HALF
    kz = ((kz_ref[0] + HALF) & (BOX - 1)) - HALF
    radius[...] = (ky * ky + kx * kx + kz * kz).astype(f32)

    @pl.loop(0, BANDS)
    def _(b):
        limit = (cut_ref[b] * cut_ref[b]).astype(f32)
        mask = jnp.where(radius[...] <= limit, 1.0, 0.0).astype(bf16)
        mask = jnp.concatenate([mask, mask], axis=0)
        high, low = sh[...] * mask, sl[...] * mask
        mid = dot(y_ref[...], jnp.concatenate([high, high, low], axis=0))
        high, low = two(jnp.concatenate([mid[:BOX], mid[BOX:]], axis=1))
        both = dot(jnp.concatenate([high, low, high], axis=1), x_ref[...])
        even, odd = both[:, :BOX], both[:, BOX:]
        top = jnp.where(cut_ref[b] >= HALF, last, 0.0)
        odd = jnp.where(alone, jnp.broadcast_to(top, odd.shape), odd)
        for c, part in enumerate((even, odd)):
            for j in range(4):
                for side in range(2):
                    for odd_block in range(2):
                        start = j * 64 + odd_block * 32
                        block = part[start : start + 32, side * LANES : (side + 1) * LANES]
                        goal = 2 * (odd_block ^ side) + side
                        out_ref[pl.ds(goal * PER + b * 8 + c * 4 + j, 32, stride=4 * PER), :] = block


def depth_kernel(core_ref, come_ref, z_ref, own_ref, other_ref, own_edge_ref, other_edge_ref, own_edge, other_edge):
    step = pl.program_id(0)
    lane = lax.broadcasted_iota(jnp.int32, (BOX, LANES), 1)
    turn = jnp.concatenate([z_ref[0], z_ref[1], z_ref[0]], axis=1)
    for out_ref, edge, core in (
        (own_ref, own_edge, core_ref[0]),
        (other_ref, other_edge, 1 - core_ref[0]),
    ):
        found = jnp.where(step == 0, 0.0, edge[...])
        for i in range(PACE):
            start = (step * PACE + i) * 8 + core * 2
            sides = [
                jnp.concatenate(
                    [come_ref[pl.ds(start + c * 4 + j, SENDERS, stride=PER), :] for j in range(2)], axis=1
                )
                for c in range(2)
            ]
            high, low = two(jnp.concatenate(sides, axis=0))
            full = dot(turn, jnp.concatenate([high, high, low], axis=0))
            for row in range(2):
                part = full[:, row * LANES : (row + 1) * LANES]
                out_ref[i, row] = part
                spot = (step * PACE + i) * 4 + row * 2
                found = jnp.where((lane >> 1) == (spot >> 1), pltpu.roll(part, spot + 1, 1), found)
        edge[...] = found

    @pl.when(step == BANDS // PACE - 1)
    def _():
        narrow = lax.broadcasted_iota(jnp.int32, (64, LANES), 1)
        for out_ref, edge in ((own_edge_ref, own_edge), (other_edge_ref, other_edge)):
            packed = edge[0:64, :]
            for q in range(1, 4):
                packed = jnp.where((narrow >> 5) == q, pltpu.roll(edge[q * 64 : (q + 1) * 64, :], q * 32, 1), packed)
            out_ref[...] = packed


def square_kernel(own_ref, other_ref, own_edge_ref, other_edge_ref, first_ref, second_ref, border):
    step = pl.program_id(0)
    lane = lax.broadcasted_iota(jnp.int32, (BOX, LANES), 1)

    @pl.when(step == 0)
    def _():
        gap = own_edge_ref[...] - other_edge_ref[...]
        gap = gap * gap
        for q in range(4):
            border[q * 64 : (q + 1) * 64, :] = pltpu.roll(gap, (LANES - q * 32) % LANES, 1)

    for i in range(PACE):
        for row, ref in enumerate((first_ref, second_ref)):
            gap = own_ref[i, row] - other_ref[i, row]
            square = gap * gap
            spot = (step * PACE + i) * 4 + row * 2
            beyond = pltpu.roll(border[...], LANES - 1 - spot, 1)
            left = pltpu.roll(jnp.where(lane == LANES - 1, beyond, square), 1, 1)
            right = pltpu.roll(jnp.where(lane == 0, beyond, square), LANES - 1, 1)
            ref[i] = square + left + right


def blend_kernel(
    swap_ref, own_ref, other_ref, first_ref, second_ref, before_ref, after_ref, out_a_ref, out_b_ref, sums
):
    step = pl.program_id(0)

    @pl.when(step == 0)
    def _():
        sums[...] = jnp.zeros_like(sums)

    for row in range(2):
        mine, theirs, total = sums[row, 0], sums[row, 1], sums[row, 2]
        for i in range(PACE):
            wide = first_ref[i] + second_ref[i] + (before_ref if row == 0 else after_ref)[i]
            full = wide + pltpu.roll(wide, 1, 0) + pltpu.roll(wide, BOX - 1, 0)
            weight = 1.0 / (full / 27.0 + error_floor)
            mine = mine + weight * own_ref[i, row]
            theirs = theirs + weight * other_ref[i, row]
            total = total + weight
        sums[row, 0], sums[row, 1], sums[row, 2] = mine, theirs, total

    @pl.when(step == BANDS // PACE - 1)
    def _():
        swap = swap_ref[0] == 1
        for row in range(2):
            mine = sums[row, 0] / sums[row, 2]
            theirs = sums[row, 1] / sums[row, 2]
            out_a_ref[row] = jnp.where(swap, theirs, mine)
            out_b_ref[row] = jnp.where(swap, mine, theirs)


def chip(depth, spot):
    return depth // 2 * SLABS + spot * 2 + depth % 2


def mirror_pairs(ahead):
    pairs = []
    for depth in range(8):
        for spot in range(16):
            goal = (depth, 15 - spot)
            if spot >= 8 and (depth + ahead) % 8 // 2 == 0:
                goal = ((depth + 1) % 8, 15 - spot) if depth % 2 else ((depth - 1) % 8, (16 - spot) % 8)
            pairs.append((chip(depth, spot), chip(*goal)))
    return pairs


def ring_pairs(step):
    return [(chip(d, s), chip((d + step) % 8, s)) for d in range(8) for s in range(16)]


def holder(block, side, core):
    return (2 * (block ^ side) + side) * 2 + core


def row_pairs(step):
    pairs = []
    for n in range(SENDERS):
        goal = (n + step) % SENDERS
        pairs += [(holder(n // 2, side, n % 2), holder(goal // 2, side, goal % 2)) for side in range(2)]
    return pairs


def edge_pairs(flip):
    return [
        (holder(block, side, core), holder(block, 1 - side, core ^ flip))
        for block in range(64)
        for side in range(2)
        for core in range(2)
    ]


def home_pairs(flip):
    return [
        (holder(block, side, core), (2 * block + core) * 2 + (side ^ flip))
        for block in range(64)
        for side in range(2)
        for core in range(2)
    ]


def on_device(tiles, tile_index, pose_bin, bin_gain, cutoffs):
    slab_pos = lax.axis_index("slab")
    group_pos = lax.axis_index("particle")
    half_pos = lax.axis_index("half")
    side_pos = slab_pos % 2
    everyone = ("particle", "slab", "half")
    tile_width = 2 * TILE_ROWS * BOX
    _, particles, touched, _ = tiles.shape
    entries = particles * touched
    late = (slab_pos >= SLABS // 2).astype(jnp.int32)
    heights = [BLOCKS, BLOCKS, BLOCKS // 2, BLOCKS // 2] + [BLOCKS] * 5
    own, ahead, far_a, far_b, behind, *sent = pl.pallas_call(
        place_kernel,
        grid=(2,),
        out_shape=tuple(jax.ShapeDtypeStruct((h, tile_width), f32) for h in heights),
        in_specs=[
            SMEM,
            SMEM,
            pl.BlockSpec((touched, particles), lambda i: (0, 0)),
            pl.BlockSpec((1, particles), lambda i: (0, 0)),
            pl.BlockSpec((1, bin_gain.shape[1]), lambda i: (0, 0)),
            pl.BlockSpec((particles, touched, tile_width // 2), lambda i: (0, 0, i)),
        ],
        out_specs=tuple(pl.BlockSpec((h, tile_width // 2), lambda i: (0, i)) for h in heights),
        scratch_shapes=[pltpu.VMEM((4 * BLOCKS, entries), bf16)] * 3
        + [pltpu.VMEM((BOX, BOX), bf16), pltpu.VMEM((4 * BLOCKS, BOX), f32)],
        name="place",
    )(slab_pos.reshape(1), group_pos.reshape(1), tile_index[0].T, pose_bin, bin_gain, tiles[0])
    here = ("particle", "slab")
    up, down = ring_pairs(1), ring_pairs(-1)
    rise, sink = lax.ppermute(far_a, here, up), lax.ppermute(far_b, here, down)
    come = [lax.ppermute(part, here, mirror_pairs(e)) for part, e in zip(sent, (3, -3, 1, -1))]
    cut = BLOCKS // 2
    rise = jnp.concatenate([come[0][:cut] + rise, come[0][cut:]], axis=0)
    sink = jnp.concatenate([come[1][:cut], come[1][cut:] + sink], axis=0)
    rise, sink = lax.ppermute(rise, here, up), lax.ppermute(sink, here, down)
    rise, sink = lax.ppermute(ahead + rise, here, up), lax.ppermute(behind + sink, here, down)
    rise, sink = lax.ppermute(come[2] + rise, here, up), lax.ppermute(come[3] + sink, here, down)
    plane = (slab_pos * 8 + group_pos * 2 + late).reshape(1)

    constants = [jnp.asarray(t) for t in tables()]
    square = (2 * BOX, BOX)
    sent = pl.pallas_call(
        planes_kernel,
        out_shape=jax.ShapeDtypeStruct((SENDERS * PER, LANES), f32),
        in_specs=[SMEM, SMEM] + [VMEM] * 5,
        out_specs=VMEM,
        scratch_shapes=[
            pltpu.VMEM(square, bf16),
            pltpu.VMEM(square, bf16),
            pltpu.VMEM((BOX, BOX), f32),
            pltpu.VMEM((2 * BOX, 6 * BOX), bf16),
            pltpu.VMEM((6 * BOX, 2 * BOX), bf16),
        ],
        name="planes",
    )(cutoffs, plane, own, rise, sink, *constants[:2])
    gathered = lax.all_to_all(
        sent.reshape(SENDERS, PER, LANES), ("particle", "slab"), split_axis=0, concat_axis=0, tiled=True
    ).reshape(SENDERS * PER, LANES)

    steps = BANDS // PACE
    rows_spec = pl.BlockSpec((PACE, 2, BOX, LANES), lambda b: (b, 0, 0, 0))
    rows_shape = jax.ShapeDtypeStruct((BANDS, 2, BOX, LANES), f32)
    row_spec = pl.BlockSpec((PACE, BOX, LANES), lambda b: (b, 0, 0))
    row_shape = jax.ShapeDtypeStruct((BANDS, BOX, LANES), f32)
    edge_spec = pl.BlockSpec((64, LANES), lambda b: (0, 0))
    edge_shape = jax.ShapeDtypeStruct((64, LANES), f32)
    edge_room = pltpu.VMEM((BOX, LANES), f32)
    own, leaving, own_edge, other_edge = pl.pallas_call(
        depth_kernel,
        grid=(steps,),
        out_shape=(rows_shape, rows_shape, edge_shape, edge_shape),
        in_specs=[
            SMEM,
            pl.BlockSpec((SENDERS * PER, LANES), lambda b: (0, 0)),
            pl.BlockSpec((2, BOX, BOX), lambda b: (0, 0, 0)),
        ],
        out_specs=(rows_spec, rows_spec, edge_spec, edge_spec),
        scratch_shapes=[edge_room, edge_room],
        name="depth",
    )(half_pos.reshape(1), gathered, constants[2])
    own_edge = lax.ppermute(own_edge, everyone, edge_pairs(0))
    other_edge = lax.ppermute(other_edge, everyone, edge_pairs(1))
    other = lax.ppermute(leaving, "half", [(0, 1), (1, 0)])
    first, second = pl.pallas_call(
        square_kernel,
        grid=(steps,),
        out_shape=(row_shape, row_shape),
        in_specs=[rows_spec, rows_spec, edge_spec, edge_spec],
        out_specs=(row_spec, row_spec),
        scratch_shapes=[edge_room],
        name="square",
    )(own, other, own_edge, other_edge)
    before = lax.ppermute(second, everyone, row_pairs(1))
    after = lax.ppermute(first, everyone, row_pairs(-1))
    swap = (side_pos != half_pos).astype(jnp.int32).reshape(1)
    block_spec = pl.BlockSpec((2, BOX, LANES), lambda b: (0, 0, 0))
    block_shape = jax.ShapeDtypeStruct((2, BOX, LANES), f32)
    near, far = pl.pallas_call(
        blend_kernel,
        grid=(steps,),
        out_shape=(block_shape, block_shape),
        in_specs=[SMEM, rows_spec, rows_spec] + [row_spec] * 4,
        out_specs=(block_spec, block_spec),
        scratch_shapes=[pltpu.VMEM((2, 3, BOX, LANES), f32)],
        name="blend",
    )(swap, own, other, first, second, before, after)
    near = lax.ppermute(near, everyone, home_pairs(0))
    far = lax.ppermute(far, everyone, home_pairs(1))
    low = jnp.where(half_pos == 0, near, far)
    high = jnp.where(half_pos == 0, far, near)
    refined = jnp.concatenate([low, high], axis=2)
    return jnp.transpose(refined, (1, 0, 2))[None]


def solution(mesh):
    placed = (
        P("half", "particle", "slab", None),
        P("half", "particle", "slab"),
        P("half", "particle"),
        P("half", None),
        P(),
    )
    return jax.shard_map(
        on_device,
        mesh=mesh,
        in_specs=placed,
        out_specs=P("half", None, ("particle", "slab"), None),
        check_vma=False,
    )
```

```python
import math

import jax
import jax.numpy as jnp
import numpy as np
from jax import lax
from jax.experimental import pallas as pl
from jax.experimental.pallas import tpu as pltpu
from jax.sharding import PartitionSpec as P

BOX = 256
HALF = BOX // 2
TILE_ROWS = 8
BLOCKS = BOX // TILE_ROWS
BANDS = 6
PACE = 2
GROUPS = 4
SLABS = 32
SENDERS = GROUPS * SLABS
PER = BANDS * 8
LANES = 128
error_floor = 1.0
bf16 = jnp.bfloat16
f32 = jnp.float32
VMEM = pl.BlockSpec(memory_space=pltpu.VMEM)
SMEM = pl.BlockSpec(memory_space=pltpu.SMEM)


def split(table):
    high = table.astype(np.float32).astype(jnp.bfloat16)
    low = (table - high.astype(np.float64)).astype(np.float32).astype(jnp.bfloat16)
    return high, low


def angles(left, right):
    return (np.outer(left, right) % BOX) * (2.0 * math.pi / BOX)


def tables():
    places = np.arange(BOX)
    near = np.arange(HALF)
    along_y, along_x = [], []
    for odd in range(2):
        turn = angles(near, near % BLOCKS * TILE_ROWS + near // BLOCKS * 2 + odd)
        cosine, sine = np.cos(turn), np.sin(turn)
        along_y.append(np.stack(split(np.block([[cosine, -sine], [sine, cosine]]))))
        turn = angles(2 * near + odd, near)
        cosine, sine = np.cos(turn), np.sin(turn)
        along_x.append(np.stack(split(np.block([[cosine, sine], [-sine, cosine]]))))
    along_y, along_x = np.stack(along_y), np.stack(along_x)
    sender = np.arange(SENDERS)
    group, slab = sender // SLABS, sender % SLABS
    plane = slab * 8 + group * 2 + (slab >= SLABS // 2)
    turn = angles(places, plane)
    even, odd = np.cos(turn), -np.sin(turn)
    odd[:, 0] = np.cos(math.pi * places)
    along_z = np.stack(split(np.concatenate([even, odd], axis=1) / BOX))
    return along_y, along_x, along_z


def two(value):
    high = value.astype(bf16)
    return high, (value - high.astype(f32)).astype(bf16)


def dot(a, b):
    return jnp.dot(a, b, preferred_element_type=f32)


def mark(rows, slots, gains):
    return jnp.where(rows == slots, gains, 0.0).astype(bf16)


def place_kernel(slab_ref, group_ref, index_ref, bin_ref, gain_ref, tile_ref, *refs):
    outs, (kept_mark, sent_mark, sent_mark_first, turn, moved, saved) = refs[:9], refs[9:]
    step = pl.program_id(0)
    slab, group = slab_ref[0], group_ref[0]
    depth, late = group * 2 + slab % 2, slab // (SLABS // 2)
    row = lax.broadcasted_iota(jnp.int32, (BLOCKS, BOX), 0)
    col = lax.broadcasted_iota(jnp.int32, (BLOCKS, BOX), 1)
    own_line = [((depth + d) & 7) // 2 for d in (0, 2, 4, 6)]
    sent_line = [((depth + d) & 7) // 2 for d in (3, 5, 1, 7)]

    @pl.when(step == 0)
    def _():
        touched, particles = index_ref.shape
        entries = touched * particles
        bins = gain_ref.shape[1]
        line = lax.broadcasted_iota(jnp.int32, (particles, entries), 0)
        wide = lax.broadcasted_iota(jnp.int32, (particles, entries), 1)
        spread = jnp.where(wide // touched == line, 1.0, 0.0).astype(bf16)
        slots = dot(index_ref[...].astype(f32).astype(bf16), spread)
        line = lax.broadcasted_iota(jnp.int32, slots.shape, 0)
        wide = lax.broadcasted_iota(jnp.int32, slots.shape, 1)
        slots = jnp.sum(jnp.where(wide % touched == line, slots, 0.0), axis=0, keepdims=True)
        slots = jnp.broadcast_to(slots, (BLOCKS, entries)).astype(jnp.int32)
        line = lax.broadcasted_iota(jnp.int32, (bins, bins), 0)
        wide = lax.broadcasted_iota(jnp.int32, (bins, bins), 1)
        table = jnp.broadcast_to(gain_ref[...].astype(f32), (bins, bins))
        table = jnp.sum(jnp.where(line == wide, table, 0.0), axis=1, keepdims=True)
        line = lax.broadcasted_iota(jnp.int32, (bins, particles), 0)
        gains = jnp.where(line == bin_ref[...], table, 0.0).astype(bf16)
        gains = jnp.sum(dot(gains, spread), axis=0, keepdims=True)
        gains = jnp.broadcast_to(gains, (BLOCKS, entries))
        for i in range(4):
            rows = pl.ds(i * BLOCKS, BLOCKS)
            kept_mark[rows, :] = mark((2 * own_line[i] + late) * BLOCKS + row, slots, gains)
            start = jnp.where(late == 1, (8 - 2 * sent_line[i]) & 7, 7 - 2 * sent_line[i]) * BLOCKS
            sent_mark[rows, :] = mark(start + BLOCKS - 1 - row, slots, gains)
            sent_mark_first[rows, :] = mark(start + ((BLOCKS - row) & (BLOCKS - 1)), slots, gains)
        line = lax.broadcasted_iota(jnp.int32, (BOX, BOX), 0)
        wide = lax.broadcasted_iota(jnp.int32, (BOX, BOX), 1)
        wide = (wide & (HALF - 1)) * 2 + (wide >> 7)
        turn[:, :BOX] = jnp.where(line == wide, 1.0, 0.0).astype(bf16)
        turn[:, BOX:] = jnp.where(((line + wide) & (BOX - 1)) == 0, 1.0, 0.0).astype(bf16)

    sign = jnp.where(step == 1, -1.0, 1.0)
    tile = tile_ref[...].reshape(-1, TILE_ROWS * BOX)
    for r in range(TILE_ROWS):
        both = dot(tile[:, r * BOX : (r + 1) * BOX], turn[...])
        moved[r, 0] = both[:, :BOX].astype(bf16)
        moved[r, 1] = (both[:, BOX:] * sign).astype(bf16)
    for r in range(TILE_ROWS):
        cols = pl.ds(r * BOX, BOX)
        kept = dot(kept_mark[...], moved[r, 0])
        sent = dot((sent_mark if r else sent_mark_first)[...], moved[(TILE_ROWS - r) % TILE_ROWS, 1])
        if r == 0:
            first = (row == 0) & (col == 0)
            last_sent = saved[...]
            saved[...] = sent
        parts = []
        for i in range(4):
            part = kept[i * BLOCKS : (i + 1) * BLOCKS]
            if r == 0:
                part = jnp.where(first & (step == 1) & (slab == 0) & (own_line[i] == 0), 0.0, part)
            parts.append(part)
        for i in range(4):
            part = sent[i * BLOCKS : (i + 1) * BLOCKS]
            alone = 0.0
            if r == 0:
                alone = jnp.where(first & (step == 1), last_sent[i * BLOCKS : (i + 1) * BLOCKS], 0.0)
            parts.append(jnp.where((slab == SLABS // 2) & (sent_line[i] == 0), alone, part))
        parts[2:3] = [parts[2][: BLOCKS // 2], parts[2][BLOCKS // 2 :]]
        for out_ref, part in zip(outs, parts):
            out_ref[:, cols] = part


def beside(*parts):
    return jnp.concatenate(parts, axis=1)


def above(*parts):
    return jnp.concatenate(parts, axis=0)


def planes_kernel(cut_ref, kz_ref, own_ref, up_ref, down_ref, y_ref, x_ref, out_ref, sh, sl, radius):
    alone = kz_ref[0] == 0
    for i in range(16):
        c, r = divmod(i, TILE_ROWS)
        cols = pl.ds(i * BOX, BOX)
        rows = pl.ds(r % 2 * BOX + c * HALF + r // 2 * BLOCKS, BLOCKS)
        whole = own_ref[:, cols] + up_ref[:, cols] + down_ref[:, cols]
        if i == TILE_ROWS:
            last = whole[0:1, 0:1]
        sh[rows, :], sl[rows, :] = two(whole)
    line = lax.broadcasted_iota(jnp.int32, (BOX, BOX), 0)
    col = lax.broadcasted_iota(jnp.int32, (BOX, BOX), 1)
    ky = (line & (BLOCKS - 1)) * TILE_ROWS + ((line >> 5) & 3) * 2 + (line >> 7)
    kx = (col & (HALF - 1)) * 2 + (col >> 7)
    ky = ((ky + HALF) & (BOX - 1)) - HALF
    kx = ((kx + HALF) & (BOX - 1)) - HALF
    kz = ((kz_ref[0] + HALF) & (BOX - 1)) - HALF
    radius[...] = (ky * ky + kx * kx + kz * kz).astype(f32)
    upper = lax.broadcasted_iota(jnp.int32, (BLOCKS, 8, LANES), 1) < 4

    @pl.loop(0, BANDS // 2)
    def _(pair):
        parts = []
        for odd in range(2):
            sides = []
            for i in range(2):
                cut = cut_ref[pair * 2 + i]
                near = radius[odd * HALF : (odd + 1) * HALF, :] <= (cut * cut).astype(f32)
                mask = jnp.where(near, 1.0, 0.0).astype(bf16)
                mask = above(mask, mask)
                rows = pl.ds(odd * BOX, BOX)
                high, low = sh[rows, :] * mask, sl[rows, :] * mask
                sides.append(above(high, high, low))
            parts.append(dot(beside(y_ref[odd, 0], y_ref[odd, 1], y_ref[odd, 0]), beside(*sides)))
        plus, minus = parts[0] + parts[1], parts[0] - parts[1]
        mids = ([], [])
        for i in range(2):
            cols = slice(i * BOX, (i + 1) * BOX)
            real = two(above(plus[:HALF, cols], minus[:HALF, cols]))
            imag = two(above(plus[HALF:, cols], minus[HALF:, cols]))
            for odd in range(2):
                few = slice(odd * HALF, (odd + 1) * HALF)
                high = beside(real[0][:, few], imag[0][:, few])
                low = beside(real[1][:, few], imag[1][:, few])
                mids[odd].append(beside(high, low, high))
        parts = [dot(above(*mids[odd]), above(x_ref[odd, 0], x_ref[odd, 0], x_ref[odd, 1])) for odd in range(2)]
        for i in range(2):
            b = pair * 2 + i
            value = jnp.where(cut_ref[b] >= HALF, last, 0.0)
            first, second = parts[0][i * BOX : (i + 1) * BOX], parts[1][i * BOX : (i + 1) * BOX]
            for side, full in enumerate((first + second, first - second)):
                even, odd = full[:, :LANES], full[:, LANES:]
                odd = jnp.where(alone, jnp.broadcast_to(value, odd.shape), odd)
                even, odd = even.reshape(BLOCKS, 8, LANES), odd.reshape(BLOCKS, 8, LANES)
                out_ref[:, 3 * side, b] = jnp.where(upper, even, pltpu.roll(odd, 4, 1))
                out_ref[:, 2 - side, b] = jnp.where(upper, pltpu.roll(even, 4, 1), odd)


def depth_kernel(core_ref, come_ref, z_ref, own_ref, other_ref, own_edge_ref, other_edge_ref, own_edge, other_edge):
    step = pl.program_id(0)
    lane = lax.broadcasted_iota(jnp.int32, (BOX, LANES), 1)
    turn = jnp.concatenate([z_ref[0], z_ref[1], z_ref[0]], axis=1)
    for out_ref, edge, core in (
        (own_ref, own_edge, core_ref[0]),
        (other_ref, other_edge, 1 - core_ref[0]),
    ):
        found = jnp.where(step == 0, 0.0, edge[...])
        for i in range(PACE):
            start = (step * PACE + i) * 8 + core * 2
            sides = [
                jnp.concatenate(
                    [come_ref[pl.ds(start + c * 4 + j, SENDERS, stride=PER), :] for j in range(2)], axis=1
                )
                for c in range(2)
            ]
            high, low = two(jnp.concatenate(sides, axis=0))
            full = dot(turn, jnp.concatenate([high, high, low], axis=0))
            for row in range(2):
                part = full[:, row * LANES : (row + 1) * LANES]
                out_ref[i, row] = part
                spot = (step * PACE + i) * 4 + row * 2
                found = jnp.where((lane >> 1) == (spot >> 1), pltpu.roll(part, spot + 1, 1), found)
        edge[...] = found

    @pl.when(step == BANDS // PACE - 1)
    def _():
        narrow = lax.broadcasted_iota(jnp.int32, (64, LANES), 1)
        for out_ref, edge in ((own_edge_ref, own_edge), (other_edge_ref, other_edge)):
            packed = edge[0:64, :]
            for q in range(1, 4):
                packed = jnp.where((narrow >> 5) == q, pltpu.roll(edge[q * 64 : (q + 1) * 64, :], q * 32, 1), packed)
            out_ref[...] = packed


def square_kernel(own_ref, other_ref, own_edge_ref, other_edge_ref, first_ref, second_ref, border):
    step = pl.program_id(0)
    lane = lax.broadcasted_iota(jnp.int32, (BOX, LANES), 1)

    @pl.when(step == 0)
    def _():
        gap = own_edge_ref[...] - other_edge_ref[...]
        gap = gap * gap
        for q in range(4):
            border[q * 64 : (q + 1) * 64, :] = pltpu.roll(gap, (LANES - q * 32) % LANES, 1)

    for i in range(PACE):
        for row, ref in enumerate((first_ref, second_ref)):
            gap = own_ref[i, row] - other_ref[i, row]
            square = gap * gap
            spot = (step * PACE + i) * 4 + row * 2
            beyond = pltpu.roll(border[...], LANES - 1 - spot, 1)
            left = pltpu.roll(jnp.where(lane == LANES - 1, beyond, square), 1, 1)
            right = pltpu.roll(jnp.where(lane == 0, beyond, square), LANES - 1, 1)
            ref[i] = square + left + right


def blend_kernel(
    swap_ref, own_ref, other_ref, first_ref, second_ref, before_ref, after_ref, out_a_ref, out_b_ref, sums
):
    step = pl.program_id(0)

    @pl.when(step == 0)
    def _():
        sums[...] = jnp.zeros_like(sums)

    for row in range(2):
        mine, theirs, total = sums[row, 0], sums[row, 1], sums[row, 2]
        for i in range(PACE):
            wide = first_ref[i] + second_ref[i] + (before_ref if row == 0 else after_ref)[i]
            full = wide + pltpu.roll(wide, 1, 0) + pltpu.roll(wide, BOX - 1, 0)
            weight = 1.0 / (full / 27.0 + error_floor)
            mine = mine + weight * own_ref[i, row]
            theirs = theirs + weight * other_ref[i, row]
            total = total + weight
        sums[row, 0], sums[row, 1], sums[row, 2] = mine, theirs, total

    @pl.when(step == BANDS // PACE - 1)
    def _():
        swap = swap_ref[0] == 1
        for row in range(2):
            mine = sums[row, 0] / sums[row, 2]
            theirs = sums[row, 1] / sums[row, 2]
            out_a_ref[row] = jnp.where(swap, theirs, mine)
            out_b_ref[row] = jnp.where(swap, mine, theirs)


def chip(depth, spot):
    return depth // 2 * SLABS + spot * 2 + depth % 2


def mirror_pairs(ahead):
    pairs = []
    for depth in range(8):
        for spot in range(16):
            goal = (depth, 15 - spot)
            if spot >= 8 and (depth + ahead) % 8 // 2 == 0:
                goal = ((depth + 1) % 8, 15 - spot) if depth % 2 else ((depth - 1) % 8, (16 - spot) % 8)
            pairs.append((chip(depth, spot), chip(*goal)))
    return pairs


def ring_pairs(step):
    return [(chip(d, s), chip((d + step) % 8, s)) for d in range(8) for s in range(16)]


def holder(block, side, core):
    return (2 * (block ^ side) + side) * 2 + core


def row_pairs(step):
    pairs = []
    for n in range(SENDERS):
        goal = (n + step) % SENDERS
        pairs += [(holder(n // 2, side, n % 2), holder(goal // 2, side, goal % 2)) for side in range(2)]
    return pairs


def edge_pairs(flip):
    return [
        (holder(block, side, core), holder(block, 1 - side, core ^ flip))
        for block in range(64)
        for side in range(2)
        for core in range(2)
    ]


def home_pairs(flip):
    return [
        (holder(block, side, core), (2 * block + core) * 2 + (side ^ flip))
        for block in range(64)
        for side in range(2)
        for core in range(2)
    ]


def on_device(tiles, tile_index, pose_bin, bin_gain, cutoffs):
    slab_pos = lax.axis_index("slab")
    group_pos = lax.axis_index("particle")
    half_pos = lax.axis_index("half")
    side_pos = slab_pos % 2
    everyone = ("particle", "slab", "half")
    tile_width = 2 * TILE_ROWS * BOX
    _, particles, touched, _ = tiles.shape
    entries = particles * touched
    late = (slab_pos >= SLABS // 2).astype(jnp.int32)
    heights = [BLOCKS, BLOCKS, BLOCKS // 2, BLOCKS // 2] + [BLOCKS] * 5
    own, ahead, far_a, far_b, behind, *sent = pl.pallas_call(
        place_kernel,
        grid=(2,),
        out_shape=tuple(jax.ShapeDtypeStruct((h, tile_width), f32) for h in heights),
        in_specs=[
            SMEM,
            SMEM,
            pl.BlockSpec((touched, particles), lambda i: (0, 0)),
            pl.BlockSpec((1, particles), lambda i: (0, 0)),
            pl.BlockSpec((1, bin_gain.shape[1]), lambda i: (0, 0)),
            pl.BlockSpec((particles, touched, tile_width // 2), lambda i: (0, 0, i)),
        ],
        out_specs=tuple(pl.BlockSpec((h, tile_width // 2), lambda i: (0, i)) for h in heights),
        scratch_shapes=[pltpu.VMEM((4 * BLOCKS, entries), bf16)] * 3
        + [pltpu.VMEM((BOX, 2 * BOX), bf16), pltpu.VMEM((TILE_ROWS, 2, entries, BOX), bf16)]
        + [pltpu.VMEM((4 * BLOCKS, BOX), f32)],
        name="place",
    )(slab_pos.reshape(1), group_pos.reshape(1), tile_index[0].T, pose_bin, bin_gain, tiles[0])
    here = ("particle", "slab")
    up, down = ring_pairs(1), ring_pairs(-1)
    cut = BLOCKS // 2

    def send(part, pairs):
        return lax.ppermute(part, here, pairs)

    come = [send(sent[i], mirror_pairs(e)) for i, e in enumerate((3, -3, 1, -1))]
    rise, sink = send(far_a, up), send(far_b, down)
    rise = jnp.concatenate([come[0][:cut] + rise, come[0][cut:]], axis=0)
    sink = jnp.concatenate([come[1][:cut], come[1][cut:] + sink], axis=0)
    rise, sink = send(rise, up), send(sink, down)
    rise, sink = send(ahead + rise, up), send(behind + sink, down)
    rise, sink = send(come[2] + rise, up), send(come[3] + sink, down)
    plane = (slab_pos * 8 + group_pos * 2 + late).reshape(1)

    constants = [jnp.asarray(t) for t in tables()]
    sent = pl.pallas_call(
        planes_kernel,
        out_shape=jax.ShapeDtypeStruct((SENDERS // 4, 4, BANDS, 8, LANES), f32),
        in_specs=[SMEM, SMEM] + [VMEM] * 5,
        out_specs=VMEM,
        scratch_shapes=[pltpu.VMEM((2 * BOX, BOX), bf16)] * 2 + [pltpu.VMEM((BOX, BOX), f32)],
        name="planes",
    )(cutoffs, plane, own, rise, sink, *constants[:2])
    gathered = lax.all_to_all(
        sent.reshape(SENDERS, PER, LANES), ("particle", "slab"), split_axis=0, concat_axis=0, tiled=True
    ).reshape(SENDERS * PER, LANES)

    steps = BANDS // PACE
    rows_spec = pl.BlockSpec((PACE, 2, BOX, LANES), lambda b: (b, 0, 0, 0))
    rows_shape = jax.ShapeDtypeStruct((BANDS, 2, BOX, LANES), f32)
    row_spec = pl.BlockSpec((PACE, BOX, LANES), lambda b: (b, 0, 0))
    row_shape = jax.ShapeDtypeStruct((BANDS, BOX, LANES), f32)
    edge_spec = pl.BlockSpec((64, LANES), lambda b: (0, 0))
    edge_shape = jax.ShapeDtypeStruct((64, LANES), f32)
    edge_room = pltpu.VMEM((BOX, LANES), f32)
    own, leaving, own_edge, other_edge = pl.pallas_call(
        depth_kernel,
        grid=(steps,),
        out_shape=(rows_shape, rows_shape, edge_shape, edge_shape),
        in_specs=[
            SMEM,
            pl.BlockSpec((SENDERS * PER, LANES), lambda b: (0, 0)),
            pl.BlockSpec((2, BOX, BOX), lambda b: (0, 0, 0)),
        ],
        out_specs=(rows_spec, rows_spec, edge_spec, edge_spec),
        scratch_shapes=[edge_room, edge_room],
        name="depth",
    )(half_pos.reshape(1), gathered, constants[2])
    own_edge = lax.ppermute(own_edge, everyone, edge_pairs(0))
    other_edge = lax.ppermute(other_edge, everyone, edge_pairs(1))
    other = lax.ppermute(leaving, "half", [(0, 1), (1, 0)])
    first, second = pl.pallas_call(
        square_kernel,
        grid=(steps,),
        out_shape=(row_shape, row_shape),
        in_specs=[rows_spec, rows_spec, edge_spec, edge_spec],
        out_specs=(row_spec, row_spec),
        scratch_shapes=[edge_room],
        name="square",
    )(own, other, own_edge, other_edge)
    before = lax.ppermute(second, everyone, row_pairs(1))
    after = lax.ppermute(first, everyone, row_pairs(-1))
    swap = (side_pos != half_pos).astype(jnp.int32).reshape(1)
    block_spec = pl.BlockSpec((2, BOX, LANES), lambda b: (0, 0, 0))
    block_shape = jax.ShapeDtypeStruct((2, BOX, LANES), f32)
    near, far = pl.pallas_call(
        blend_kernel,
        grid=(steps,),
        out_shape=(block_shape, block_shape),
        in_specs=[SMEM, rows_spec, rows_spec] + [row_spec] * 4,
        out_specs=(block_spec, block_spec),
        scratch_shapes=[pltpu.VMEM((2, 3, BOX, LANES), f32)],
        name="blend",
    )(swap, own, other, first, second, before, after)
    near = lax.ppermute(near, everyone, home_pairs(0))
    far = lax.ppermute(far, everyone, home_pairs(1))
    low = jnp.where(half_pos == 0, near, far)
    high = jnp.where(half_pos == 0, far, near)
    refined = jnp.concatenate([low, high], axis=2)
    return jnp.transpose(refined, (1, 0, 2))[None]


def solution(mesh):
    placed = (
        P("half", "particle", "slab", None),
        P("half", "particle", "slab"),
        P("half", "particle"),
        P("half", None),
        P(),
    )

    return jax.shard_map(
        on_device,
        mesh=mesh,
        in_specs=placed,
        out_specs=P("half", None, ("particle", "slab"), None),
        check_vma=False,
    )
```

```python
import math

import jax
import jax.numpy as jnp
import numpy as np
from jax import lax
from jax.experimental import pallas as pl
from jax.experimental.pallas import tpu as pltpu
from jax.sharding import PartitionSpec as P

BOX = 256
HALF = BOX // 2
TILE_ROWS = 8
BLOCKS = BOX // TILE_ROWS
BANDS = 6
PACE = 2
GROUPS = 4
SLABS = 32
SENDERS = GROUPS * SLABS
PER = BANDS * 4
LANES = 128
error_floor = 1.0
bf16 = jnp.bfloat16
f32 = jnp.float32
VMEM = pl.BlockSpec(memory_space=pltpu.VMEM)
SMEM = pl.BlockSpec(memory_space=pltpu.SMEM)


def split(table):
    high = table.astype(np.float32).astype(jnp.bfloat16)
    low = (table - high.astype(np.float64)).astype(np.float32).astype(jnp.bfloat16)
    return high, low


def angles(left, right):
    return (np.outer(left, right) % BOX) * (2.0 * math.pi / BOX)


def tables():
    places = np.arange(BOX)
    near = np.arange(HALF)
    along_y, along_x = [], []
    for odd in range(2):
        turn = angles(near, near % BLOCKS * TILE_ROWS + near // BLOCKS * 2 + odd)
        cosine, sine = np.cos(turn), np.sin(turn)
        along_y.append(np.stack(split(np.block([[cosine, -sine], [sine, cosine]]))))
        turn = angles(2 * near + odd, near)
        cosine, sine = np.cos(turn), np.sin(turn)
        along_x.append(np.stack(split(np.block([[cosine, sine], [-sine, cosine]]))))
    along_y, along_x = np.stack(along_y), np.stack(along_x)
    sender = np.arange(SENDERS)
    group, slab = sender // SLABS, sender % SLABS
    plane = slab * 8 + group * 2 + (slab >= SLABS // 2)
    turn = angles(places, plane)
    even, odd = np.cos(turn), -np.sin(turn)
    odd[:, 0] = np.cos(math.pi * places)
    along_z = np.stack(split(np.concatenate([even, odd], axis=1) / BOX))
    return along_y, along_x, along_z


def two(value):
    high = value.astype(bf16)
    return high, (value - high.astype(f32)).astype(bf16)


def dot(a, b):
    return jnp.dot(a, b, preferred_element_type=f32)


def mark(rows, slots, gains):
    return jnp.where(rows == slots, gains, 0.0).astype(bf16)


def place_kernel(slab_ref, group_ref, index_ref, bin_ref, gain_ref, tile_ref, *refs):
    outs, (kept_mark, sent_mark, sent_mark_first, turn, moved, saved) = refs[:9], refs[9:]
    step = pl.program_id(0)
    slab, group = slab_ref[0], group_ref[0]
    depth, late = group * 2 + slab % 2, slab // (SLABS // 2)
    row = lax.broadcasted_iota(jnp.int32, (BLOCKS, BOX), 0)
    col = lax.broadcasted_iota(jnp.int32, (BLOCKS, BOX), 1)
    own_line = [((depth + d) & 7) // 2 for d in (0, 2, 4, 6)]
    sent_line = [((depth + d) & 7) // 2 for d in (3, 5, 1, 7)]

    @pl.when(step == 0)
    def _():
        touched, particles = index_ref.shape
        entries = touched * particles
        bins = gain_ref.shape[1]
        line = lax.broadcasted_iota(jnp.int32, (particles, entries), 0)
        wide = lax.broadcasted_iota(jnp.int32, (particles, entries), 1)
        spread = jnp.where(wide // touched == line, 1.0, 0.0).astype(bf16)
        slots = dot(index_ref[...].astype(f32).astype(bf16), spread)
        line = lax.broadcasted_iota(jnp.int32, slots.shape, 0)
        wide = lax.broadcasted_iota(jnp.int32, slots.shape, 1)
        slots = jnp.sum(jnp.where(wide % touched == line, slots, 0.0), axis=0, keepdims=True)
        slots = jnp.broadcast_to(slots, (BLOCKS, entries)).astype(jnp.int32)
        line = lax.broadcasted_iota(jnp.int32, (bins, bins), 0)
        wide = lax.broadcasted_iota(jnp.int32, (bins, bins), 1)
        table = jnp.broadcast_to(gain_ref[...].astype(f32), (bins, bins))
        table = jnp.sum(jnp.where(line == wide, table, 0.0), axis=1, keepdims=True)
        line = lax.broadcasted_iota(jnp.int32, (bins, particles), 0)
        gains = jnp.where(line == bin_ref[...], table, 0.0).astype(bf16)
        gains = jnp.sum(dot(gains, spread), axis=0, keepdims=True)
        gains = jnp.broadcast_to(gains, (BLOCKS, entries))
        for i in range(4):
            rows = pl.ds(i * BLOCKS, BLOCKS)
            kept_mark[rows, :] = mark((2 * own_line[i] + late) * BLOCKS + row, slots, gains)
            start = jnp.where(late == 1, (8 - 2 * sent_line[i]) & 7, 7 - 2 * sent_line[i]) * BLOCKS
            sent_mark[rows, :] = mark(start + BLOCKS - 1 - row, slots, gains)
            sent_mark_first[rows, :] = mark(start + ((BLOCKS - row) & (BLOCKS - 1)), slots, gains)
        line = lax.broadcasted_iota(jnp.int32, (BOX, BOX), 0)
        wide = lax.broadcasted_iota(jnp.int32, (BOX, BOX), 1)
        wide = (wide & (HALF - 1)) * 2 + (wide >> 7)
        turn[:, :BOX] = jnp.where(line == wide, 1.0, 0.0).astype(bf16)
        turn[:, BOX:] = jnp.where(((line + wide) & (BOX - 1)) == 0, 1.0, 0.0).astype(bf16)

    sign = jnp.where(step == 1, -1.0, 1.0)
    tile = tile_ref[...].reshape(-1, TILE_ROWS * BOX)
    for r in range(TILE_ROWS):
        both = dot(tile[:, r * BOX : (r + 1) * BOX], turn[...])
        moved[r, 0] = both[:, :BOX].astype(bf16)
        moved[r, 1] = (both[:, BOX:] * sign).astype(bf16)
    for r in range(TILE_ROWS):
        cols = pl.ds(r * BOX, BOX)
        kept = dot(kept_mark[...], moved[r, 0])
        sent = dot((sent_mark if r else sent_mark_first)[...], moved[(TILE_ROWS - r) % TILE_ROWS, 1])
        if r == 0:
            first = (row == 0) & (col == 0)
            last_sent = saved[...]
            saved[...] = sent
        parts = []
        for i in range(4):
            part = kept[i * BLOCKS : (i + 1) * BLOCKS]
            if r == 0:
                part = jnp.where(first & (step == 1) & (slab == 0) & (own_line[i] == 0), 0.0, part)
            parts.append(part)
        for i in range(4):
            part = sent[i * BLOCKS : (i + 1) * BLOCKS]
            alone = 0.0
            if r == 0:
                alone = jnp.where(first & (step == 1), last_sent[i * BLOCKS : (i + 1) * BLOCKS], 0.0)
            parts.append(jnp.where((slab == SLABS // 2) & (sent_line[i] == 0), alone, part))
        parts[2:3] = [parts[2][: BLOCKS // 2], parts[2][BLOCKS // 2 :]]
        for out_ref, part in zip(outs, parts):
            out_ref[:, cols] = part


def beside(*parts):
    return jnp.concatenate(parts, axis=1)


def above(*parts):
    return jnp.concatenate(parts, axis=0)


def planes_kernel(cut_ref, kz_ref, own_ref, up_ref, down_ref, y_ref, x_ref, out_ref, sh, sl, radius):
    alone = kz_ref[0] == 0
    for i in range(16):
        c, r = divmod(i, TILE_ROWS)
        cols = pl.ds(i * BOX, BOX)
        rows = pl.ds(r % 2 * BOX + c * HALF + r // 2 * BLOCKS, BLOCKS)
        whole = own_ref[:, cols] + up_ref[:, cols] + down_ref[:, cols]
        if i == TILE_ROWS:
            last = whole[0:1, 0:1]
        sh[rows, :], sl[rows, :] = two(whole)
    line = lax.broadcasted_iota(jnp.int32, (BOX, BOX), 0)
    col = lax.broadcasted_iota(jnp.int32, (BOX, BOX), 1)
    ky = (line & (BLOCKS - 1)) * TILE_ROWS + ((line >> 5) & 3) * 2 + (line >> 7)
    kx = (col & (HALF - 1)) * 2 + (col >> 7)
    ky = ((ky + HALF) & (BOX - 1)) - HALF
    kx = ((kx + HALF) & (BOX - 1)) - HALF
    kz = ((kz_ref[0] + HALF) & (BOX - 1)) - HALF
    radius[...] = (ky * ky + kx * kx + kz * kz).astype(f32)
    place_in = lax.broadcasted_iota(jnp.int32, (BLOCKS, 8, LANES), 1)
    upper, even_unit = place_in < 4, (place_in & 2) == 0

    @pl.loop(0, BANDS // 2)
    def _(pair):
        parts = []
        for odd in range(2):
            sides = []
            for i in range(2):
                cut = cut_ref[pair * 2 + i]
                near = radius[odd * HALF : (odd + 1) * HALF, :] <= (cut * cut).astype(f32)
                mask = jnp.where(near, 1.0, 0.0).astype(bf16)
                mask = above(mask, mask)
                rows = pl.ds(odd * BOX, BOX)
                high, low = sh[rows, :] * mask, sl[rows, :] * mask
                sides.append(above(high, high, low))
            parts.append(dot(beside(y_ref[odd, 0], y_ref[odd, 1], y_ref[odd, 0]), beside(*sides)))
        plus, minus = parts[0] + parts[1], parts[0] - parts[1]
        mids = ([], [])
        for i in range(2):
            cols = slice(i * BOX, (i + 1) * BOX)
            real = two(above(plus[:HALF, cols], minus[:HALF, cols]))
            imag = two(above(plus[HALF:, cols], minus[HALF:, cols]))
            for odd in range(2):
                few = slice(odd * HALF, (odd + 1) * HALF)
                high = beside(real[0][:, few], imag[0][:, few])
                low = beside(real[1][:, few], imag[1][:, few])
                mids[odd].append(beside(high, low, high))
        parts = [dot(above(*mids[odd]), above(x_ref[odd, 0], x_ref[odd, 0], x_ref[odd, 1])) for odd in range(2)]
        for side in range(2):
            units = []
            for i in range(2):
                value = jnp.where(cut_ref[pair * 2 + i] >= HALF, last, 0.0)
                first, second = parts[0][i * BOX : (i + 1) * BOX], parts[1][i * BOX : (i + 1) * BOX]
                full = first - second if side else first + second
                even, odd = full[:, :LANES], full[:, LANES:]
                odd = jnp.where(alone, jnp.broadcast_to(value, odd.shape), odd)
                units += [even.reshape(BLOCKS, 8, LANES), odd.reshape(BLOCKS, 8, LANES)]
            for odd_block in range(2):
                if odd_block:
                    halves = [jnp.where(upper, pltpu.roll(units[q], 4, 1), units[q + 2]) for q in range(2)]
                else:
                    halves = [jnp.where(upper, units[q], pltpu.roll(units[q + 2], 4, 1)) for q in range(2)]
                goal = 2 * (2 * (odd_block ^ side) + side)
                out_ref[:, goal, pair] = jnp.where(even_unit, halves[0], pltpu.roll(halves[1], 2, 1))
                out_ref[:, goal + 1, pair] = jnp.where(even_unit, pltpu.roll(halves[0], 6, 1), halves[1])


def depth_kernel(come_ref, z_ref, low_half_ref, high_half_ref, first_ref, second_ref, edge_ref, edge):
    pair = pl.program_id(0)
    lane = lax.broadcasted_iota(jnp.int32, (BOX, LANES), 1)
    turn = beside(z_ref[0], z_ref[1], z_ref[0])
    found = jnp.where(pair == 0, 0.0, edge[...])
    for i in range(2):
        maps = []
        for half in range(2):
            start = half * PER + pair * 8 + i * 4
            sides = [
                beside(*[come_ref[pl.ds(start + c * 2 + j, SENDERS, stride=2 * PER), :] for j in range(2)])
                for c in range(2)
            ]
            high, low = two(above(*sides))
            maps.append(dot(turn, above(high, high, low)))
        gap = maps[0] - maps[1]
        gap = gap * gap
        for row in range(2):
            cols = slice(row * LANES, (row + 1) * LANES)
            low_half_ref[i, row] = maps[0][:, cols]
            high_half_ref[i, row] = maps[1][:, cols]
            part = gap[:, cols]
            (first_ref, second_ref)[row][i] = part
            spot = (pair * 2 + i) * 4 + row * 2
            found = jnp.where((lane >> 1) == (spot >> 1), pltpu.roll(part, spot + 1, 1), found)
    edge[...] = found

    @pl.when(pair == BANDS // 2 - 1)
    def _():
        narrow = lax.broadcasted_iota(jnp.int32, (64, LANES), 1)
        packed = edge[0:64, :]
        for q in range(1, 4):
            packed = jnp.where((narrow >> 5) == q, pltpu.roll(edge[q * 64 : (q + 1) * 64, :], q * 32, 1), packed)
        edge_ref[...] = packed


def blend_kernel(
    side_ref,
    low_half_ref,
    high_half_ref,
    first_ref,
    second_ref,
    before_ref,
    after_ref,
    edge_ref,
    edge_before_ref,
    edge_after_ref,
    out_a_ref,
    out_b_ref,
    sums,
    border,
):
    step = pl.program_id(0)
    lane = lax.broadcasted_iota(jnp.int32, (BOX, LANES), 1)

    @pl.when(step == 0)
    def _():
        sums[...] = jnp.zeros_like(sums)
        here = edge_ref[...]
        here = here + pltpu.roll(here, LANES - 2, 1)
        for row, packed in enumerate((here + pltpu.roll(edge_before_ref[...], LANES - 2, 1), here + edge_after_ref[...])):
            for q in range(4):
                border[row, q * 64 : (q + 1) * 64, :] = pltpu.roll(packed, (LANES - q * 32) % LANES, 1)

    for row in range(2):
        low, high, total = sums[row, 0], sums[row, 1], sums[row, 2]
        for i in range(PACE):
            tall = first_ref[i] + second_ref[i] + (after_ref if row else before_ref)[i]
            beyond = pltpu.roll(border[row], LANES - 1 - (step * PACE + i) * 4, 1)
            left = pltpu.roll(jnp.where(lane == LANES - 1, beyond, tall), 1, 1)
            right = pltpu.roll(jnp.where(lane == 0, beyond, tall), LANES - 1, 1)
            wide = tall + left + right
            full = wide + pltpu.roll(wide, 1, 0) + pltpu.roll(wide, BOX - 1, 0)
            weight = 1.0 / (full / 27.0 + error_floor)
            low = low + weight * low_half_ref[i, row]
            high = high + weight * high_half_ref[i, row]
            total = total + weight
        sums[row, 0], sums[row, 1], sums[row, 2] = low, high, total

    @pl.when(step == BANDS // PACE - 1)
    def _():
        swap = side_ref[0] == 1
        for row in range(2):
            low = sums[row, 0] / sums[row, 2]
            high = sums[row, 1] / sums[row, 2]
            out_a_ref[row] = jnp.where(swap, high, low)
            out_b_ref[row] = jnp.where(swap, low, high)


def chip(depth, spot):
    return depth // 2 * SLABS + spot * 2 + depth % 2


def mirror_pairs(ahead):
    pairs = []
    for depth in range(8):
        for spot in range(16):
            goal = (depth, 15 - spot)
            if spot >= 8 and (depth + ahead) % 8 // 2 == 0:
                goal = ((depth + 1) % 8, 15 - spot) if depth % 2 else ((depth - 1) % 8, (16 - spot) % 8)
            pairs.append((chip(depth, spot), chip(*goal)))
    return pairs


def ring_pairs(step):
    return [(chip(d, s), chip((d + step) % 8, s)) for d in range(8) for s in range(16)]


def holder(block, side, core):
    return (2 * (block ^ side) + side) * 2 + core


def row_pairs(step, flip):
    pairs = []
    for n in range(SENDERS):
        goal = (n + step) % SENDERS
        pairs += [(holder(n // 2, side, n % 2), holder(goal // 2, side ^ flip, goal % 2)) for side in range(2)]
    return pairs


def home_pairs(flip):
    return [
        (holder(block, side, core), (2 * block + core) * 2 + (side ^ flip))
        for block in range(64)
        for side in range(2)
        for core in range(2)
    ]


def on_device(tiles, tile_index, pose_bin, bin_gain, cutoffs):
    slab_pos = lax.axis_index("slab")
    group_pos = lax.axis_index("particle")
    half_pos = lax.axis_index("half")
    side_pos = slab_pos % 2
    everyone = ("particle", "slab", "half")
    tile_width = 2 * TILE_ROWS * BOX
    _, particles, touched, _ = tiles.shape
    entries = particles * touched
    late = (slab_pos >= SLABS // 2).astype(jnp.int32)
    heights = [BLOCKS, BLOCKS, BLOCKS // 2, BLOCKS // 2] + [BLOCKS] * 5
    own, ahead, far_a, far_b, behind, *sent = pl.pallas_call(
        place_kernel,
        grid=(2,),
        out_shape=tuple(jax.ShapeDtypeStruct((h, tile_width), f32) for h in heights),
        in_specs=[
            SMEM,
            SMEM,
            pl.BlockSpec((touched, particles), lambda i: (0, 0)),
            pl.BlockSpec((1, particles), lambda i: (0, 0)),
            pl.BlockSpec((1, bin_gain.shape[1]), lambda i: (0, 0)),
            pl.BlockSpec((particles, touched, tile_width // 2), lambda i: (0, 0, i)),
        ],
        out_specs=tuple(pl.BlockSpec((h, tile_width // 2), lambda i: (0, i)) for h in heights),
        scratch_shapes=[pltpu.VMEM((4 * BLOCKS, entries), bf16)] * 3
        + [pltpu.VMEM((BOX, 2 * BOX), bf16), pltpu.VMEM((TILE_ROWS, 2, entries, BOX), bf16)]
        + [pltpu.VMEM((4 * BLOCKS, BOX), f32)],
        name="place",
    )(slab_pos.reshape(1), group_pos.reshape(1), tile_index[0].T, pose_bin, bin_gain, tiles[0])
    here = ("particle", "slab")
    up, down = ring_pairs(1), ring_pairs(-1)
    cut = BLOCKS // 2

    def send(part, pairs):
        return lax.ppermute(part, here, pairs)

    come = [send(sent[i], mirror_pairs(e)) for i, e in enumerate((3, -3, 1, -1))]
    rise, sink = send(far_a, up), send(far_b, down)
    rise = jnp.concatenate([come[0][:cut] + rise, come[0][cut:]], axis=0)
    sink = jnp.concatenate([come[1][:cut], come[1][cut:] + sink], axis=0)
    rise, sink = send(rise, up), send(sink, down)
    rise, sink = send(ahead + rise, up), send(behind + sink, down)
    rise, sink = send(come[2] + rise, up), send(come[3] + sink, down)
    plane = (slab_pos * 8 + group_pos * 2 + late).reshape(1)

    constants = [jnp.asarray(t) for t in tables()]
    sent = pl.pallas_call(
        planes_kernel,
        out_shape=jax.ShapeDtypeStruct((SENDERS // 4, 8, BANDS // 2, 8, LANES), f32),
        in_specs=[SMEM, SMEM] + [VMEM] * 5,
        out_specs=VMEM,
        scratch_shapes=[pltpu.VMEM((2 * BOX, BOX), bf16)] * 2 + [pltpu.VMEM((BOX, BOX), f32)],
        name="planes",
    )(cutoffs, plane, own, rise, sink, *constants[:2])
    gathered = lax.all_to_all(
        sent.reshape(2 * SENDERS, PER, LANES), everyone, split_axis=0, concat_axis=0, tiled=True
    ).reshape(2 * SENDERS * PER, LANES)

    steps = BANDS // PACE
    rows_spec = pl.BlockSpec((PACE, 2, BOX, LANES), lambda b: (b, 0, 0, 0))
    rows_shape = jax.ShapeDtypeStruct((BANDS, 2, BOX, LANES), f32)
    row_spec = pl.BlockSpec((PACE, BOX, LANES), lambda b: (b, 0, 0))
    row_shape = jax.ShapeDtypeStruct((BANDS, BOX, LANES), f32)
    edge_spec = pl.BlockSpec((64, LANES), lambda b: (0, 0))
    low_half, high_half, first, second, edge = pl.pallas_call(
        depth_kernel,
        grid=(BANDS // 2,),
        out_shape=(rows_shape, rows_shape, row_shape, row_shape, jax.ShapeDtypeStruct((64, LANES), f32)),
        in_specs=[
            pl.BlockSpec((2 * SENDERS * PER, LANES), lambda b: (0, 0)),
            pl.BlockSpec((2, BOX, BOX), lambda b: (0, 0, 0)),
        ],
        out_specs=(rows_spec, rows_spec, row_spec, row_spec, edge_spec),
        scratch_shapes=[pltpu.VMEM((BOX, LANES), f32)],
        name="depth",
    )(gathered, constants[2])
    before = lax.ppermute(second, everyone, row_pairs(1, 0))
    after = lax.ppermute(first, everyone, row_pairs(-1, 0))
    edges = [lax.ppermute(edge, everyone, row_pairs(n, 1)) for n in (0, 1, -1)]
    block_spec = pl.BlockSpec((2, BOX, LANES), lambda b: (0, 0, 0))
    block_shape = jax.ShapeDtypeStruct((2, BOX, LANES), f32)
    near, far = pl.pallas_call(
        blend_kernel,
        grid=(steps,),
        out_shape=(block_shape, block_shape),
        in_specs=[SMEM, rows_spec, rows_spec] + [row_spec] * 4 + [edge_spec] * 3,
        out_specs=(block_spec, block_spec),
        scratch_shapes=[pltpu.VMEM((2, 3, BOX, LANES), f32), pltpu.VMEM((2, BOX, LANES), f32)],
        name="blend",
    )(side_pos.reshape(1), low_half, high_half, first, second, before, after, *edges)
    near = lax.ppermute(near, everyone, home_pairs(0))
    far = lax.ppermute(far, everyone, home_pairs(1))
    low = jnp.where(half_pos == 0, near, far)
    high = jnp.where(half_pos == 0, far, near)
    refined = jnp.concatenate([low, high], axis=2)
    return jnp.transpose(refined, (1, 0, 2))[None]


def solution(mesh):
    placed = (
        P("half", "particle", "slab", None),
        P("half", "particle", "slab"),
        P("half", "particle"),
        P("half", None),
        P(),
    )

    return jax.shard_map(
        on_device,
        mesh=mesh,
        in_specs=placed,
        out_specs=P("half", None, ("particle", "slab"), None),
        check_vma=False,
    )
```

```python
import math

import jax
import jax.numpy as jnp
import numpy as np
from jax import lax
from jax.experimental import pallas as pl
from jax.experimental.pallas import tpu as pltpu
from jax.sharding import PartitionSpec as P

BOX = 256
HALF = BOX // 2
TILE_ROWS = 8
BLOCKS = BOX // TILE_ROWS
BANDS = 6
PACE = 2
GROUPS = 4
SLABS = 32
SENDERS = GROUPS * SLABS
PER = BANDS * 4
LANES = 128
error_floor = 1.0
bf16 = jnp.bfloat16
f32 = jnp.float32
VMEM = pl.BlockSpec(memory_space=pltpu.VMEM)
SMEM = pl.BlockSpec(memory_space=pltpu.SMEM)


def split(table):
    high = table.astype(np.float32).astype(jnp.bfloat16)
    low = (table - high.astype(np.float64)).astype(np.float32).astype(jnp.bfloat16)
    return high, low


def angles(left, right):
    return (np.outer(left, right) % BOX) * (2.0 * math.pi / BOX)


def tables():
    places = np.arange(BOX)
    near = np.arange(HALF)
    along_y, along_x = [], []
    for odd in range(2):
        turn = angles(near, near % BLOCKS * TILE_ROWS + near // BLOCKS * 2 + odd)
        cosine, sine = np.cos(turn), np.sin(turn)
        along_y.append(np.stack(split(np.block([[cosine, -sine], [sine, cosine]]))))
        turn = angles(2 * near + odd, near)
        cosine, sine = np.cos(turn), np.sin(turn)
        along_x.append(np.stack(split(np.block([[cosine, sine], [-sine, cosine]]))))
    along_y, along_x = np.stack(along_y), np.stack(along_x)
    sender = np.arange(SENDERS)
    group, slab = sender // SLABS, sender % SLABS
    plane = (slab ^ 1) * 8 + group * 2 + (slab >= SLABS // 2)
    turn = angles(places, plane)
    even, odd = np.cos(turn), -np.sin(turn)
    odd[:, plane == 0] = np.cos(math.pi * places)[:, None]
    along_z = np.stack(split(np.concatenate([even, odd], axis=1) / BOX))
    return along_y, along_x, along_z


def two(value):
    high = value.astype(bf16)
    return high, (value - high.astype(f32)).astype(bf16)


def dot(a, b):
    return jnp.dot(a, b, preferred_element_type=f32)


def mark(rows, slots, gains):
    return jnp.where(rows == slots, gains, 0.0).astype(bf16)


def place_kernel(slab_ref, group_ref, index_ref, bin_ref, gain_ref, tile_ref, *refs):
    outs, (kept_mark, sent_mark, sent_mark_first, turn, moved, saved) = refs[:9], refs[9:]
    step = pl.program_id(0)
    slab, group = slab_ref[0], group_ref[0]
    depth, late = group * 2 + slab % 2, slab // (SLABS // 2)
    row = lax.broadcasted_iota(jnp.int32, (BLOCKS, BOX), 0)
    col = lax.broadcasted_iota(jnp.int32, (BLOCKS, BOX), 1)
    own_line = [((depth + d) & 7) // 2 for d in (3, 5, 1, 7)]
    sent_line = [((depth + d) & 7) // 2 for d in (4, 2, 6, 0)]

    @pl.when(step == 0)
    def _():
        touched, particles = index_ref.shape
        entries = touched * particles
        bins = gain_ref.shape[1]
        line = lax.broadcasted_iota(jnp.int32, (particles, entries), 0)
        wide = lax.broadcasted_iota(jnp.int32, (particles, entries), 1)
        spread = jnp.where(wide // touched == line, 1.0, 0.0).astype(bf16)
        slots = dot(index_ref[...].astype(f32).astype(bf16), spread)
        line = lax.broadcasted_iota(jnp.int32, slots.shape, 0)
        wide = lax.broadcasted_iota(jnp.int32, slots.shape, 1)
        slots = jnp.sum(jnp.where(wide % touched == line, slots, 0.0), axis=0, keepdims=True)
        slots = jnp.broadcast_to(slots, (BLOCKS, entries)).astype(jnp.int32)
        line = lax.broadcasted_iota(jnp.int32, (bins, bins), 0)
        wide = lax.broadcasted_iota(jnp.int32, (bins, bins), 1)
        table = jnp.broadcast_to(gain_ref[...].astype(f32), (bins, bins))
        table = jnp.sum(jnp.where(line == wide, table, 0.0), axis=1, keepdims=True)
        line = lax.broadcasted_iota(jnp.int32, (bins, particles), 0)
        gains = jnp.where(line == bin_ref[...], table, 0.0).astype(bf16)
        gains = jnp.sum(dot(gains, spread), axis=0, keepdims=True)
        gains = jnp.broadcast_to(gains, (BLOCKS, entries))
        for i in range(4):
            rows = pl.ds(i * BLOCKS, BLOCKS)
            kept_mark[rows, :] = mark((2 * own_line[i] + late) * BLOCKS + row, slots, gains)
            start = jnp.where(late == 1, (8 - 2 * sent_line[i]) & 7, 7 - 2 * sent_line[i]) * BLOCKS
            sent_mark[rows, :] = mark(start + BLOCKS - 1 - row, slots, gains)
            sent_mark_first[rows, :] = mark(start + ((BLOCKS - row) & (BLOCKS - 1)), slots, gains)
        line = lax.broadcasted_iota(jnp.int32, (BOX, BOX), 0)
        wide = lax.broadcasted_iota(jnp.int32, (BOX, BOX), 1)
        wide = (wide & (HALF - 1)) * 2 + (wide >> 7)
        turn[:, :BOX] = jnp.where(line == wide, 1.0, 0.0).astype(bf16)
        turn[:, BOX:] = jnp.where(((line + wide) & (BOX - 1)) == 0, 1.0, 0.0).astype(bf16)

    sign = jnp.where(step == 1, -1.0, 1.0)
    tile = tile_ref[...].reshape(-1, TILE_ROWS * BOX)
    for r in range(TILE_ROWS):
        both = dot(tile[:, r * BOX : (r + 1) * BOX], turn[...])
        moved[r, 0] = both[:, :BOX].astype(bf16)
        moved[r, 1] = (both[:, BOX:] * sign).astype(bf16)
    for r in range(TILE_ROWS):
        cols = pl.ds(r * BOX, BOX)
        kept = dot(kept_mark[...], moved[r, 0])
        sent = dot((sent_mark if r else sent_mark_first)[...], moved[(TILE_ROWS - r) % TILE_ROWS, 1])
        if r == 0:
            first = (row == 0) & (col == 0)
            last_sent = saved[...]
            saved[...] = sent
        parts = []
        for i in range(4):
            part = kept[i * BLOCKS : (i + 1) * BLOCKS]
            if r == 0:
                part = jnp.where(first & (step == 1) & (slab == 0) & (own_line[i] == 0), 0.0, part)
            parts.append(part)
        for i in range(4):
            part = sent[i * BLOCKS : (i + 1) * BLOCKS]
            alone = 0.0
            if r == 0:
                alone = jnp.where(first & (step == 1), last_sent[i * BLOCKS : (i + 1) * BLOCKS], 0.0)
            parts.append(jnp.where((slab == SLABS // 2) & (sent_line[i] == 0), alone, part))
        parts[4:5] = [parts[4][: BLOCKS // 2], parts[4][BLOCKS // 2 :]]
        for out_ref, part in zip(outs, parts):
            out_ref[:, cols] = part


def beside(*parts):
    return jnp.concatenate(parts, axis=1)


def above(*parts):
    return jnp.concatenate(parts, axis=0)


def planes_kernel(cut_ref, kz_ref, own_ref, up_ref, down_ref, y_ref, x_ref, out_ref, sh, sl, radius):
    alone = kz_ref[0] == 0
    for i in range(16):
        c, r = divmod(i, TILE_ROWS)
        cols = pl.ds(i * BOX, BOX)
        rows = pl.ds(r % 2 * BOX + c * HALF + r // 2 * BLOCKS, BLOCKS)
        whole = own_ref[:, cols] + up_ref[:, cols] + down_ref[:, cols]
        if i == TILE_ROWS:
            last = whole[0:1, 0:1]
        sh[rows, :], sl[rows, :] = two(whole)
    line = lax.broadcasted_iota(jnp.int32, (BOX, BOX), 0)
    col = lax.broadcasted_iota(jnp.int32, (BOX, BOX), 1)
    ky = (line & (BLOCKS - 1)) * TILE_ROWS + ((line >> 5) & 3) * 2 + (line >> 7)
    kx = (col & (HALF - 1)) * 2 + (col >> 7)
    ky = ((ky + HALF) & (BOX - 1)) - HALF
    kx = ((kx + HALF) & (BOX - 1)) - HALF
    kz = ((kz_ref[0] + HALF) & (BOX - 1)) - HALF
    radius[...] = (ky * ky + kx * kx + kz * kz).astype(f32)
    place_in = lax.broadcasted_iota(jnp.int32, (BLOCKS, 8, LANES), 1)
    upper, even_unit = place_in < 4, (place_in & 2) == 0

    @pl.loop(0, BANDS // 2)
    def _(pair):
        parts = []
        for odd in range(2):
            sides = []
            for i in range(2):
                cut = cut_ref[pair * 2 + i]
                near = radius[odd * HALF : (odd + 1) * HALF, :] <= (cut * cut).astype(f32)
                mask = jnp.where(near, 1.0, 0.0).astype(bf16)
                mask = above(mask, mask)
                rows = pl.ds(odd * BOX, BOX)
                high, low = sh[rows, :] * mask, sl[rows, :] * mask
                sides.append(above(high, high, low))
            parts.append(dot(beside(y_ref[odd, 0], y_ref[odd, 1], y_ref[odd, 0]), beside(*sides)))
        plus, minus = parts[0] + parts[1], parts[0] - parts[1]
        mids = ([], [])
        for i in range(2):
            cols = slice(i * BOX, (i + 1) * BOX)
            real = two(above(plus[:HALF, cols], minus[:HALF, cols]))
            imag = two(above(plus[HALF:, cols], minus[HALF:, cols]))
            for odd in range(2):
                few = slice(odd * HALF, (odd + 1) * HALF)
                high = beside(real[0][:, few], imag[0][:, few])
                low = beside(real[1][:, few], imag[1][:, few])
                mids[odd].append(beside(high, low, high))
        parts = [dot(above(*mids[odd]), above(x_ref[odd, 0], x_ref[odd, 0], x_ref[odd, 1])) for odd in range(2)]
        for side in range(2):
            units = []
            for i in range(2):
                value = jnp.where(cut_ref[pair * 2 + i] >= HALF, last, 0.0)
                first, second = parts[0][i * BOX : (i + 1) * BOX], parts[1][i * BOX : (i + 1) * BOX]
                full = first - second if side else first + second
                even, odd = full[:, :LANES], full[:, LANES:]
                odd = jnp.where(alone, jnp.broadcast_to(value, odd.shape), odd)
                units += [even.reshape(BLOCKS, 8, LANES), odd.reshape(BLOCKS, 8, LANES)]
            for odd_block in range(2):
                if odd_block:
                    halves = [jnp.where(upper, pltpu.roll(units[q], 4, 1), units[q + 2]) for q in range(2)]
                else:
                    halves = [jnp.where(upper, units[q], pltpu.roll(units[q + 2], 4, 1)) for q in range(2)]
                goal = 2 * (2 * (odd_block ^ side) + side)
                out_ref[:, goal, pair] = jnp.where(even_unit, halves[0], pltpu.roll(halves[1], 2, 1))
                out_ref[:, goal + 1, pair] = jnp.where(even_unit, pltpu.roll(halves[0], 6, 1), halves[1])


def depth_kernel(come_ref, z_ref, low_half_ref, high_half_ref, first_ref, second_ref, edge_ref, edge):
    pair = pl.program_id(0)
    lane = lax.broadcasted_iota(jnp.int32, (BOX, LANES), 1)
    turn = beside(z_ref[0], z_ref[1], z_ref[0])
    found = jnp.where(pair == 0, 0.0, edge[...])
    for i in range(2):
        maps = []
        for half in range(2):
            start = half * PER + pair * 8 + i * 4
            sides = [
                beside(*[come_ref[pl.ds(start + c * 2 + j, SENDERS, stride=2 * PER), :] for j in range(2)])
                for c in range(2)
            ]
            high, low = two(above(*sides))
            maps.append(dot(turn, above(high, high, low)))
        gap = maps[0] - maps[1]
        gap = gap * gap
        for row in range(2):
            cols = slice(row * LANES, (row + 1) * LANES)
            low_half_ref[i, row] = maps[0][:, cols]
            high_half_ref[i, row] = maps[1][:, cols]
            part = gap[:, cols]
            (first_ref, second_ref)[row][i] = part
            spot = (pair * 2 + i) * 4 + row * 2
            found = jnp.where((lane >> 1) == (spot >> 1), pltpu.roll(part, spot + 1, 1), found)
    edge[...] = found

    @pl.when(pair == BANDS // 2 - 1)
    def _():
        narrow = lax.broadcasted_iota(jnp.int32, (64, LANES), 1)
        packed = edge[0:64, :]
        for q in range(1, 4):
            packed = jnp.where((narrow >> 5) == q, pltpu.roll(edge[q * 64 : (q + 1) * 64, :], q * 32, 1), packed)
        edge_ref[...] = packed


def blend_kernel(
    side_ref,
    low_half_ref,
    high_half_ref,
    first_ref,
    second_ref,
    before_ref,
    after_ref,
    edge_ref,
    edge_before_ref,
    edge_after_ref,
    out_a_ref,
    out_b_ref,
    sums,
    border,
):
    step = pl.program_id(0)
    lane = lax.broadcasted_iota(jnp.int32, (BOX, LANES), 1)

    @pl.when(step == 0)
    def _():
        sums[...] = jnp.zeros_like(sums)
        here = edge_ref[...]
        here = here + pltpu.roll(here, LANES - 2, 1)
        for row, packed in enumerate((here + pltpu.roll(edge_before_ref[...], LANES - 2, 1), here + edge_after_ref[...])):
            for q in range(4):
                border[row, q * 64 : (q + 1) * 64, :] = pltpu.roll(packed, (LANES - q * 32) % LANES, 1)

    for row in range(2):
        low, high, total = sums[row, 0], sums[row, 1], sums[row, 2]
        for i in range(PACE):
            tall = first_ref[i] + second_ref[i] + (after_ref if row else before_ref)[i]
            beyond = pltpu.roll(border[row], LANES - 1 - (step * PACE + i) * 4, 1)
            left = pltpu.roll(jnp.where(lane == LANES - 1, beyond, tall), 1, 1)
            right = pltpu.roll(jnp.where(lane == 0, beyond, tall), LANES - 1, 1)
            wide = tall + left + right
            full = wide + pltpu.roll(wide, 1, 0) + pltpu.roll(wide, BOX - 1, 0)
            weight = 1.0 / (full / 27.0 + error_floor)
            low = low + weight * low_half_ref[i, row]
            high = high + weight * high_half_ref[i, row]
            total = total + weight
        sums[row, 0], sums[row, 1], sums[row, 2] = low, high, total

    @pl.when(step == BANDS // PACE - 1)
    def _():
        swap = side_ref[0] == 1
        for row in range(2):
            low = sums[row, 0] / sums[row, 2]
            high = sums[row, 1] / sums[row, 2]
            out_a_ref[row] = jnp.where(swap, high, low)
            out_b_ref[row] = jnp.where(swap, low, high)


def chip(depth, spot):
    return depth // 2 * SLABS + spot * 2 + depth % 2


def mirror_pairs(ahead):
    pairs = []
    for depth in range(8):
        for spot in range(16):
            goal = (depth, 15 - spot)
            if spot >= 8 and (depth + ahead) % 8 // 2 == 0:
                goal = (depth ^ 1, 15 - spot if depth % 2 else (16 - spot) % 8)
            pairs.append((chip(depth, spot), chip(*goal)))
    return pairs


def ring_pairs(step):
    return [(chip(d, s), chip((d + step) % 8, s)) for d in range(8) for s in range(16)]


def holder(block, side, core):
    return (2 * (block ^ side) + side) * 2 + core


def row_pairs(step, flip):
    pairs = []
    for n in range(SENDERS):
        goal = (n + step) % SENDERS
        pairs += [(holder(n // 2, side, n % 2), holder(goal // 2, side ^ flip, goal % 2)) for side in range(2)]
    return pairs


def home_pairs(flip):
    return [
        (holder(block, side, core), (2 * block + core) * 2 + (side ^ flip))
        for block in range(64)
        for side in range(2)
        for core in range(2)
    ]


def on_device(tiles, tile_index, pose_bin, bin_gain, cutoffs):
    slab_pos = lax.axis_index("slab")
    group_pos = lax.axis_index("particle")
    half_pos = lax.axis_index("half")
    side_pos = slab_pos % 2
    everyone = ("particle", "slab", "half")
    tile_width = 2 * TILE_ROWS * BOX
    _, particles, touched, _ = tiles.shape
    entries = particles * touched
    late = (slab_pos >= SLABS // 2).astype(jnp.int32)
    heights = [BLOCKS] * 4 + [BLOCKS // 2] * 2 + [BLOCKS] * 3
    *own, far_a, far_b, ahead, behind, home = pl.pallas_call(
        place_kernel,
        grid=(2,),
        out_shape=tuple(jax.ShapeDtypeStruct((h, tile_width), f32) for h in heights),
        in_specs=[
            SMEM,
            SMEM,
            pl.BlockSpec((touched, particles), lambda i: (0, 0)),
            pl.BlockSpec((1, particles), lambda i: (0, 0)),
            pl.BlockSpec((1, bin_gain.shape[1]), lambda i: (0, 0)),
            pl.BlockSpec((particles, touched, tile_width // 2), lambda i: (0, 0, i)),
        ],
        out_specs=tuple(pl.BlockSpec((h, tile_width // 2), lambda i: (0, i)) for h in heights),
        scratch_shapes=[pltpu.VMEM((4 * BLOCKS, entries), bf16)] * 3
        + [pltpu.VMEM((BOX, 2 * BOX), bf16), pltpu.VMEM((TILE_ROWS, 2, entries, BOX), bf16)]
        + [pltpu.VMEM((4 * BLOCKS, BOX), f32)],
        name="place",
    )(slab_pos.reshape(1), group_pos.reshape(1), tile_index[0].T, pose_bin, bin_gain, tiles[0])
    here = ("particle", "slab")
    up, down = ring_pairs(1), ring_pairs(-1)
    cut = BLOCKS // 2

    def send(part, pairs):
        return lax.ppermute(part, here, pairs)

    rise = send(far_a, mirror_pairs(4))
    sink = send(far_b, mirror_pairs(4))
    ahead = send(ahead, mirror_pairs(2))
    behind = send(behind, mirror_pairs(-2))
    home = send(home, mirror_pairs(0))
    rise, sink = send(rise, up), send(sink, down)
    rise = jnp.concatenate([own[0][:cut] + rise, own[0][cut:]], axis=0)
    sink = jnp.concatenate([own[1][:cut], own[1][cut:] + sink], axis=0)
    rise, sink = send(rise, up), send(sink, down)
    rise, sink = send(ahead + rise, up), send(behind + sink, down)
    rise, sink = send(own[2] + rise, up), send(own[3] + sink, down)
    plane = ((slab_pos ^ 1) * 8 + group_pos * 2 + late).reshape(1)

    constants = [jnp.asarray(t) for t in tables()]
    sent = pl.pallas_call(
        planes_kernel,
        out_shape=jax.ShapeDtypeStruct((SENDERS // 4, 8, BANDS // 2, 8, LANES), f32),
        in_specs=[SMEM, SMEM] + [VMEM] * 5,
        out_specs=VMEM,
        scratch_shapes=[pltpu.VMEM((2 * BOX, BOX), bf16)] * 2 + [pltpu.VMEM((BOX, BOX), f32)],
        name="planes",
    )(cutoffs, plane, home, rise, sink, *constants[:2])
    gathered = lax.all_to_all(sent.reshape(2 * SENDERS, PER, LANES), everyone, split_axis=0, concat_axis=0, tiled=True)
    gathered = gathered.reshape(2 * SENDERS * PER, LANES)
    side_flag = jnp.where(jnp.arange(LANES, dtype=jnp.int32) == 0, side_pos, 0)

    steps = BANDS // PACE
    rows_spec = pl.BlockSpec((PACE, 2, BOX, LANES), lambda b: (b, 0, 0, 0))
    rows_shape = jax.ShapeDtypeStruct((BANDS, 2, BOX, LANES), f32)
    row_spec = pl.BlockSpec((PACE, BOX, LANES), lambda b: (b, 0, 0))
    row_shape = jax.ShapeDtypeStruct((BANDS, BOX, LANES), f32)
    edge_spec = pl.BlockSpec((64, LANES), lambda b: (0, 0))
    low_half, high_half, first, second, edge = pl.pallas_call(
        depth_kernel,
        grid=(BANDS // 2,),
        out_shape=(rows_shape, rows_shape, row_shape, row_shape, jax.ShapeDtypeStruct((64, LANES), f32)),
        in_specs=[
            pl.BlockSpec((2 * SENDERS * PER, LANES), lambda b: (0, 0)),
            pl.BlockSpec((2, BOX, BOX), lambda b: (0, 0, 0)),
        ],
        out_specs=(rows_spec, rows_spec, row_spec, row_spec, edge_spec),
        scratch_shapes=[pltpu.VMEM((BOX, LANES), f32)],
        name="depth",
    )(gathered, constants[2])
    before = lax.ppermute(second, everyone, row_pairs(1, 0))
    after = lax.ppermute(first, everyone, row_pairs(-1, 0))
    edges = [lax.ppermute(edge, everyone, row_pairs(n, 1)) for n in (0, 1, -1)]
    block_spec = pl.BlockSpec((2, BOX, LANES), lambda b: (0, 0, 0))
    block_shape = jax.ShapeDtypeStruct((2, BOX, LANES), f32)
    near, far = pl.pallas_call(
        blend_kernel,
        grid=(steps,),
        out_shape=(block_shape, block_shape),
        in_specs=[SMEM, rows_spec, rows_spec] + [row_spec] * 4 + [edge_spec] * 3,
        out_specs=(block_spec, block_spec),
        scratch_shapes=[pltpu.VMEM((2, 3, BOX, LANES), f32), pltpu.VMEM((2, BOX, LANES), f32)],
        name="blend",
    )(side_flag, low_half, high_half, first, second, before, after, *edges)
    near = lax.ppermute(near, everyone, home_pairs(0))
    far = lax.ppermute(far, everyone, home_pairs(1))
    low = jnp.where(half_pos == 0, near, far)
    high = jnp.where(half_pos == 0, far, near)
    refined = jnp.concatenate([low, high], axis=2)
    return jnp.transpose(refined, (1, 0, 2))[None]


def solution(mesh):
    placed = (
        P("half", "particle", "slab", None),
        P("half", "particle", "slab"),
        P("half", "particle"),
        P("half", None),
        P(),
    )

    return jax.shard_map(
        on_device,
        mesh=mesh,
        in_specs=placed,
        out_specs=P("half", None, ("particle", "slab"), None),
        check_vma=False,
    )
```

```python
import math

import jax
import jax.numpy as jnp
import numpy as np
from jax import lax
from jax.experimental import pallas as pl
from jax.experimental.pallas import tpu as pltpu
from jax.sharding import PartitionSpec as P

BOX = 256
HALF = BOX // 2
TILE_ROWS = 8
BLOCKS = BOX // TILE_ROWS
BANDS = 6
PACE = 2
GROUPS = 4
SLABS = 32
SENDERS = GROUPS * SLABS
PER = BANDS * 4
LANES = 128
error_floor = 1.0
bf16 = jnp.bfloat16
f32 = jnp.float32
VMEM = pl.BlockSpec(memory_space=pltpu.VMEM)
SMEM = pl.BlockSpec(memory_space=pltpu.SMEM)


def split(table):
    high = table.astype(np.float32).astype(jnp.bfloat16)
    low = (table - high.astype(np.float64)).astype(np.float32).astype(jnp.bfloat16)
    return high, low


def angles(left, right):
    return (np.outer(left, right) % BOX) * (2.0 * math.pi / BOX)


def tables():
    places = np.arange(BOX)
    near = np.arange(HALF)
    along_y, along_x = [], []
    for odd in range(2):
        turn = angles(near, near % BLOCKS * TILE_ROWS + near // BLOCKS * 2 + odd)
        cosine, sine = np.cos(turn), np.sin(turn)
        along_y.append(np.stack(split(np.block([[cosine, -sine], [sine, cosine]]))))
        turn = angles(2 * near + odd, near)
        cosine, sine = np.cos(turn), np.sin(turn)
        along_x.append(np.stack(split(np.block([[cosine, sine], [-sine, cosine]]))))
    along_y, along_x = np.stack(along_y), np.stack(along_x)
    sender = np.arange(SENDERS)
    group, slab = sender // SLABS, sender % SLABS
    plane = slab * 8 + group * 2 + (slab >= SLABS // 2)
    turn = angles(places, plane)
    even, odd = np.cos(turn), -np.sin(turn)
    odd[:, 0] = np.cos(math.pi * places)
    along_z = np.stack(split(np.concatenate([even, odd], axis=1) / BOX))
    return along_y, along_x, along_z


def two(value):
    high = value.astype(bf16)
    return high, (value - high.astype(f32)).astype(bf16)


def dot(a, b):
    return jnp.dot(a, b, preferred_element_type=f32)


def mark(rows, slots, gains):
    return jnp.where(rows == slots, gains, 0.0).astype(bf16)


def place_kernel(slab_ref, group_ref, index_ref, bin_ref, gain_ref, tile_ref, *refs):
    outs, (kept_mark, sent_mark, sent_mark_first, turn, moved, saved) = refs[:9], refs[9:]
    step = pl.program_id(0)
    slab, group = slab_ref[0], group_ref[0]
    depth, late = group * 2 + slab % 2, slab // (SLABS // 2)
    row = lax.broadcasted_iota(jnp.int32, (BLOCKS, BOX), 0)
    col = lax.broadcasted_iota(jnp.int32, (BLOCKS, BOX), 1)
    own_line = [((depth + d) & 7) // 2 for d in (0, 2, 4, 6)]
    sent_line = [((depth + d) & 7) // 2 for d in (3, 5, 1, 7)]

    @pl.when(step == 0)
    def _():
        touched, particles = index_ref.shape
        entries = touched * particles
        bins = gain_ref.shape[1]
        line = lax.broadcasted_iota(jnp.int32, (particles, entries), 0)
        wide = lax.broadcasted_iota(jnp.int32, (particles, entries), 1)
        spread = jnp.where(wide // touched == line, 1.0, 0.0).astype(bf16)
        slots = dot(index_ref[...].astype(f32).astype(bf16), spread)
        line = lax.broadcasted_iota(jnp.int32, slots.shape, 0)
        wide = lax.broadcasted_iota(jnp.int32, slots.shape, 1)
        slots = jnp.sum(jnp.where(wide % touched == line, slots, 0.0), axis=0, keepdims=True)
        slots = jnp.broadcast_to(slots, (BLOCKS, entries)).astype(jnp.int32)
        line = lax.broadcasted_iota(jnp.int32, (bins, bins), 0)
        wide = lax.broadcasted_iota(jnp.int32, (bins, bins), 1)
        table = jnp.broadcast_to(gain_ref[...].astype(f32), (bins, bins))
        table = jnp.sum(jnp.where(line == wide, table, 0.0), axis=1, keepdims=True)
        line = lax.broadcasted_iota(jnp.int32, (bins, particles), 0)
        gains = jnp.where(line == bin_ref[...], table, 0.0).astype(bf16)
        gains = jnp.sum(dot(gains, spread), axis=0, keepdims=True)
        gains = jnp.broadcast_to(gains, (BLOCKS, entries))
        for i in range(4):
            rows = pl.ds(i * BLOCKS, BLOCKS)
            kept_mark[rows, :] = mark((2 * own_line[i] + late) * BLOCKS + row, slots, gains)
            start = jnp.where(late == 1, (8 - 2 * sent_line[i]) & 7, 7 - 2 * sent_line[i]) * BLOCKS
            sent_mark[rows, :] = mark(start + BLOCKS - 1 - row, slots, gains)
            sent_mark_first[rows, :] = mark(start + ((BLOCKS - row) & (BLOCKS - 1)), slots, gains)
        line = lax.broadcasted_iota(jnp.int32, (BOX, BOX), 0)
        wide = lax.broadcasted_iota(jnp.int32, (BOX, BOX), 1)
        wide = (wide & (HALF - 1)) * 2 + (wide >> 7)
        turn[:, :BOX] = jnp.where(line == wide, 1.0, 0.0).astype(bf16)
        turn[:, BOX:] = jnp.where(((line + wide) & (BOX - 1)) == 0, 1.0, 0.0).astype(bf16)

    sign = jnp.where(step == 1, -1.0, 1.0)
    tile = tile_ref[...].reshape(-1, TILE_ROWS * BOX)
    for r in range(TILE_ROWS):
        both = dot(tile[:, r * BOX : (r + 1) * BOX], turn[...])
        moved[r, 0] = both[:, :BOX].astype(bf16)
        moved[r, 1] = (both[:, BOX:] * sign).astype(bf16)
    for r in range(TILE_ROWS):
        cols = pl.ds(r * BOX, BOX)
        kept = dot(kept_mark[...], moved[r, 0])
        sent = dot((sent_mark if r else sent_mark_first)[...], moved[(TILE_ROWS - r) % TILE_ROWS, 1])
        if r == 0:
            first = (row == 0) & (col == 0)
            last_sent = saved[...]
            saved[...] = sent
        parts = []
        for i in range(4):
            part = kept[i * BLOCKS : (i + 1) * BLOCKS]
            if r == 0:
                part = jnp.where(first & (step == 1) & (slab == 0) & (own_line[i] == 0), 0.0, part)
            parts.append(part)
        for i in range(4):
            part = sent[i * BLOCKS : (i + 1) * BLOCKS]
            alone = 0.0
            if r == 0:
                alone = jnp.where(first & (step == 1), last_sent[i * BLOCKS : (i + 1) * BLOCKS], 0.0)
            parts.append(jnp.where((slab == SLABS // 2) & (sent_line[i] == 0), alone, part))
        parts[2:3] = [parts[2][: BLOCKS // 2], parts[2][BLOCKS // 2 :]]
        for out_ref, part in zip(outs, parts):
            out_ref[:, cols] = part


def beside(*parts):
    return jnp.concatenate(parts, axis=1)


def above(*parts):
    return jnp.concatenate(parts, axis=0)


def planes_kernel(cut_ref, kz_ref, own_ref, up_ref, down_ref, y_ref, x_ref, out_ref, sh, sl, radius):
    alone = kz_ref[0] == 0
    for i in range(16):
        c, r = divmod(i, TILE_ROWS)
        cols = pl.ds(i * BOX, BOX)
        rows = pl.ds(r % 2 * BOX + c * HALF + r // 2 * BLOCKS, BLOCKS)
        whole = own_ref[:, cols] + up_ref[:, cols] + down_ref[:, cols]
        if i == TILE_ROWS:
            last = whole[0:1, 0:1]
        sh[rows, :], sl[rows, :] = two(whole)
    line = lax.broadcasted_iota(jnp.int32, (BOX, BOX), 0)
    col = lax.broadcasted_iota(jnp.int32, (BOX, BOX), 1)
    ky = (line & (BLOCKS - 1)) * TILE_ROWS + ((line >> 5) & 3) * 2 + (line >> 7)
    kx = (col & (HALF - 1)) * 2 + (col >> 7)
    ky = ((ky + HALF) & (BOX - 1)) - HALF
    kx = ((kx + HALF) & (BOX - 1)) - HALF
    kz = ((kz_ref[0] + HALF) & (BOX - 1)) - HALF
    radius[...] = (ky * ky + kx * kx + kz * kz).astype(f32)
    place_in = lax.broadcasted_iota(jnp.int32, (BLOCKS, 8, LANES), 1)
    upper, even_unit = place_in < 4, (place_in & 2) == 0

    @pl.loop(0, BANDS // 2)
    def _(pair):
        parts = []
        for odd in range(2):
            sides = []
            for i in range(2):
                cut = cut_ref[pair * 2 + i]
                near = radius[odd * HALF : (odd + 1) * HALF, :] <= (cut * cut).astype(f32)
                mask = jnp.where(near, 1.0, 0.0).astype(bf16)
                mask = above(mask, mask)
                rows = pl.ds(odd * BOX, BOX)
                high, low = sh[rows, :] * mask, sl[rows, :] * mask
                sides.append(above(high, high, low))
            parts.append(dot(beside(y_ref[odd, 0], y_ref[odd, 1], y_ref[odd, 0]), beside(*sides)))
        plus, minus = parts[0] + parts[1], parts[0] - parts[1]
        mids = ([], [])
        for i in range(2):
            cols = slice(i * BOX, (i + 1) * BOX)
            real = two(above(plus[:HALF, cols], minus[:HALF, cols]))
            imag = two(above(plus[HALF:, cols], minus[HALF:, cols]))
            for odd in range(2):
                few = slice(odd * HALF, (odd + 1) * HALF)
                high = beside(real[0][:, few], imag[0][:, few])
                low = beside(real[1][:, few], imag[1][:, few])
                mids[odd].append(beside(high, low, high))
        parts = [dot(above(*mids[odd]), above(x_ref[odd, 0], x_ref[odd, 0], x_ref[odd, 1])) for odd in range(2)]
        for side in range(2):
            units = []
            for i in range(2):
                value = jnp.where(cut_ref[pair * 2 + i] >= HALF, last, 0.0)
                first, second = parts[0][i * BOX : (i + 1) * BOX], parts[1][i * BOX : (i + 1) * BOX]
                full = first - second if side else first + second
                even, odd = full[:, :LANES], full[:, LANES:]
                odd = jnp.where(alone, jnp.broadcast_to(value, odd.shape), odd)
                units += [even.reshape(BLOCKS, 8, LANES), odd.reshape(BLOCKS, 8, LANES)]
            for odd_block in range(2):
                if odd_block:
                    halves = [jnp.where(upper, pltpu.roll(units[q], 4, 1), units[q + 2]) for q in range(2)]
                else:
                    halves = [jnp.where(upper, units[q], pltpu.roll(units[q + 2], 4, 1)) for q in range(2)]
                goal = 2 * (2 * (odd_block ^ side) + side)
                out_ref[:, goal, pair] = jnp.where(even_unit, halves[0], pltpu.roll(halves[1], 2, 1))
                out_ref[:, goal + 1, pair] = jnp.where(even_unit, pltpu.roll(halves[0], 6, 1), halves[1])


def depth_kernel(come_ref, z_ref, low_half_ref, high_half_ref, first_ref, second_ref, edge_ref, edge):
    pair = pl.program_id(0)
    lane = lax.broadcasted_iota(jnp.int32, (BOX, LANES), 1)
    turn = beside(z_ref[0], z_ref[1], z_ref[0])
    found = jnp.where(pair == 0, 0.0, edge[...])
    for i in range(2):
        maps = []
        for half in range(2):
            start = half * PER + pair * 8 + i * 4
            sides = [
                beside(*[come_ref[pl.ds(start + c * 2 + j, SENDERS, stride=2 * PER), :] for j in range(2)])
                for c in range(2)
            ]
            high, low = two(above(*sides))
            maps.append(dot(turn, above(high, high, low)))
        gap = maps[0] - maps[1]
        gap = gap * gap
        for row in range(2):
            cols = slice(row * LANES, (row + 1) * LANES)
            low_half_ref[i, row] = maps[0][:, cols]
            high_half_ref[i, row] = maps[1][:, cols]
            part = gap[:, cols]
            (first_ref, second_ref)[row][i] = part
            spot = (pair * 2 + i) * 4 + row * 2
            found = jnp.where((lane >> 1) == (spot >> 1), pltpu.roll(part, spot + 1, 1), found)
    edge[...] = found

    @pl.when(pair == BANDS // 2 - 1)
    def _():
        narrow = lax.broadcasted_iota(jnp.int32, (64, LANES), 1)
        packed = edge[0:64, :]
        for q in range(1, 4):
            packed = jnp.where((narrow >> 5) == q, pltpu.roll(edge[q * 64 : (q + 1) * 64, :], q * 32, 1), packed)
        edge_ref[...] = packed


def blend_kernel(
    side_ref,
    low_half_ref,
    high_half_ref,
    first_ref,
    second_ref,
    before_ref,
    after_ref,
    edge_ref,
    edge_before_ref,
    edge_after_ref,
    out_a_ref,
    out_b_ref,
    sums,
    border,
):
    step = pl.program_id(0)
    lane = lax.broadcasted_iota(jnp.int32, (BOX, LANES), 1)

    @pl.when(step == 0)
    def _():
        sums[...] = jnp.zeros_like(sums)
        here = edge_ref[...]
        here = here + pltpu.roll(here, LANES - 2, 1)
        for row, packed in enumerate((here + pltpu.roll(edge_before_ref[...], LANES - 2, 1), here + edge_after_ref[...])):
            for q in range(4):
                border[row, q * 64 : (q + 1) * 64, :] = pltpu.roll(packed, (LANES - q * 32) % LANES, 1)

    for row in range(2):
        low, high, total = sums[row, 0], sums[row, 1], sums[row, 2]
        for i in range(PACE):
            tall = first_ref[i] + second_ref[i] + (after_ref if row else before_ref)[i]
            beyond = pltpu.roll(border[row], LANES - 1 - (step * PACE + i) * 4, 1)
            left = pltpu.roll(jnp.where(lane == LANES - 1, beyond, tall), 1, 1)
            right = pltpu.roll(jnp.where(lane == 0, beyond, tall), LANES - 1, 1)
            wide = tall + left + right
            full = wide + pltpu.roll(wide, 1, 0) + pltpu.roll(wide, BOX - 1, 0)
            weight = 1.0 / (full / 27.0 + error_floor)
            low = low + weight * low_half_ref[i, row]
            high = high + weight * high_half_ref[i, row]
            total = total + weight
        sums[row, 0], sums[row, 1], sums[row, 2] = low, high, total

    @pl.when(step == BANDS // PACE - 1)
    def _():
        swap = side_ref[0] == 1
        for row in range(2):
            low = sums[row, 0] / sums[row, 2]
            high = sums[row, 1] / sums[row, 2]
            out_a_ref[row] = jnp.where(swap, high, low)
            out_b_ref[row] = jnp.where(swap, low, high)


def chip(depth, spot):
    return depth // 2 * SLABS + spot * 2 + depth % 2


def mirror_pairs(ahead):
    pairs = []
    for depth in range(8):
        for spot in range(16):
            goal = (depth, 15 - spot)
            if spot >= 8 and (depth + ahead) % 8 // 2 == 0:
                goal = ((depth + 1) % 8, 15 - spot) if depth % 2 else ((depth - 1) % 8, (16 - spot) % 8)
            pairs.append((chip(depth, spot), chip(*goal)))
    return pairs


def ring_pairs(step):
    return [(chip(d, s), chip((d + step) % 8, s)) for d in range(8) for s in range(16)]


def holder(block, side, core):
    return (2 * (block ^ side) + side) * 2 + core


def row_pairs(step, flip):
    pairs = []
    for n in range(SENDERS):
        goal = (n + step) % SENDERS
        pairs += [(holder(n // 2, side, n % 2), holder(goal // 2, side ^ flip, goal % 2)) for side in range(2)]
    return pairs


def home_pairs(flip):
    return [
        (holder(block, side, core), (2 * block + core) * 2 + (side ^ flip))
        for block in range(64)
        for side in range(2)
        for core in range(2)
    ]


def on_device(tiles, tile_index, pose_bin, bin_gain, cutoffs):
    slab_pos = lax.axis_index("slab")
    group_pos = lax.axis_index("particle")
    half_pos = lax.axis_index("half")
    side_pos = slab_pos % 2
    everyone = ("particle", "slab", "half")
    tile_width = 2 * TILE_ROWS * BOX
    _, particles, touched, _ = tiles.shape
    entries = particles * touched
    late = (slab_pos >= SLABS // 2).astype(jnp.int32)
    heights = [BLOCKS, BLOCKS, BLOCKS // 2, BLOCKS // 2] + [BLOCKS] * 5
    own, ahead, far_a, far_b, behind, *sent = pl.pallas_call(
        place_kernel,
        grid=(2,),
        out_shape=tuple(jax.ShapeDtypeStruct((h, tile_width), f32) for h in heights),
        in_specs=[
            SMEM,
            SMEM,
            pl.BlockSpec((touched, particles), lambda i: (0, 0)),
            pl.BlockSpec((1, particles), lambda i: (0, 0)),
            pl.BlockSpec((1, bin_gain.shape[1]), lambda i: (0, 0)),
            pl.BlockSpec((particles, touched, tile_width // 2), lambda i: (0, 0, i)),
        ],
        out_specs=tuple(pl.BlockSpec((h, tile_width // 2), lambda i: (0, i)) for h in heights),
        scratch_shapes=[pltpu.VMEM((4 * BLOCKS, entries), bf16)] * 3
        + [pltpu.VMEM((BOX, 2 * BOX), bf16), pltpu.VMEM((TILE_ROWS, 2, entries, BOX), bf16)]
        + [pltpu.VMEM((4 * BLOCKS, BOX), f32)],
        name="place",
    )(slab_pos.reshape(1), group_pos.reshape(1), tile_index[0].T, pose_bin, bin_gain, tiles[0])
    here = ("particle", "slab")
    up, down = ring_pairs(1), ring_pairs(-1)
    cut = BLOCKS // 2

    def send(part, pairs):
        return lax.ppermute(part, here, pairs)

    come = [send(sent[i], mirror_pairs(e)) for i, e in enumerate((3, -3, 1, -1))]
    rise, sink = send(far_a, up), send(far_b, down)
    rise = jnp.concatenate([come[0][:cut] + rise, come[0][cut:]], axis=0)
    sink = jnp.concatenate([come[1][:cut], come[1][cut:] + sink], axis=0)
    rise, sink = send(rise, up), send(sink, down)
    rise, sink = send(ahead + rise, up), send(behind + sink, down)
    rise, sink = send(come[2] + rise, up), send(come[3] + sink, down)
    plane = (slab_pos * 8 + group_pos * 2 + late).reshape(1)

    constants = [jnp.asarray(t) for t in tables()]
    sent = pl.pallas_call(
        planes_kernel,
        out_shape=jax.ShapeDtypeStruct((SENDERS // 4, 8, BANDS // 2, 8, LANES), f32),
        in_specs=[SMEM, SMEM] + [VMEM] * 5,
        out_specs=VMEM,
        scratch_shapes=[pltpu.VMEM((2 * BOX, BOX), bf16)] * 2 + [pltpu.VMEM((BOX, BOX), f32)],
        name="planes",
    )(cutoffs, plane, own, rise, sink, *constants[:2])
    gathered = lax.all_to_all(sent.reshape(2 * SENDERS, PER, LANES), everyone, split_axis=0, concat_axis=0, tiled=True)
    gathered = gathered.reshape(2 * SENDERS * PER, LANES)
    side_flag = jnp.where(jnp.arange(LANES, dtype=jnp.int32) == 0, side_pos, 0)

    steps = BANDS // PACE
    rows_spec = pl.BlockSpec((PACE, 2, BOX, LANES), lambda b: (b, 0, 0, 0))
    rows_shape = jax.ShapeDtypeStruct((BANDS, 2, BOX, LANES), f32)
    row_spec = pl.BlockSpec((PACE, BOX, LANES), lambda b: (b, 0, 0))
    row_shape = jax.ShapeDtypeStruct((BANDS, BOX, LANES), f32)
    edge_spec = pl.BlockSpec((64, LANES), lambda b: (0, 0))
    low_half, high_half, first, second, edge = pl.pallas_call(
        depth_kernel,
        grid=(BANDS // 2,),
        out_shape=(rows_shape, rows_shape, row_shape, row_shape, jax.ShapeDtypeStruct((64, LANES), f32)),
        in_specs=[
            pl.BlockSpec((2 * SENDERS * PER, LANES), lambda b: (0, 0)),
            pl.BlockSpec((2, BOX, BOX), lambda b: (0, 0, 0)),
        ],
        out_specs=(rows_spec, rows_spec, row_spec, row_spec, edge_spec),
        scratch_shapes=[pltpu.VMEM((BOX, LANES), f32)],
        name="depth",
    )(gathered, constants[2])
    before = lax.ppermute(second, everyone, row_pairs(1, 0))
    after = lax.ppermute(first, everyone, row_pairs(-1, 0))
    edges = [lax.ppermute(edge, everyone, row_pairs(n, 1)) for n in (0, 1, -1)]
    block_spec = pl.BlockSpec((2, BOX, LANES), lambda b: (0, 0, 0))
    block_shape = jax.ShapeDtypeStruct((2, BOX, LANES), f32)
    near, far = pl.pallas_call(
        blend_kernel,
        grid=(steps,),
        out_shape=(block_shape, block_shape),
        in_specs=[SMEM, rows_spec, rows_spec] + [row_spec] * 4 + [edge_spec] * 3,
        out_specs=(block_spec, block_spec),
        scratch_shapes=[pltpu.VMEM((2, 3, BOX, LANES), f32), pltpu.VMEM((2, BOX, LANES), f32)],
        name="blend",
    )(side_flag, low_half, high_half, first, second, before, after, *edges)
    near = lax.ppermute(near, everyone, home_pairs(0))
    far = lax.ppermute(far, everyone, home_pairs(1))
    low = jnp.where(half_pos == 0, near, far)
    high = jnp.where(half_pos == 0, far, near)
    refined = jnp.concatenate([low, high], axis=2)
    return jnp.transpose(refined, (1, 0, 2))[None]


def solution(mesh):
    placed = (
        P("half", "particle", "slab", None),
        P("half", "particle", "slab"),
        P("half", "particle"),
        P("half", None),
        P(),
    )

    return jax.shard_map(
        on_device,
        mesh=mesh,
        in_specs=placed,
        out_specs=P("half", None, ("particle", "slab"), None),
        check_vma=False,
    )
```

```python
import math

import jax
import jax.numpy as jnp
import numpy as np
from jax import lax
from jax.experimental import pallas as pl
from jax.experimental.pallas import tpu as pltpu
from jax.sharding import PartitionSpec as P

BOX = 256
HALF = BOX // 2
TILE_ROWS = 8
BLOCKS = BOX // TILE_ROWS
BANDS = 6
PACE = 2
GROUPS = 4
SLABS = 32
SENDERS = GROUPS * SLABS
PER = BANDS * 4
LANES = 128
error_floor = 1.0
bf16 = jnp.bfloat16
f32 = jnp.float32
VMEM = pl.BlockSpec(memory_space=pltpu.VMEM)
SMEM = pl.BlockSpec(memory_space=pltpu.SMEM)


def split(table):
    high = table.astype(np.float32).astype(jnp.bfloat16)
    low = (table - high.astype(np.float64)).astype(np.float32).astype(jnp.bfloat16)
    return high, low


def angles(left, right):
    return (np.outer(left, right) % BOX) * (2.0 * math.pi / BOX)


def tables():
    places = np.arange(BOX)
    near = np.arange(HALF)
    along_y, along_x = [], []
    for odd in range(2):
        turn = angles(near, near % BLOCKS * TILE_ROWS + near // BLOCKS * 2 + odd)
        cosine, sine = np.cos(turn), np.sin(turn)
        along_y.append(np.stack(split(np.block([[cosine, -sine], [sine, cosine]]))))
        turn = angles(2 * near + odd, near)
        cosine, sine = np.cos(turn), np.sin(turn)
        along_x.append(np.stack(split(np.block([[cosine, sine], [-sine, cosine]]))))
    along_y, along_x = np.stack(along_y), np.stack(along_x)
    sender = np.arange(SENDERS)
    group, slab = sender // SLABS, sender % SLABS
    plane = slab * 8 + group * 2 + (slab >= SLABS // 2)
    turn = angles(places, plane)
    even, odd = np.cos(turn), -np.sin(turn)
    odd[:, 0] = np.cos(math.pi * places)
    along_z = np.stack(split(np.concatenate([even, odd], axis=1) / BOX))
    return along_y, along_x, along_z


def two(value):
    high = value.astype(bf16)
    return high, (value - high.astype(f32)).astype(bf16)


def dot(a, b):
    return jnp.dot(a, b, preferred_element_type=f32)


def mark(rows, slots, gains):
    return jnp.where(rows == slots, gains, 0.0).astype(bf16)


def place_kernel(slab_ref, group_ref, index_ref, bin_ref, gain_ref, tile_ref, *refs):
    outs, (kept_mark, sent_mark, sent_mark_first, turn, moved, saved) = refs[:9], refs[9:]
    step = pl.program_id(0)
    slab, group = slab_ref[0], group_ref[0]
    depth, late = group * 2 + slab % 2, slab // (SLABS // 2)
    row = lax.broadcasted_iota(jnp.int32, (BLOCKS, BOX), 0)
    col = lax.broadcasted_iota(jnp.int32, (BLOCKS, BOX), 1)
    own_line = [((depth + d) & 7) // 2 for d in (0, 2, 4, 6)]
    sent_line = [((depth + d) & 7) // 2 for d in (3, 5, 1, 7)]

    @pl.when(step == 0)
    def _():
        touched, particles = index_ref.shape
        entries = touched * particles
        bins = gain_ref.shape[1]
        line = lax.broadcasted_iota(jnp.int32, (particles, entries), 0)
        wide = lax.broadcasted_iota(jnp.int32, (particles, entries), 1)
        spread = jnp.where(wide // touched == line, 1.0, 0.0).astype(bf16)
        slots = dot(index_ref[...].astype(f32).astype(bf16), spread)
        line = lax.broadcasted_iota(jnp.int32, slots.shape, 0)
        wide = lax.broadcasted_iota(jnp.int32, slots.shape, 1)
        slots = jnp.sum(jnp.where(wide % touched == line, slots, 0.0), axis=0, keepdims=True)
        slots = jnp.broadcast_to(slots, (BLOCKS, entries)).astype(jnp.int32)
        line = lax.broadcasted_iota(jnp.int32, (bins, bins), 0)
        wide = lax.broadcasted_iota(jnp.int32, (bins, bins), 1)
        table = jnp.broadcast_to(gain_ref[...].astype(f32), (bins, bins))
        table = jnp.sum(jnp.where(line == wide, table, 0.0), axis=1, keepdims=True)
        line = lax.broadcasted_iota(jnp.int32, (bins, particles), 0)
        gains = jnp.where(line == bin_ref[...], table, 0.0).astype(bf16)
        gains = jnp.sum(dot(gains, spread), axis=0, keepdims=True)
        gains = jnp.broadcast_to(gains, (BLOCKS, entries))
        for i in range(4):
            rows = pl.ds(i * BLOCKS, BLOCKS)
            kept_mark[rows, :] = mark((2 * own_line[i] + late) * BLOCKS + row, slots, gains)
            start = jnp.where(late == 1, (8 - 2 * sent_line[i]) & 7, 7 - 2 * sent_line[i]) * BLOCKS
            sent_mark[rows, :] = mark(start + BLOCKS - 1 - row, slots, gains)
            sent_mark_first[rows, :] = mark(start + ((BLOCKS - row) & (BLOCKS - 1)), slots, gains)
        line = lax.broadcasted_iota(jnp.int32, (BOX, BOX), 0)
        wide = lax.broadcasted_iota(jnp.int32, (BOX, BOX), 1)
        wide = (wide & (HALF - 1)) * 2 + (wide >> 7)
        turn[:, :BOX] = jnp.where(line == wide, 1.0, 0.0).astype(bf16)
        turn[:, BOX:] = jnp.where(((line + wide) & (BOX - 1)) == 0, 1.0, 0.0).astype(bf16)

    sign = jnp.where(step == 1, -1.0, 1.0)
    tile = tile_ref[...].reshape(-1, TILE_ROWS * BOX)
    for r in range(TILE_ROWS):
        both = dot(tile[:, r * BOX : (r + 1) * BOX], turn[...])
        moved[r, 0] = both[:, :BOX].astype(bf16)
        moved[r, 1] = (both[:, BOX:] * sign).astype(bf16)
    for r in range(TILE_ROWS):
        cols = pl.ds(r * BOX, BOX)
        kept = dot(kept_mark[...], moved[r, 0])
        sent = dot((sent_mark if r else sent_mark_first)[...], moved[(TILE_ROWS - r) % TILE_ROWS, 1])
        if r == 0:
            first = (row == 0) & (col == 0)
            last_sent = saved[...]
            saved[...] = sent
        parts = []
        for i in range(4):
            part = kept[i * BLOCKS : (i + 1) * BLOCKS]
            if r == 0:
                part = jnp.where(first & (step == 1) & (slab == 0) & (own_line[i] == 0), 0.0, part)
            parts.append(part)
        for i in range(4):
            part = sent[i * BLOCKS : (i + 1) * BLOCKS]
            alone = 0.0
            if r == 0:
                alone = jnp.where(first & (step == 1), last_sent[i * BLOCKS : (i + 1) * BLOCKS], 0.0)
            parts.append(jnp.where((slab == SLABS // 2) & (sent_line[i] == 0), alone, part))
        parts[2:3] = [parts[2][: BLOCKS // 2], parts[2][BLOCKS // 2 :]]
        for out_ref, part in zip(outs, parts):
            out_ref[:, cols] = part


def beside(*parts):
    return jnp.concatenate(parts, axis=1)


def above(*parts):
    return jnp.concatenate(parts, axis=0)


def planes_kernel(
    cut_ref, kz_ref, own_ref, up_ref, down_ref, y_ref, x_ref, out_ref, sh, sl, radius, ready, done
):
    alone = kz_ref[0] == 0
    for i in range(16):
        c, r = divmod(i, TILE_ROWS)
        cols = pl.ds(i * BOX, BOX)
        rows = pl.ds(r % 2 * BOX + c * HALF + r // 2 * BLOCKS, BLOCKS)
        whole = own_ref[:, cols] + up_ref[:, cols] + down_ref[:, cols]
        if i == TILE_ROWS:
            last = whole[0:1, 0:1]
        sh[rows, :], sl[rows, :] = two(whole)
    line = lax.broadcasted_iota(jnp.int32, (BOX, BOX), 0)
    col = lax.broadcasted_iota(jnp.int32, (BOX, BOX), 1)
    ky = (line & (BLOCKS - 1)) * TILE_ROWS + ((line >> 5) & 3) * 2 + (line >> 7)
    kx = (col & (HALF - 1)) * 2 + (col >> 7)
    ky = ((ky + HALF) & (BOX - 1)) - HALF
    kx = ((kx + HALF) & (BOX - 1)) - HALF
    kz = ((kz_ref[0] + HALF) & (BOX - 1)) - HALF
    radius[...] = (ky * ky + kx * kx + kz * kz).astype(f32)
    place_in = lax.broadcasted_iota(jnp.int32, (BLOCKS, 8, LANES), 1)
    upper, even_unit = place_in < 4, (place_in & 2) == 0

    @pl.loop(0, BANDS // 2)
    def _(pair):
        parts = []
        for odd in range(2):
            sides = []
            for i in range(2):
                cut = cut_ref[pair * 2 + i]
                near = radius[odd * HALF : (odd + 1) * HALF, :] <= (cut * cut).astype(f32)
                mask = jnp.where(near, 1.0, 0.0).astype(bf16)
                mask = above(mask, mask)
                rows = pl.ds(odd * BOX, BOX)
                high, low = sh[rows, :] * mask, sl[rows, :] * mask
                sides.append(above(high, high, low))
            parts.append(dot(beside(y_ref[odd, 0], y_ref[odd, 1], y_ref[odd, 0]), beside(*sides)))
        plus, minus = parts[0] + parts[1], parts[0] - parts[1]
        mids = ([], [])
        for i in range(2):
            cols = slice(i * BOX, (i + 1) * BOX)
            real = two(above(plus[:HALF, cols], minus[:HALF, cols]))
            imag = two(above(plus[HALF:, cols], minus[HALF:, cols]))
            for odd in range(2):
                few = slice(odd * HALF, (odd + 1) * HALF)
                high = beside(real[0][:, few], imag[0][:, few])
                low = beside(real[1][:, few], imag[1][:, few])
                mids[odd].append(beside(high, low, high))
        parts = [dot(above(*mids[odd]), above(x_ref[odd, 0], x_ref[odd, 0], x_ref[odd, 1])) for odd in range(2)]
        for side in range(2):
            units = []
            for i in range(2):
                value = jnp.where(cut_ref[pair * 2 + i] >= HALF, last, 0.0)
                first, second = parts[0][i * BOX : (i + 1) * BOX], parts[1][i * BOX : (i + 1) * BOX]
                full = first - second if side else first + second
                even, odd = full[:, :LANES], full[:, LANES:]
                odd = jnp.where(alone, jnp.broadcast_to(value, odd.shape), odd)
                units += [even.reshape(BLOCKS, 8, LANES), odd.reshape(BLOCKS, 8, LANES)]
            for odd_block in range(2):
                if odd_block:
                    halves = [jnp.where(upper, pltpu.roll(units[q], 4, 1), units[q + 2]) for q in range(2)]
                else:
                    halves = [jnp.where(upper, units[q], pltpu.roll(units[q + 2], 4, 1)) for q in range(2)]
                goal = 2 * (2 * (odd_block ^ side) + side)
                ready[pair, :, goal] = jnp.where(even_unit, halves[0], pltpu.roll(halves[1], 2, 1))
                ready[pair, :, goal + 1] = jnp.where(even_unit, pltpu.roll(halves[0], 6, 1), halves[1])
        pltpu.make_async_copy(ready.at[pair], out_ref.at[:, :, pair], done.at[pair]).start()

    for pair in range(BANDS // 2):
        pltpu.make_async_copy(ready.at[pair], out_ref.at[:, :, pair], done.at[pair]).wait()


def depth_kernel(come_ref, z_ref, low_half_ref, high_half_ref, first_ref, second_ref, edge_ref, edge):
    pair = pl.program_id(0)
    lane = lax.broadcasted_iota(jnp.int32, (BOX, LANES), 1)
    turn = beside(z_ref[0], z_ref[1], z_ref[0])
    found = jnp.where(pair == 0, 0.0, edge[...])
    for i in range(2):
        maps = []
        for half in range(2):
            start = half * PER + pair * 8 + i * 4
            sides = [
                beside(*[come_ref[pl.ds(start + c * 2 + j, SENDERS, stride=2 * PER), :] for j in range(2)])
                for c in range(2)
            ]
            high, low = two(above(*sides))
            maps.append(dot(turn, above(high, high, low)))
        gap = maps[0] - maps[1]
        gap = gap * gap
        for row in range(2):
            cols = slice(row * LANES, (row + 1) * LANES)
            low_half_ref[i, row] = maps[0][:, cols]
            high_half_ref[i, row] = maps[1][:, cols]
            part = gap[:, cols]
            (first_ref, second_ref)[row][i] = part
            spot = (pair * 2 + i) * 4 + row * 2
            found = jnp.where((lane >> 1) == (spot >> 1), pltpu.roll(part, spot + 1, 1), found)
    edge[...] = found

    @pl.when(pair == BANDS // 2 - 1)
    def _():
        narrow = lax.broadcasted_iota(jnp.int32, (64, LANES), 1)
        packed = edge[0:64, :]
        for q in range(1, 4):
            packed = jnp.where((narrow >> 5) == q, pltpu.roll(edge[q * 64 : (q + 1) * 64, :], q * 32, 1), packed)
        edge_ref[...] = packed


def blend_kernel(
    side_ref,
    low_half_ref,
    high_half_ref,
    first_ref,
    second_ref,
    before_ref,
    after_ref,
    edge_ref,
    edge_before_ref,
    edge_after_ref,
    out_a_ref,
    out_b_ref,
    sums,
    border,
):
    step = pl.program_id(0)
    lane = lax.broadcasted_iota(jnp.int32, (BOX, LANES), 1)

    @pl.when(step == 0)
    def _():
        sums[...] = jnp.zeros_like(sums)
        here = edge_ref[...]
        here = here + pltpu.roll(here, LANES - 2, 1)
        for row, packed in enumerate((here + pltpu.roll(edge_before_ref[...], LANES - 2, 1), here + edge_after_ref[...])):
            for q in range(4):
                border[row, q * 64 : (q + 1) * 64, :] = pltpu.roll(packed, (LANES - q * 32) % LANES, 1)

    for row in range(2):
        low, high, total = sums[row, 0], sums[row, 1], sums[row, 2]
        for i in range(PACE):
            tall = first_ref[i] + second_ref[i] + (after_ref if row else before_ref)[i]
            beyond = pltpu.roll(border[row], LANES - 1 - (step * PACE + i) * 4, 1)
            left = pltpu.roll(jnp.where(lane == LANES - 1, beyond, tall), 1, 1)
            right = pltpu.roll(jnp.where(lane == 0, beyond, tall), LANES - 1, 1)
            wide = tall + left + right
            full = wide + pltpu.roll(wide, 1, 0) + pltpu.roll(wide, BOX - 1, 0)
            weight = 1.0 / (full + 27.0 * error_floor)
            low = low + weight * low_half_ref[i, row]
            high = high + weight * high_half_ref[i, row]
            total = total + weight
        sums[row, 0], sums[row, 1], sums[row, 2] = low, high, total

    @pl.when(step == BANDS // PACE - 1)
    def _():
        swap = side_ref[0] == 1
        for row in range(2):
            low = sums[row, 0] / sums[row, 2]
            high = sums[row, 1] / sums[row, 2]
            out_a_ref[row] = jnp.where(swap, high, low)
            out_b_ref[row] = jnp.where(swap, low, high)


def chip(depth, spot):
    return depth // 2 * SLABS + spot * 2 + depth % 2


def mirror_pairs(ahead):
    pairs = []
    for depth in range(8):
        for spot in range(16):
            goal = (depth, 15 - spot)
            if spot >= 8 and (depth + ahead) % 8 // 2 == 0:
                goal = ((depth + 1) % 8, 15 - spot) if depth % 2 else ((depth - 1) % 8, (16 - spot) % 8)
            pairs.append((chip(depth, spot), chip(*goal)))
    return pairs


def ring_pairs(step):
    return [(chip(d, s), chip((d + step) % 8, s)) for d in range(8) for s in range(16)]


def holder(block, side, core):
    return (2 * (block ^ side) + side) * 2 + core


def row_pairs(step, flip):
    pairs = []
    for n in range(SENDERS):
        goal = (n + step) % SENDERS
        pairs += [(holder(n // 2, side, n % 2), holder(goal // 2, side ^ flip, goal % 2)) for side in range(2)]
    return pairs


def home_pairs(flip):
    return [
        (holder(block, side, core), (2 * block + core) * 2 + (side ^ flip))
        for block in range(64)
        for side in range(2)
        for core in range(2)
    ]


def on_device(tiles, tile_index, pose_bin, bin_gain, cutoffs):
    slab_pos = lax.axis_index("slab")
    group_pos = lax.axis_index("particle")
    half_pos = lax.axis_index("half")
    side_pos = slab_pos % 2
    everyone = ("particle", "slab", "half")
    tile_width = 2 * TILE_ROWS * BOX
    _, particles, touched, _ = tiles.shape
    entries = particles * touched
    late = (slab_pos >= SLABS // 2).astype(jnp.int32)
    heights = [BLOCKS, BLOCKS, BLOCKS // 2, BLOCKS // 2] + [BLOCKS] * 5
    own, ahead, far_a, far_b, behind, *sent = pl.pallas_call(
        place_kernel,
        grid=(2,),
        out_shape=tuple(jax.ShapeDtypeStruct((h, tile_width), f32) for h in heights),
        in_specs=[
            SMEM,
            SMEM,
            pl.BlockSpec((touched, particles), lambda i: (0, 0)),
            pl.BlockSpec((1, particles), lambda i: (0, 0)),
            pl.BlockSpec((1, bin_gain.shape[1]), lambda i: (0, 0)),
            pl.BlockSpec((particles, touched, tile_width // 2), lambda i: (0, 0, i)),
        ],
        out_specs=tuple(pl.BlockSpec((h, tile_width // 2), lambda i: (0, i)) for h in heights),
        scratch_shapes=[pltpu.VMEM((4 * BLOCKS, entries), bf16)] * 3
        + [pltpu.VMEM((BOX, 2 * BOX), bf16), pltpu.VMEM((TILE_ROWS, 2, entries, BOX), bf16)]
        + [pltpu.VMEM((4 * BLOCKS, BOX), f32)],
        name="place",
    )(slab_pos.reshape(1), group_pos.reshape(1), tile_index[0].T, pose_bin, bin_gain, tiles[0])
    here = ("particle", "slab")
    up, down = ring_pairs(1), ring_pairs(-1)
    cut = BLOCKS // 2

    def send(part, pairs):
        return lax.ppermute(part, here, pairs)

    come = [send(sent[i], mirror_pairs(e)) for i, e in enumerate((3, -3, 1, -1))]
    rise, sink = send(far_a, up), send(far_b, down)
    rise = jnp.concatenate([come[0][:cut] + rise, come[0][cut:]], axis=0)
    sink = jnp.concatenate([come[1][:cut], come[1][cut:] + sink], axis=0)
    rise, sink = send(rise, up), send(sink, down)
    rise, sink = send(ahead + rise, up), send(behind + sink, down)
    rise, sink = send(come[2] + rise, up), send(come[3] + sink, down)
    plane = (slab_pos * 8 + group_pos * 2 + late).reshape(1)

    constants = [jnp.asarray(t) for t in tables()]
    sent = pl.pallas_call(
        planes_kernel,
        out_shape=pltpu.HBM((SENDERS // 4, 8, BANDS // 2, 8, LANES), f32),
        in_specs=[SMEM, SMEM] + [VMEM] * 5,
        out_specs=pl.BlockSpec(memory_space=pltpu.HBM),
        scratch_shapes=[pltpu.VMEM((2 * BOX, BOX), bf16)] * 2
        + [
            pltpu.VMEM((BOX, BOX), f32),
            pltpu.VMEM((BANDS // 2, SENDERS // 4, 8, 8, LANES), f32),
            pltpu.SemaphoreType.DMA((BANDS // 2,)),
        ],
        name="planes",
        compiler_params=pltpu.CompilerParams(vmem_limit_bytes=16 * 2**20),
    )(cutoffs, plane, own, rise, sink, *constants[:2])
    gathered = lax.all_to_all(sent.reshape(2 * SENDERS, PER, LANES), everyone, split_axis=0, concat_axis=0, tiled=True)
    gathered = gathered.reshape(2 * SENDERS * PER, LANES)
    side_flag = jnp.where(jnp.arange(LANES, dtype=jnp.int32) == 0, side_pos, 0)

    steps = BANDS // PACE
    rows_spec = pl.BlockSpec((PACE, 2, BOX, LANES), lambda b: (b, 0, 0, 0))
    rows_shape = jax.ShapeDtypeStruct((BANDS, 2, BOX, LANES), f32)
    row_spec = pl.BlockSpec((PACE, BOX, LANES), lambda b: (b, 0, 0))
    row_shape = jax.ShapeDtypeStruct((BANDS, BOX, LANES), f32)
    edge_spec = pl.BlockSpec((64, LANES), lambda b: (0, 0))
    low_half, high_half, first, second, edge = pl.pallas_call(
        depth_kernel,
        grid=(BANDS // 2,),
        out_shape=(rows_shape, rows_shape, row_shape, row_shape, jax.ShapeDtypeStruct((64, LANES), f32)),
        in_specs=[
            pl.BlockSpec((2 * SENDERS * PER, LANES), lambda b: (0, 0)),
            pl.BlockSpec((2, BOX, BOX), lambda b: (0, 0, 0)),
        ],
        out_specs=(rows_spec, rows_spec, row_spec, row_spec, edge_spec),
        scratch_shapes=[pltpu.VMEM((BOX, LANES), f32)],
        name="depth",
        compiler_params=pltpu.CompilerParams(vmem_limit_bytes=20 * 2**20),
    )(gathered, constants[2])
    before = lax.ppermute(second, everyone, row_pairs(1, 0))
    after = lax.ppermute(first, everyone, row_pairs(-1, 0))
    edges = [lax.ppermute(edge, everyone, row_pairs(n, 1)) for n in (0, 1, -1)]
    block_spec = pl.BlockSpec((2, BOX, LANES), lambda b: (0, 0, 0))
    block_shape = jax.ShapeDtypeStruct((2, BOX, LANES), f32)
    near, far = pl.pallas_call(
        blend_kernel,
        grid=(steps,),
        out_shape=(block_shape, block_shape),
        in_specs=[SMEM, rows_spec, rows_spec] + [row_spec] * 4 + [edge_spec] * 3,
        out_specs=(block_spec, block_spec),
        scratch_shapes=[pltpu.VMEM((2, 3, BOX, LANES), f32), pltpu.VMEM((2, BOX, LANES), f32)],
        name="blend",
        compiler_params=pltpu.CompilerParams(vmem_limit_bytes=16 * 2**20),
    )(side_flag, low_half, high_half, first, second, before, after, *edges)
    near = lax.ppermute(near, everyone, home_pairs(0))
    far = lax.ppermute(far, everyone, home_pairs(1))
    low = jnp.where(half_pos == 0, near, far)
    high = jnp.where(half_pos == 0, far, near)
    refined = jnp.concatenate([low, high], axis=2)
    return jnp.transpose(refined, (1, 0, 2))[None]


def solution(mesh):
    placed = (
        P("half", "particle", "slab", None),
        P("half", "particle", "slab"),
        P("half", "particle"),
        P("half", None),
        P(),
    )

    return jax.shard_map(
        on_device,
        mesh=mesh,
        in_specs=placed,
        out_specs=P("half", None, ("particle", "slab"), None),
        check_vma=False,
    )
```

```python
import math

import jax
import jax.numpy as jnp
import numpy as np
from jax import lax
from jax.experimental import pallas as pl
from jax.experimental.pallas import tpu as pltpu
from jax.sharding import PartitionSpec as P

BOX = 256
HALF = BOX // 2
TILE_ROWS = 8
BLOCKS = BOX // TILE_ROWS
BANDS = 6
PACE = 2
GROUPS = 4
SLABS = 32
SENDERS = GROUPS * SLABS
PER = BANDS * 4
LANES = 128
error_floor = 1.0
bf16 = jnp.bfloat16
f32 = jnp.float32
VMEM = pl.BlockSpec(memory_space=pltpu.VMEM)
SMEM = pl.BlockSpec(memory_space=pltpu.SMEM)


def split(table):
    high = table.astype(np.float32).astype(jnp.bfloat16)
    low = (table - high.astype(np.float64)).astype(np.float32).astype(jnp.bfloat16)
    return high, low


def angles(left, right):
    return (np.outer(left, right) % BOX) * (2.0 * math.pi / BOX)


def tables():
    places = np.arange(BOX)
    near = np.arange(HALF)
    along_y, along_x = [], []
    for odd in range(2):
        turn = angles(near, near % BLOCKS * TILE_ROWS + near // BLOCKS * 2 + odd)
        cosine, sine = np.cos(turn), np.sin(turn)
        along_y.append(np.stack(split(np.concatenate([cosine, sine], axis=1))))
        turn = angles(2 * near + odd, near)
        cosine, sine = np.cos(turn), np.sin(turn)
        along_x.append(np.stack(split(np.concatenate([cosine, sine], axis=1))))
    along_y, along_x = np.stack(along_y), np.stack(along_x)
    sender = np.arange(SENDERS)
    group, slab = sender // SLABS, sender % SLABS
    plane = slab * 8 + group * 2 + (slab >= SLABS // 2)
    turn = angles(places, plane)
    even, odd = np.cos(turn), -np.sin(turn)
    odd[:, 0] = np.cos(math.pi * places)
    along_z = np.stack(split(np.concatenate([even, odd], axis=1) / BOX))
    return along_y, along_x, along_z


def two(value):
    high = value.astype(bf16)
    return high, (value - high.astype(f32)).astype(bf16)


def dot(a, b):
    return jnp.dot(a, b, preferred_element_type=f32)


def mark(rows, slots, gains):
    return jnp.where(rows == slots, gains, 0.0).astype(bf16)


def place_kernel(slab_ref, group_ref, index_ref, bin_ref, gain_ref, tile_ref, *refs):
    outs, (kept_mark, sent_mark, sent_mark_first, turn, moved, saved) = refs[:15], refs[15:]
    step = pl.program_id(0)
    slab, group = slab_ref[0], group_ref[0]
    depth, late = group * 2 + slab % 2, slab // (SLABS // 2)
    row = lax.broadcasted_iota(jnp.int32, (BLOCKS, BOX), 0)
    col = lax.broadcasted_iota(jnp.int32, (BLOCKS, BOX), 1)
    own_line = [((depth + d) & 7) // 2 for d in (0, 2, 4, 6)]
    sent_line = [((depth + d) & 7) // 2 for d in (3, 5, 1, 7)]

    @pl.when(step == 0)
    def _():
        touched, particles = index_ref.shape
        entries = touched * particles
        bins = gain_ref.shape[1]
        line = lax.broadcasted_iota(jnp.int32, (particles, entries), 0)
        wide = lax.broadcasted_iota(jnp.int32, (particles, entries), 1)
        spread = jnp.where(wide // touched == line, 1.0, 0.0).astype(bf16)
        slots = dot(index_ref[...].astype(f32).astype(bf16), spread)
        line = lax.broadcasted_iota(jnp.int32, slots.shape, 0)
        wide = lax.broadcasted_iota(jnp.int32, slots.shape, 1)
        slots = jnp.sum(jnp.where(wide % touched == line, slots, 0.0), axis=0, keepdims=True)
        slots = jnp.broadcast_to(slots, (BLOCKS, entries)).astype(jnp.int32)
        line = lax.broadcasted_iota(jnp.int32, (bins, bins), 0)
        wide = lax.broadcasted_iota(jnp.int32, (bins, bins), 1)
        table = jnp.broadcast_to(gain_ref[...].astype(f32), (bins, bins))
        table = jnp.sum(jnp.where(line == wide, table, 0.0), axis=1, keepdims=True)
        line = lax.broadcasted_iota(jnp.int32, (bins, particles), 0)
        gains = jnp.where(line == bin_ref[...], table, 0.0).astype(bf16)
        gains = jnp.sum(dot(gains, spread), axis=0, keepdims=True)
        gains = jnp.broadcast_to(gains, (BLOCKS, entries))
        for i in range(4):
            rows = pl.ds(i * BLOCKS, BLOCKS)
            kept_mark[rows, :] = mark((2 * own_line[i] + late) * BLOCKS + row, slots, gains)
            start = jnp.where(late == 1, (8 - 2 * sent_line[i]) & 7, 7 - 2 * sent_line[i]) * BLOCKS
            sent_mark[rows, :] = mark(start + BLOCKS - 1 - row, slots, gains)
            sent_mark_first[rows, :] = mark(start + ((BLOCKS - row) & (BLOCKS - 1)), slots, gains)
        line = lax.broadcasted_iota(jnp.int32, (BOX, BOX), 0)
        wide = lax.broadcasted_iota(jnp.int32, (BOX, BOX), 1)
        wide = (wide & (HALF - 1)) * 2 + (wide >> 7)
        turn[:, :BOX] = jnp.where(line == wide, 1.0, 0.0).astype(bf16)
        turn[:, BOX:] = jnp.where(((line + wide) & (BOX - 1)) == 0, 1.0, 0.0).astype(bf16)

    sign = jnp.where(step == 1, -1.0, 1.0)
    tile = tile_ref[...].reshape(-1, TILE_ROWS * BOX)
    for r in range(TILE_ROWS):
        both = dot(tile[:, r * BOX : (r + 1) * BOX], turn[...])
        moved[r, 0] = both[:, :BOX].astype(bf16)
        moved[r, 1] = (both[:, BOX:] * sign).astype(bf16)
    for r in range(TILE_ROWS):
        cols = pl.ds(r * BOX, BOX)
        kept = dot(kept_mark[...], moved[r, 0])
        sent = dot((sent_mark if r else sent_mark_first)[...], moved[(TILE_ROWS - r) % TILE_ROWS, 1])
        if r == 0:
            first = (row == 0) & (col == 0)
            last_sent = saved[...]
            saved[...] = sent
        parts = []
        for i in range(4):
            part = kept[i * BLOCKS : (i + 1) * BLOCKS]
            if r == 0:
                part = jnp.where(first & (step == 1) & (slab == 0) & (own_line[i] == 0), 0.0, part)
            parts.append(part)
        for i in range(4):
            part = sent[i * BLOCKS : (i + 1) * BLOCKS]
            alone = 0.0
            if r == 0:
                alone = jnp.where(first & (step == 1), last_sent[i * BLOCKS : (i + 1) * BLOCKS], 0.0)
            parts.append(jnp.where((slab == SLABS // 2) & (sent_line[i] == 0), alone, part))
        parts = parts[:1] + [part[start : start + BLOCKS // 2] for part in parts[1:] for start in (0, BLOCKS // 2)]
        for out_ref, part in zip(outs, parts):
            out_ref[:, cols] = part


def beside(*parts):
    return jnp.concatenate(parts, axis=1)


def above(*parts):
    return jnp.concatenate(parts, axis=0)


def planes_kernel(
    cut_ref, kz_ref, own_ref, up_a_ref, up_b_ref, down_a_ref, down_b_ref, few_y_ref, few_x_ref, out_ref, sh, sl, radius, ready, done, y_ref, x_ref
):
    for odd in range(2):
        for part in range(2):
            cosine, sine = few_y_ref[odd, part, :, :HALF], few_y_ref[odd, part, :, HALF:]
            y_ref[odd, part] = above(beside(cosine, -sine), beside(sine, cosine))
            cosine, sine = few_x_ref[odd, part, :, :HALF], few_x_ref[odd, part, :, HALF:]
            x_ref[odd, part] = above(beside(cosine, sine), beside(-sine, cosine))
    alone = kz_ref[0] == 0
    for i in range(16):
        c, r = divmod(i, TILE_ROWS)
        cols = pl.ds(i * BOX, BOX)
        rows = pl.ds(r % 2 * BOX + c * HALF + r // 2 * BLOCKS, BLOCKS)
        whole = above(up_a_ref[:, cols] + down_a_ref[:, cols], up_b_ref[:, cols] + down_b_ref[:, cols])
        whole = own_ref[:, cols] + whole
        if i == TILE_ROWS:
            last = whole[0:1, 0:1]
        sh[rows, :], sl[rows, :] = two(whole)
    line = lax.broadcasted_iota(jnp.int32, (BOX, BOX), 0)
    col = lax.broadcasted_iota(jnp.int32, (BOX, BOX), 1)
    ky = (line & (BLOCKS - 1)) * TILE_ROWS + ((line >> 5) & 3) * 2 + (line >> 7)
    kx = (col & (HALF - 1)) * 2 + (col >> 7)
    ky = ((ky + HALF) & (BOX - 1)) - HALF
    kx = ((kx + HALF) & (BOX - 1)) - HALF
    kz = ((kz_ref[0] + HALF) & (BOX - 1)) - HALF
    radius[...] = (ky * ky + kx * kx + kz * kz).astype(f32)
    place_in = lax.broadcasted_iota(jnp.int32, (BLOCKS, 8, LANES), 1)
    upper, even_unit = place_in < 4, (place_in & 2) == 0

    @pl.loop(0, BANDS // 2)
    def _(pair):
        parts = []
        for odd in range(2):
            sides = []
            for i in range(2):
                cut = cut_ref[pair * 2 + i]
                near = radius[odd * HALF : (odd + 1) * HALF, :] <= (cut * cut).astype(f32)
                mask = jnp.where(near, 1.0, 0.0).astype(bf16)
                mask = above(mask, mask)
                rows = pl.ds(odd * BOX, BOX)
                high, low = sh[rows, :] * mask, sl[rows, :] * mask
                sides.append(above(high, high, low))
            parts.append(dot(beside(y_ref[odd, 0], y_ref[odd, 1], y_ref[odd, 0]), beside(*sides)))
        plus, minus = parts[0] + parts[1], parts[0] - parts[1]
        mids = ([], [])
        for i in range(2):
            cols = slice(i * BOX, (i + 1) * BOX)
            real = two(above(plus[:HALF, cols], minus[:HALF, cols]))
            imag = two(above(plus[HALF:, cols], minus[HALF:, cols]))
            for odd in range(2):
                few = slice(odd * HALF, (odd + 1) * HALF)
                high = beside(real[0][:, few], imag[0][:, few])
                low = beside(real[1][:, few], imag[1][:, few])
                mids[odd].append(beside(high, low, high))
        parts = [dot(above(*mids[odd]), above(x_ref[odd, 0], x_ref[odd, 0], x_ref[odd, 1])) for odd in range(2)]
        for side in range(2):
            units = []
            for i in range(2):
                value = jnp.where(cut_ref[pair * 2 + i] >= HALF, last, 0.0)
                first, second = parts[0][i * BOX : (i + 1) * BOX], parts[1][i * BOX : (i + 1) * BOX]
                full = first - second if side else first + second
                even, odd = full[:, :LANES], full[:, LANES:]
                odd = jnp.where(alone, jnp.broadcast_to(value, odd.shape), odd)
                units += [even.reshape(BLOCKS, 8, LANES), odd.reshape(BLOCKS, 8, LANES)]
            for odd_block in range(2):
                if odd_block:
                    halves = [jnp.where(upper, pltpu.roll(units[q], 4, 1), units[q + 2]) for q in range(2)]
                else:
                    halves = [jnp.where(upper, units[q], pltpu.roll(units[q + 2], 4, 1)) for q in range(2)]
                goal = 2 * (2 * (odd_block ^ side) + side)
                ready[pair, :, goal] = jnp.where(even_unit, halves[0], pltpu.roll(halves[1], 2, 1))
                ready[pair, :, goal + 1] = jnp.where(even_unit, pltpu.roll(halves[0], 6, 1), halves[1])
        pltpu.make_async_copy(ready.at[pair], out_ref.at[:, :, pair], done.at[pair]).start()

    for pair in range(BANDS // 2):
        pltpu.make_async_copy(ready.at[pair], out_ref.at[:, :, pair], done.at[pair]).wait()


def depth_kernel(come_ref, z_ref, low_half_ref, high_half_ref, first_ref, second_ref, edge_ref, edge):
    pair = pl.program_id(0)
    lane = lax.broadcasted_iota(jnp.int32, (BOX, LANES), 1)
    turn = beside(z_ref[0], z_ref[1], z_ref[0])
    found = jnp.where(pair == 0, 0.0, edge[...])
    for i in range(2):
        maps = []
        for half in range(2):
            start = half * PER + pair * 8 + i * 4
            sides = [
                beside(*[come_ref[pl.ds(start + c * 2 + j, SENDERS, stride=2 * PER), :] for j in range(2)])
                for c in range(2)
            ]
            high, low = two(above(*sides))
            maps.append(dot(turn, above(high, high, low)))
        gap = maps[0] - maps[1]
        gap = gap * gap
        for row in range(2):
            cols = slice(row * LANES, (row + 1) * LANES)
            low_half_ref[i, row] = maps[0][:, cols]
            high_half_ref[i, row] = maps[1][:, cols]
            part = gap[:, cols]
            (first_ref, second_ref)[row][i] = part
            spot = (pair * 2 + i) * 4 + row * 2
            found = jnp.where((lane >> 1) == (spot >> 1), pltpu.roll(part, spot + 1, 1), found)
    edge[...] = found

    @pl.when(pair == BANDS // 2 - 1)
    def _():
        narrow = lax.broadcasted_iota(jnp.int32, (64, LANES), 1)
        packed = edge[0:64, :]
        for q in range(1, 4):
            packed = jnp.where((narrow >> 5) == q, pltpu.roll(edge[q * 64 : (q + 1) * 64, :], q * 32, 1), packed)
        edge_ref[...] = packed


def blend_kernel(
    side_ref,
    low_half_ref,
    high_half_ref,
    first_ref,
    second_ref,
    before_ref,
    after_ref,
    edge_ref,
    edge_before_ref,
    edge_after_ref,
    out_a_ref,
    out_b_ref,
    sums,
    border,
):
    step = pl.program_id(0)
    lane = lax.broadcasted_iota(jnp.int32, (BOX, LANES), 1)

    @pl.when(step == 0)
    def _():
        sums[...] = jnp.zeros_like(sums)
        here = edge_ref[...]
        here = here + pltpu.roll(here, LANES - 2, 1)
        for row, packed in enumerate((here + pltpu.roll(edge_before_ref[...], LANES - 2, 1), here + edge_after_ref[...])):
            for q in range(4):
                border[row, q * 64 : (q + 1) * 64, :] = pltpu.roll(packed, (LANES - q * 32) % LANES, 1)

    for row in range(2):
        low, high, total = sums[row, 0], sums[row, 1], sums[row, 2]
        for i in range(PACE):
            tall = first_ref[i] + second_ref[i] + (after_ref if row else before_ref)[i]
            beyond = pltpu.roll(border[row], LANES - 1 - (step * PACE + i) * 4, 1)
            left = pltpu.roll(jnp.where(lane == LANES - 1, beyond, tall), 1, 1)
            right = pltpu.roll(jnp.where(lane == 0, beyond, tall), LANES - 1, 1)
            wide = tall + left + right
            full = wide + pltpu.roll(wide, 1, 0) + pltpu.roll(wide, BOX - 1, 0)
            weight = 1.0 / (full + 27.0 * error_floor)
            low = low + weight * low_half_ref[i, row]
            high = high + weight * high_half_ref[i, row]
            total = total + weight
        sums[row, 0], sums[row, 1], sums[row, 2] = low, high, total

    @pl.when(step == BANDS // PACE - 1)
    def _():
        swap = side_ref[0] == 1
        for row in range(2):
            low = sums[row, 0] / sums[row, 2]
            high = sums[row, 1] / sums[row, 2]
            out_a_ref[row] = jnp.where(swap, high, low)
            out_b_ref[row] = jnp.where(swap, low, high)


def chip(depth, spot):
    return depth // 2 * SLABS + spot * 2 + depth % 2


def mirror_pairs(ahead):
    pairs = []
    for depth in range(8):
        for spot in range(16):
            goal = (depth, 15 - spot)
            if spot >= 8 and (depth + ahead) % 8 // 2 == 0:
                goal = ((depth + 1) % 8, 15 - spot) if depth % 2 else ((depth - 1) % 8, (16 - spot) % 8)
            pairs.append((chip(depth, spot), chip(*goal)))
    return pairs


def ring_pairs(step):
    return [(chip(d, s), chip((d + step) % 8, s)) for d in range(8) for s in range(16)]


def holder(block, side, core):
    return (2 * (block ^ side) + side) * 2 + core


def row_pairs(step, flip):
    pairs = []
    for n in range(SENDERS):
        goal = (n + step) % SENDERS
        pairs += [(holder(n // 2, side, n % 2), holder(goal // 2, side ^ flip, goal % 2)) for side in range(2)]
    return pairs


def home_pairs(flip):
    return [
        (holder(block, side, core), (2 * block + core) * 2 + (side ^ flip))
        for block in range(64)
        for side in range(2)
        for core in range(2)
    ]


def on_device(tiles, tile_index, pose_bin, bin_gain, cutoffs):
    slab_pos = lax.axis_index("slab")
    group_pos = lax.axis_index("particle")
    half_pos = lax.axis_index("half")
    side_pos = slab_pos % 2
    everyone = ("particle", "slab", "half")
    tile_width = 2 * TILE_ROWS * BOX
    _, particles, touched, _ = tiles.shape
    entries = particles * touched
    late = (slab_pos >= SLABS // 2).astype(jnp.int32)
    heights = [BLOCKS] + [BLOCKS // 2] * 14
    own, *halves = pl.pallas_call(
        place_kernel,
        grid=(2,),
        out_shape=tuple(jax.ShapeDtypeStruct((h, tile_width), f32) for h in heights),
        in_specs=[
            SMEM,
            SMEM,
            pl.BlockSpec((touched, particles), lambda i: (0, 0)),
            pl.BlockSpec((1, particles), lambda i: (0, 0)),
            pl.BlockSpec((1, bin_gain.shape[1]), lambda i: (0, 0)),
            pl.BlockSpec((particles, touched, tile_width // 2), lambda i: (0, 0, i)),
        ],
        out_specs=tuple(pl.BlockSpec((h, tile_width // 2), lambda i: (0, i)) for h in heights),
        scratch_shapes=[pltpu.VMEM((4 * BLOCKS, entries), bf16)] * 3
        + [pltpu.VMEM((BOX, 2 * BOX), bf16), pltpu.VMEM((TILE_ROWS, 2, entries, BOX), bf16)]
        + [pltpu.VMEM((4 * BLOCKS, BOX), f32)],
        name="place",
    )(slab_pos.reshape(1), group_pos.reshape(1), tile_index[0].T, pose_bin, bin_gain, tiles[0])
    here = ("particle", "slab")
    up, down = ring_pairs(1), ring_pairs(-1)

    def send(part, pairs):
        return lax.ppermute(part, here, pairs)

    ahead, far, behind, *sent = [halves[i : i + 2] for i in range(0, 14, 2)]
    come = [[send(sent[i][half], mirror_pairs(e)) for half in range(2)] for i, e in enumerate((3, -3, 1, -1))]
    rise, sink = [], []
    for half in range(2):
        for way, done, (first, own_part, last), pairs in (
            ("rise", rise, (come[0], ahead, come[2]), up),
            ("sink", sink, (come[1], behind, come[3]), down),
        ):
            part = first[half]
            if (way == "rise") == (half == 0):
                part = part + send(far[half], pairs)
            part = send(part, pairs)
            part = send(own_part[half] + part, pairs)
            done.append(send(last[half] + part, pairs))
    plane = (slab_pos * 8 + group_pos * 2 + late).reshape(1)

    constants = [jnp.asarray(t) for t in tables()]
    sent = pl.pallas_call(
        planes_kernel,
        out_shape=pltpu.HBM((SENDERS // 4, 8, BANDS // 2, 8, LANES), f32),
        in_specs=[SMEM, SMEM] + [VMEM] * 7,
        out_specs=pl.BlockSpec(memory_space=pltpu.HBM),
        scratch_shapes=[pltpu.VMEM((2 * BOX, BOX), bf16)] * 2
        + [
            pltpu.VMEM((BOX, BOX), f32),
            pltpu.VMEM((BANDS // 2, SENDERS // 4, 8, 8, LANES), f32),
            pltpu.SemaphoreType.DMA((BANDS // 2,)),
        ]
        + [pltpu.VMEM((2, 2, BOX, BOX), bf16)] * 2,
        name="planes",
        compiler_params=pltpu.CompilerParams(vmem_limit_bytes=16 * 2**20),
    )(cutoffs, plane, own, *rise, *sink, *constants[:2])
    gathered = lax.all_to_all(sent.reshape(2 * SENDERS, PER, LANES), everyone, split_axis=0, concat_axis=0, tiled=True)
    gathered = gathered.reshape(2 * SENDERS * PER, LANES)
    side_flag = jnp.where(jnp.arange(LANES, dtype=jnp.int32) == 0, side_pos, 0)

    steps = BANDS // PACE
    rows_spec = pl.BlockSpec((PACE, 2, BOX, LANES), lambda b: (b, 0, 0, 0))
    rows_shape = jax.ShapeDtypeStruct((BANDS, 2, BOX, LANES), f32)
    row_spec = pl.BlockSpec((PACE, BOX, LANES), lambda b: (b, 0, 0))
    row_shape = jax.ShapeDtypeStruct((BANDS, BOX, LANES), f32)
    edge_spec = pl.BlockSpec((64, LANES), lambda b: (0, 0))
    low_half, high_half, first, second, edge = pl.pallas_call(
        depth_kernel,
        grid=(BANDS // 2,),
        out_shape=(rows_shape, rows_shape, row_shape, row_shape, jax.ShapeDtypeStruct((64, LANES), f32)),
        in_specs=[
            pl.BlockSpec((2 * SENDERS * PER, LANES), lambda b: (0, 0)),
            pl.BlockSpec((2, BOX, BOX), lambda b: (0, 0, 0)),
        ],
        out_specs=(rows_spec, rows_spec, row_spec, row_spec, edge_spec),
        scratch_shapes=[pltpu.VMEM((BOX, LANES), f32)],
        name="depth",
        compiler_params=pltpu.CompilerParams(vmem_limit_bytes=20 * 2**20),
    )(gathered, constants[2])
    before = lax.ppermute(second, everyone, row_pairs(1, 0))
    after = lax.ppermute(first, everyone, row_pairs(-1, 0))
    edges = [lax.ppermute(edge, everyone, row_pairs(n, 1)) for n in (0, 1, -1)]
    block_spec = pl.BlockSpec((2, BOX, LANES), lambda b: (0, 0, 0))
    block_shape = jax.ShapeDtypeStruct((2, BOX, LANES), f32)
    near, far = pl.pallas_call(
        blend_kernel,
        grid=(steps,),
        out_shape=(block_shape, block_shape),
        in_specs=[SMEM, rows_spec, rows_spec] + [row_spec] * 4 + [edge_spec] * 3,
        out_specs=(block_spec, block_spec),
        scratch_shapes=[pltpu.VMEM((2, 3, BOX, LANES), f32), pltpu.VMEM((2, BOX, LANES), f32)],
        name="blend",
        compiler_params=pltpu.CompilerParams(vmem_limit_bytes=16 * 2**20),
    )(side_flag, low_half, high_half, first, second, before, after, *edges)
    near = lax.ppermute(near, everyone, home_pairs(0))
    far = lax.ppermute(far, everyone, home_pairs(1))
    low = jnp.where(half_pos == 0, near, far)
    high = jnp.where(half_pos == 0, far, near)
    refined = jnp.concatenate([low, high], axis=2)
    return jnp.transpose(refined, (1, 0, 2))[None]


def solution(mesh):
    placed = (
        P("half", "particle", "slab", None),
        P("half", "particle", "slab"),
        P("half", "particle"),
        P("half", None),
        P(),
    )

    return jax.shard_map(
        on_device,
        mesh=mesh,
        in_specs=placed,
        out_specs=P("half", None, ("particle", "slab"), None),
        check_vma=False,
    )
```
